512 devices in a mesh: lon: 32 (over z_lo, y), lat: 8 (over x, core), section: 2 (over z_hi).
Axes of the slice: x: 4, y: 8, z: 8 (z_hi: 2, z_lo: 4; z = z_hi * 4 + z_lo), core: 2. Of those that a mesh axis runs over, the one named last changes fastest.
Arguments:
- upper_fields: bfloat16 [5, 6, 192, 1536], P(None, None, 'lat', 'lon'), may hold values from -6 to 6
- surface_fields: bfloat16 [4, 192, 1536], P(None, 'lat', 'lon'), may hold values from -6 to 6
- upper_embed: bfloat16 [160, 192], replicated, may hold values from -0.5 to 0.5
- surface_embed: bfloat16 [64, 192], replicated, may hold values from -0.75 to 0.75
- norm_gains: float32 [2, 2, 192], replicated, may hold values from 0.1 to 1.9
- qkv_weight: bfloat16 [2, 192, 576], replicated, may hold values from -0.4375 to 0.4375
- proj_weight: bfloat16 [2, 192, 192], replicated, may hold values from -0.4375 to 0.4375
- up_weight: bfloat16 [2, 192, 768], replicated, may hold values from -0.4375 to 0.4375
- down_weight: bfloat16 [2, 768, 192], replicated, may hold values from -0.21875 to 0.21875
- earth_bias: float32 [2, 8, 2, 6, 3312], P(None, 'lat', 'section'), may hold values from -4 to 402
- out_grad: bfloat16 [4, 48, 384, 192], P('section', 'lat', 'lon'), may hold values from -6 to 6
Outputs:
- latent_grad: bfloat16 [4, 48, 384, 192], P('section', 'lat', 'lon')
- upper_embed_grad: float32 [160, 192], replicated
- surface_embed_grad: float32 [64, 192], replicated
The draws below stay inside these ranges and needn't reach their ends.
All inputs are finite; a program needn't handle non-finite values.
Results may differ from the reference program's by a relative error of at most 0.024.
Values may be sent and summed in bfloat16 or wider, within the bound.
A program may use at most 64 MiB of HBM per device.

```python
import jax
import jax.numpy as jnp
import numpy as np
from jax import lax

D = 192
HEADS = 6
FF = 768
LZ = 4
UV = 5
SV = 4
BLOCKS = 2
LAT = 48
LON = 384
LATR = 192
LONR = 1536
PL = 6
LATW = 8
ZW = 2
NPOS = 3312
UP_IN = 160
SF_IN = 64


def draw_earth_bias(key, part):
    shape = (BLOCKS, LATW, ZW, HEADS, NPOS)
    subkeys = jax.random.split(key, 1)
    table = jnp.clip(jax.random.normal(subkeys[0], shape, jnp.float32), -4.0, 4.0)
    return table.astype(jnp.float32)


def level_of(stream_key, extent, cuts, smallest, largest):
    loudness, own = 1.0, jax.random.fold_in(stream_key, 6)
    for dim, shards_of in cuts:
        heights = jnp.exp(jax.random.uniform(jax.random.fold_in(own, dim), (shards_of,), jnp.float32, smallest / len(cuts), largest / len(cuts)))
        loudness = loudness * jnp.repeat(heights, extent[dim] // shards_of).reshape([-1 if axis == dim else 1 for axis in range(len(extent))])
    return loudness


def scatter_about(stream_key, shape, scale, bound, pieces=(), held_as=jnp.bfloat16):
    level = level_of(stream_key, shape, pieces, -0.22, 0.18) if pieces else 1.0
    drawn = jax.random.normal(stream_key, shape, jnp.float32) * scale * level
    return jnp.minimum(jnp.maximum(drawn, -bound), bound).astype(held_as)


def setup_inputs(seed: int = 0) -> dict:
    arg_keys = jax.random.split(jax.random.key(seed), 12)
    return {
        "upper_fields": scatter_about(arg_keys[0], (UV, PL, LATR, LONR), 1.0, 6.0, ((2, 8), (3, 32))),
        "surface_fields": scatter_about(arg_keys[1], (SV, LATR, LONR), 1.0, 6.0, ((1, 8), (2, 32))),
        "upper_embed": scatter_about(arg_keys[2], (UP_IN, D), UP_IN ** -0.5, 0.5),
        "surface_embed": scatter_about(arg_keys[3], (SF_IN, D), SF_IN ** -0.5, 0.75),
        "norm_gains": jnp.clip(1.0 + 0.18 * jax.random.normal(arg_keys[4], (BLOCKS, 2, D), jnp.float32), 0.1, 1.9),
        "qkv_weight": scatter_about(arg_keys[5], (BLOCKS, D, 3 * D), D ** -0.5, 0.4375),
        "proj_weight": scatter_about(arg_keys[6], (BLOCKS, D, D), D ** -0.5, 0.4375),
        "up_weight": scatter_about(arg_keys[7], (BLOCKS, D, FF), D ** -0.5, 0.4375),
        "down_weight": scatter_about(arg_keys[8], (BLOCKS, FF, D), FF ** -0.5, 0.21875),
        "earth_bias": draw_earth_bias(jax.random.fold_in(arg_keys[11], 71), 0),
        "out_grad": scatter_about(arg_keys[10], (LZ, LAT, LON, D), 1.0, 6.0, ((0, 2), (1, 8), (2, 32))),
    }


neg_fill = -1e+30
norm_eps = 1e-05

def layer_norm(values, gain):
    average = lax.optimization_barrier(jnp.mean(values, -1, keepdims=True))
    centred = values - average
    variance = lax.optimization_barrier(jnp.mean(centred * centred, -1, keepdims=True))
    return centred * lax.rsqrt(variance + norm_eps) * gain

def pinned(values):
    return lax.optimization_barrier(values.astype(jnp.bfloat16))

def bias_index():
    token = np.arange(144)
    level_part = token // 72
    row_part = token // 12 % 6
    col_part = token % 12
    pair = (level_part[:, None] * 2 + level_part[None, :]) * 36 + row_part[:, None] * 6 + row_part[None, :]
    return pair * 23 + col_part[:, None] - col_part[None, :] + 11

def make_patches(upper_fields, surface_fields):
    up_vars, raw_levels, raw_rows, raw_cols = upper_fields.shape
    upper_patch = upper_fields.reshape(up_vars, raw_levels // 2, 2, raw_rows // 4, 4, raw_cols // 4, 4)
    upper_patch = upper_patch.transpose(1, 3, 5, 0, 2, 4, 6).reshape(raw_levels // 2, raw_rows // 4, raw_cols // 4, up_vars * 32)
    sf_vars = surface_fields.shape[0]
    surface_patch = surface_fields.reshape(sf_vars, raw_rows // 4, 4, raw_cols // 4, 4)
    surface_patch = surface_patch.transpose(1, 3, 0, 2, 4).reshape(raw_rows // 4, raw_cols // 4, sf_vars * 16)
    return (upper_patch, surface_patch)

def region_valid(levels_total, rows_total, group, shifted):
    token = jnp.arange(144, dtype=jnp.int32)
    level = jnp.arange(levels_total // 2, dtype=jnp.int32)[:, None] * 2 + token[None, :] // 72
    row = group * 6 + token // 12 % 6
    zone_level = (level >= levels_total - 2).astype(jnp.int32) + (level >= levels_total - 1).astype(jnp.int32)
    zone_row = (row >= rows_total - 6).astype(jnp.int32) + (row >= rows_total - 3).astype(jnp.int32)
    labels = zone_level * 3 + zone_row[None, :]
    same = labels[:, :, None] == labels[:, None, :]
    if shifted:
        return same
    return jnp.ones_like(same)

def window_group(block_in, bias, allowed, params):
    gains, w_qkv, w_proj, w_up, w_down = params
    levels, rows, cols, width = block_in.shape
    head_count = bias.shape[1]
    head_size = width // head_count
    inputs = block_in.astype(jnp.float32)
    hidden = pinned(layer_norm(inputs, gains[0]))
    qkv = pinned(jnp.einsum('zycd,de->zyce', hidden.astype(jnp.float32), w_qkv.astype(jnp.float32)))
    wins = qkv.reshape(levels // 2, 2, rows, cols // 12, 12, 3, head_count, head_size)
    wins = wins.transpose(0, 3, 5, 6, 1, 2, 4, 7).reshape(levels // 2, cols // 12, 3, head_count, 144, head_size)
    wins = wins.astype(jnp.float32)
    query = wins[:, :, 0]
    keys_all = wins[:, :, 1]
    values_all = wins[:, :, 2]
    score = jnp.einsum('zwhqd,zwhkd->zwhqk', query, keys_all) * head_size ** (-0.5) + bias[:, None]
    score = jnp.where(allowed[:, None, None], score, neg_fill)
    highest = lax.stop_gradient(lax.optimization_barrier(jnp.max(score, -1, keepdims=True)))
    expo = jnp.exp(score - highest)
    weights = pinned(expo / lax.optimization_barrier(jnp.sum(expo, -1, keepdims=True)))
    mixed = pinned(jnp.einsum('zwhqk,zwhkd->zwhqd', weights.astype(jnp.float32), values_all))
    mixed = mixed.reshape(levels // 2, cols // 12, head_count, 2, rows, 12, head_size)
    mixed = mixed.transpose(0, 3, 4, 1, 5, 2, 6).reshape(levels, rows, cols, width)
    resid = inputs + jnp.einsum('zyxc,cd->zyxd', mixed.astype(jnp.float32), w_proj.astype(jnp.float32))
    normed = pinned(layer_norm(resid, gains[1]))
    upward = jnp.einsum('zyxc,cf->zyxf', normed.astype(jnp.float32), w_up.astype(jnp.float32))
    active = pinned(jax.nn.gelu(upward, approximate=False))
    return pinned(resid + jnp.einsum('zyxf,fc->zyxc', active.astype(jnp.float32), w_down.astype(jnp.float32)))

def run_block(volume, shifted, params, table):
    levels, rows_total, cols_total, width = volume.shape
    bias_all = table[..., bias_index()]
    groups = volume.reshape(levels, rows_total // 6, 6, cols_total, width).transpose(1, 0, 2, 3, 4)
    group_ids = jnp.arange(rows_total // 6, dtype=jnp.int32)

    def step(items):
        allowed = region_valid(levels, rows_total, items[2], shifted)
        return window_group(items[0], items[1], allowed, params)
    outputs = lax.map(jax.checkpoint(step), (groups, bias_all, group_ids))
    return outputs.transpose(1, 0, 2, 3, 4).reshape(levels, rows_total, cols_total, width)

def processor(latent, norm_gains, qkv_weight, proj_weight, up_weight, down_weight, earth_bias):
    first = (norm_gains[0], qkv_weight[0], proj_weight[0], up_weight[0], down_weight[0])
    second = (norm_gains[1], qkv_weight[1], proj_weight[1], up_weight[1], down_weight[1])
    volume = run_block(latent, False, first, earth_bias[0])
    volume = jnp.roll(volume, (-1, -3, -6), (0, 1, 2))
    volume = run_block(volume, True, second, earth_bias[1])
    return jnp.roll(volume, (1, 3, 6), (0, 1, 2))

def reference(upper_fields, surface_fields, upper_embed, surface_embed, norm_gains, qkv_weight, proj_weight, up_weight, down_weight, earth_bias, out_grad):
    upper_patch, surface_patch = make_patches(upper_fields, surface_fields)
    upper_latent = jnp.einsum('zyxp,pc->zyxc', upper_patch.astype(jnp.float32), upper_embed.astype(jnp.float32))
    surface_latent = jnp.einsum('yxp,pc->yxc', surface_patch.astype(jnp.float32), surface_embed.astype(jnp.float32))
    latent = pinned(jnp.concatenate((surface_latent[None], upper_latent), 0))

    def forward(volume):
        return processor(volume, norm_gains, qkv_weight, proj_weight, up_weight, down_weight, earth_bias)
    _, pullback = jax.vjp(forward, latent)
    latent_grad = pullback(out_grad)[0]
    grad_float = lax.optimization_barrier(latent_grad).astype(jnp.float32)
    scale = float(np.prod(latent.shape[:3])) ** (-0.5)
    upper_grad = jnp.einsum('zyxp,zyxc->pc', upper_patch.astype(jnp.float32), grad_float[1:]) * scale
    surface_grad = jnp.einsum('yxp,yxc->pc', surface_patch.astype(jnp.float32), grad_float[0]) * scale
    return (latent_grad, upper_grad, surface_grad)
```

```python
import jax
import jax.numpy as jnp
import numpy as np
from jax import lax
from jax.experimental import pallas as pl
from jax.experimental.pallas import tpu as pltpu
from jax.sharding import PartitionSpec as P

neg_fill = -1e30
norm_eps = 1e-05


def shifted(block, axis, distance):
    devices = range(lax.axis_size(axis))
    route = [((i - distance) % len(devices), i) for i in devices]
    return lax.ppermute(block, axis, route)


def layer_norm(values, gain):
    average = jnp.mean(values, -1, keepdims=True)
    centred = values - average
    variance = jnp.mean(centred * centred, -1, keepdims=True)
    return centred * lax.rsqrt(variance + norm_eps) * gain


def exact_gelu(values):
    return jax.nn.gelu(values, approximate=False)


def pinned_round(values):
    return lax.optimization_barrier(values.astype(jnp.bfloat16)).astype(jnp.float32)


def make_patches(upper_fields, surface_fields):
    up_vars, raw_levels, raw_rows, raw_cols = upper_fields.shape
    upper_patch = upper_fields.reshape(
        up_vars, raw_levels // 2, 2, raw_rows // 4, 4, raw_cols // 4, 4
    )
    upper_patch = upper_patch.transpose(1, 3, 5, 0, 2, 4, 6).reshape(
        raw_levels // 2, raw_rows // 4, raw_cols // 4, up_vars * 32
    )
    sf_vars = surface_fields.shape[0]
    surface_patch = surface_fields.reshape(sf_vars, raw_rows // 4, 4, raw_cols // 4, 4)
    surface_patch = surface_patch.transpose(1, 3, 0, 2, 4).reshape(
        raw_rows // 4, raw_cols // 4, sf_vars * 16
    )
    return (upper_patch, surface_patch)


def to_windows(volume):
    levels, rows, cols, channels = volume.shape
    split = volume.reshape(levels // 2, 2, rows // 6, 6, cols // 12, 12, channels)
    return split.transpose(0, 2, 4, 1, 3, 5, 6).reshape(
        levels // 2, rows // 6, cols // 12, 144, channels
    )


def from_windows(windows):
    zone_z, zone_lat, zone_lon, cells, channels = windows.shape
    split = windows.reshape(zone_z, zone_lat, zone_lon, 2, 6, 12, channels)
    return split.transpose(0, 3, 1, 4, 2, 5, 6).reshape(
        zone_z * 2, zone_lat * 6, zone_lon * 12, channels
    )


def bias_index():
    token = np.arange(144)
    level_part = token // 72
    row_part = token // 12 % 6
    col_part = token % 12
    pair = (
        (level_part[:, None] * 2 + level_part[None, :]) * 36
        + row_part[:, None] * 6
        + row_part[None, :]
    )
    return pair * 23 + col_part[:, None] - col_part[None, :] + 11


def window_bias(table):
    return table[..., bias_index()]


def region_valid(level_base, row_base, levels_total, rows_total, zone_z, zone_lat):
    level = level_base + jnp.arange(zone_z * 2, dtype=jnp.int32)
    row = row_base + jnp.arange(zone_lat * 6, dtype=jnp.int32)
    zone_level = (level >= levels_total - 2).astype(jnp.int32) + (level >= levels_total - 1).astype(
        jnp.int32
    )
    zone_row = (row >= rows_total - 6).astype(jnp.int32) + (row >= rows_total - 3).astype(jnp.int32)
    labels = zone_level.reshape(zone_z, 1, 2, 1, 1) * 3 + zone_row.reshape(1, zone_lat, 1, 6, 1)
    labels = (labels + jnp.zeros((1, 1, 1, 1, 12), jnp.int32)).reshape(zone_z, zone_lat, 144)
    return labels[:, :, :, None] == labels[:, :, None, :]


def attention_forward(qkv_win, bias, allowed):
    zone_z, zone_lat, zone_lon, cells, channels = qkv_win.shape
    head_count = bias.shape[2]
    head_size = channels // (3 * head_count)
    parts = qkv_win.reshape(zone_z, zone_lat, zone_lon, cells, 3, head_count, head_size)
    query = parts[:, :, :, :, 0]
    keys_all = parts[:, :, :, :, 1]
    values_all = parts[:, :, :, :, 2]
    score = jnp.einsum("zlwqhd,zlwkhd->zlwhqk", query, keys_all, preferred_element_type=jnp.float32)
    score = score * head_size ** (-0.5) + bias[:, :, None]
    score = jnp.where(allowed[:, :, None, None], score, neg_fill)
    highest = jnp.max(score, -1, keepdims=True)
    expo = jnp.exp(score - highest)
    prob = expo / jnp.sum(expo, -1, keepdims=True)
    weights = prob.astype(jnp.bfloat16)
    mixed = jnp.einsum(
        "zlwhqk,zlwkhd->zlwqhd", weights, values_all, preferred_element_type=jnp.float32
    )
    mixed = mixed.astype(jnp.bfloat16).reshape(zone_z, zone_lat, zone_lon, cells, channels // 3)
    return (mixed, (query, keys_all, values_all, prob, weights))


def attention_backward(dmixed_win, saved):
    query, keys_all, values_all, prob, weights = saved
    head_size = query.shape[-1]
    dmixed = dmixed_win.reshape(query.shape)
    dweights = jnp.einsum(
        "zlwqhd,zlwkhd->zlwhqk", dmixed, values_all, preferred_element_type=jnp.float32
    )
    dweights = pinned_round(dweights)
    dvalues = jnp.einsum(
        "zlwhqk,zlwqhd->zlwkhd", weights, dmixed, preferred_element_type=jnp.float32
    )
    inner = jnp.sum(dweights * prob, -1, keepdims=True)
    dscore = prob * (dweights - inner) * head_size ** (-0.5)
    dquery = jnp.einsum(
        "zlwhqk,zlwkhd->zlwqhd",
        dscore,
        keys_all.astype(jnp.float32),
        precision=lax.Precision.HIGHEST,
    )
    dkeys = jnp.einsum(
        "zlwhqk,zlwqhd->zlwkhd", dscore, query.astype(jnp.float32), precision=lax.Precision.HIGHEST
    )
    stacked = jnp.stack((dquery, dkeys, dvalues), 4).astype(jnp.bfloat16)
    shape = stacked.shape
    return stacked.reshape(shape[0], shape[1], shape[2], shape[3], shape[4] * shape[5] * shape[6])


def block_forward(volume, params, bias, allowed, final):
    gains, w_qkv, w_proj, w_up, w_down = params
    levels, rows, cols, width = volume.shape
    inputs = volume.reshape(-1, width).astype(jnp.float32)
    hidden = layer_norm(inputs, gains[0]).astype(jnp.bfloat16)
    qkv_rows = jnp.dot(hidden, w_qkv, preferred_element_type=jnp.float32).astype(jnp.bfloat16)
    qkv_win = to_windows(qkv_rows.reshape(levels, rows, cols, 3 * width))
    mixed_win, attend_saved = attention_forward(qkv_win, bias, allowed)
    mixed = from_windows(mixed_win).reshape(-1, width)
    resid = inputs + jnp.dot(mixed, w_proj, preferred_element_type=jnp.float32)
    normed = layer_norm(resid, gains[1]).astype(jnp.bfloat16)
    upward = jnp.dot(normed, w_up, preferred_element_type=jnp.float32)
    active = exact_gelu(upward).astype(jnp.bfloat16)
    saved = (volume.shape, inputs, attend_saved, resid, upward)
    if final:
        return (None, saved)
    output = resid + jnp.dot(active, w_down, preferred_element_type=jnp.float32)
    return (output.astype(jnp.bfloat16).reshape(volume.shape), saved)


def block_backward(dvolume, saved, params):
    gains, w_qkv, w_proj, w_up, w_down = params
    shape, inputs, attend_saved, resid, upward = saved
    levels, rows, cols, width = shape
    dflat = dvolume.reshape(-1, width)
    dactive = pinned_round(jnp.dot(dflat, w_down.T, preferred_element_type=jnp.float32))
    dupward = jax.vjp(exact_gelu, upward)[1](dactive)[0]
    dnormed = jnp.dot(dupward, w_up.astype(jnp.float32).T, precision=lax.Precision.HIGHEST)
    dnormed = pinned_round(dnormed)
    dresid = dflat.astype(jnp.float32) + jax.vjp(layer_norm, resid, gains[1])[1](dnormed)[0]
    dmixed = jnp.dot(dresid, w_proj.astype(jnp.float32).T, precision=lax.Precision.HIGHEST).astype(
        jnp.bfloat16
    )
    dqkv_win = attention_backward(
        to_windows(dmixed.reshape(levels, rows, cols, width)), attend_saved
    )
    dqkv = from_windows(dqkv_win).reshape(-1, 3 * width)
    dhidden = pinned_round(jnp.dot(dqkv, w_qkv.T, preferred_element_type=jnp.float32))
    dinputs = dresid + jax.vjp(layer_norm, inputs, gains[0])[1](dhidden)[0]
    return dinputs.astype(jnp.bfloat16).reshape(shape)


def move_edge(volume, axis_dim, edge_depth, direction, sender):
    length = volume.shape[axis_dim]
    if direction > 0:
        border = lax.slice_in_dim(volume, 0, edge_depth, axis=axis_dim)
        remain = lax.slice_in_dim(volume, edge_depth, length, axis=axis_dim)
        return jnp.concatenate((remain, sender(border)), axis_dim)
    border = lax.slice_in_dim(volume, length - edge_depth, length, axis=axis_dim)
    remain = lax.slice_in_dim(volume, 0, length - edge_depth, axis=axis_dim)
    return jnp.concatenate((sender(border), remain), axis_dim)


def roll_rows_levels(volume, direction):
    volume = move_edge(volume, 1, 3, direction, lambda border: shifted(border, "lat", -direction))
    return move_edge(volume, 0, 1, direction, lambda border: shifted(border, "section", -direction))


def roll_columns(volume, direction):
    return move_edge(volume, 2, 6, direction, lambda border: shifted(border, "lon", -direction))


def to_shifted(volume):
    volume = roll_rows_levels(volume, 1)
    return roll_columns(volume, 1)


def on_device(
    upper_fields,
    surface_fields,
    upper_embed,
    surface_embed,
    norm_gains,
    qkv_weight,
    proj_weight,
    up_weight,
    down_weight,
    earth_bias,
    out_grad,
):
    section_index = lax.axis_index("section")
    band_index = lax.axis_index("lat")
    level_count, row_count, column_count, width = out_grad.shape
    levels_total = level_count * lax.axis_size("section")
    rows_total = row_count * lax.axis_size("lat")
    upper_patch, surface_patch = make_patches(upper_fields, surface_fields)
    upper_latent = jnp.einsum(
        "zyxp,pc->zyxc", upper_patch, upper_embed, preferred_element_type=jnp.float32
    )
    surface_latent = jnp.einsum(
        "yxp,pc->yxc", surface_patch, surface_embed, preferred_element_type=jnp.float32
    )
    latent_all = jnp.concatenate((surface_latent[None], upper_latent), 0).astype(jnp.bfloat16)
    latent = lax.dynamic_slice_in_dim(latent_all, section_index * level_count, level_count, 0)
    zone_z = level_count // 2
    zone_lat = row_count // 6
    params_first = (norm_gains[0], qkv_weight[0], proj_weight[0], up_weight[0], down_weight[0])
    params_second = (norm_gains[1], qkv_weight[1], proj_weight[1], up_weight[1], down_weight[1])
    bias_first = window_bias(earth_bias[0].transpose(1, 0, 2, 3))
    bias_second = window_bias(earth_bias[1].transpose(1, 0, 2, 3))
    allow_all = jnp.ones((zone_z, zone_lat, 144, 144), jnp.bool_)
    allow_shifted = region_valid(
        section_index * level_count,
        band_index * row_count,
        levels_total,
        rows_total,
        zone_z,
        zone_lat,
    )
    first_out, first_saved = block_forward(latent, params_first, bias_first, allow_all, False)
    unused_out, second_saved = block_forward(
        to_shifted(first_out), params_second, bias_second, allow_shifted, True
    )
    dshifted = block_backward(to_shifted(out_grad), second_saved, params_second)
    dshifted = roll_columns(dshifted, -1)
    dmiddle = roll_rows_levels(dshifted, -1)
    latent_grad = block_backward(dmiddle, first_saved, params_first)
    spread_grad = jnp.zeros((levels_total, row_count, column_count, width), jnp.bfloat16)
    spread_grad = lax.dynamic_update_slice_in_dim(
        spread_grad, latent_grad, section_index * level_count, 0
    )
    upper_terms = jnp.einsum(
        "zyxp,zyxc->pc", upper_patch, spread_grad[1:], preferred_element_type=jnp.float32
    )
    surface_terms = jnp.einsum(
        "yxp,yxc->pc", surface_patch, spread_grad[0], preferred_element_type=jnp.float32
    )
    upper_total, surface_total = total_over_devices(upper_terms, surface_terms)
    scale = float(levels_total * rows_total * column_count * lax.axis_size("lon")) ** (-0.5)
    return (latent_grad, upper_total * scale, surface_total * scale)


MESH = pl.DeviceIdType.MESH


def wait_bytes(buffer, count, sem):
    pltpu.make_async_copy(buffer.at[pl.ds(0, count)], buffer.at[pl.ds(0, count)], sem).wait()


def total_kernel(terms, result, held, piece, across, last, sems):
    lon_count = lax.axis_size("lon")
    lat_count = lax.axis_size("lat")
    section_count = lax.axis_size("section")
    owners = terms.shape[0]
    lon = lax.axis_index("lon")
    lat = lax.axis_index("lat")
    section = lax.axis_index("section")
    group = lat_count * section_count
    mine = section * lat_count + lat
    barrier = pltpu.get_barrier_semaphore()

    def greet_lon(d, carry):
        pl.semaphore_signal(barrier, inc=1, device_id={"lon": lax.rem(lon + d, lon_count)}, device_id_type=MESH)
        return carry

    lax.fori_loop(1, lon_count, greet_lon, 0)

    def peer_of(d):
        other = lax.rem(mine + d, group)
        return {"lat": lax.rem(other, lat_count), "section": other // lat_count}

    def greet_group(d, carry):
        pl.semaphore_signal(barrier, inc=1, device_id=peer_of(d), device_id_type=MESH)
        return carry

    lax.fori_loop(1, group, greet_group, 0)
    pl.semaphore_wait(barrier, lon_count - 1 + group - 1)

    def scatter(d, carry):
        peer = lax.rem(lon + d, lon_count)

        @pl.when(peer < owners)
        def _():
            pltpu.make_async_remote_copy(
                src_ref=terms.at[peer],
                dst_ref=held.at[d - 1],
                send_sem=sems.at[0],
                recv_sem=sems.at[1],
                device_id={"lon": peer},
                device_id_type=MESH,
            ).start()

        return carry

    lax.fori_loop(1, lon_count, scatter, 0)

    @pl.when(lon < owners)
    def _():
        wait_bytes(held, lon_count - 1, sems.at[1])
        total = terms[lon].astype(jnp.float32)
        for d in range(lon_count - 1):
            total = total + held[d].astype(jnp.float32)
        piece[...] = total.astype(piece.dtype)
        across[mine] = total.astype(piece.dtype)

        def exchange(d, carry):
            pltpu.make_async_remote_copy(
                src_ref=piece,
                dst_ref=across.at[mine],
                send_sem=sems.at[2],
                recv_sem=sems.at[3],
                device_id=peer_of(d),
                device_id_type=MESH,
            ).start()
            return carry

        lax.fori_loop(1, group, exchange, 0)
        wait_bytes(across, group - 1, sems.at[3])
        whole = across[0].astype(jnp.float32)
        for d in range(1, group):
            whole = whole + across[d].astype(jnp.float32)
        last[...] = whole.astype(last.dtype)
        result[lon] = whole.astype(last.dtype)

        def gather(d, carry):
            pltpu.make_async_remote_copy(
                src_ref=last,
                dst_ref=result.at[lon],
                send_sem=sems.at[4],
                recv_sem=sems.at[5],
                device_id={"lon": lax.rem(lon + d, lon_count)},
                device_id_type=MESH,
            ).start()
            return carry

        lax.fori_loop(1, lon_count, gather, 0)
        wait_bytes(terms, owners - 1, sems.at[0])
        wait_bytes(across, group - 1, sems.at[2])
        wait_bytes(result, owners - 1, sems.at[5])
        wait_bytes(held, lon_count - 1, sems.at[4])

    @pl.when(lon >= owners)
    def _():
        wait_bytes(terms, owners, sems.at[0])
        wait_bytes(result, owners, sems.at[5])


def total_over_devices(upper_terms, surface_terms):
    terms = jnp.concatenate((upper_terms, surface_terms), 0).astype(jnp.bfloat16)
    rows, width = terms.shape
    low = terms[:, 128:]
    packed = jnp.concatenate(
        (terms[:, :128], jnp.concatenate((low[: rows // 2], low[rows // 2 :]), 1)), 0
    ).reshape(-1, 16, 128)
    lon_count = lax.axis_size("lon")
    group = lax.axis_size("lat") * lax.axis_size("section")
    total = pl.pallas_call(
        total_kernel,
        out_shape=jax.ShapeDtypeStruct(packed.shape, packed.dtype),
        in_specs=[pl.BlockSpec(memory_space=pltpu.VMEM)],
        out_specs=pl.BlockSpec(memory_space=pltpu.VMEM),
        scratch_shapes=[
            pltpu.VMEM((lon_count - 1, 16, 128), jnp.bfloat16),
            pltpu.VMEM((16, 128), jnp.bfloat16),
            pltpu.VMEM((group, 16, 128), jnp.bfloat16),
            pltpu.VMEM((16, 128), jnp.bfloat16),
            pltpu.SemaphoreType.DMA((6,)),
        ],
        compiler_params=pltpu.CompilerParams(collective_id=0, has_side_effects=True),
    )(packed)
    total = total.reshape(-1, 128).astype(jnp.float32)
    low = total[rows:]
    low = jnp.concatenate((low[:, :64], low[:, 64:]), 0)
    whole = jnp.concatenate((total[:rows], low), 1)
    return whole[: upper_terms.shape[0]], whole[upper_terms.shape[0] :]


def solution(mesh):
    placed = (
        P(None, None, "lat", "lon"),
        P(None, "lat", "lon"),
        P(),
        P(),
        P(),
        P(),
        P(),
        P(),
        P(),
        P(None, "lat", "section", None, None),
        P("section", "lat", "lon", None),
    )
    return jax.shard_map(
        on_device,
        mesh=mesh,
        in_specs=placed,
        out_specs=(P("section", "lat", "lon", None), P(), P()),
        check_vma=False,
    )
```

```python
import functools

import jax
import jax.numpy as jnp
import numpy as np
from jax import lax
from jax.experimental import pallas as pl
from jax.experimental.pallas import tpu as pltpu
from jax.sharding import PartitionSpec as P

MESH = pl.DeviceIdType.MESH
f32 = jnp.float32
bf16 = jnp.bfloat16
norm_eps = 1e-05
HEADS = 6
TOKENS = 144
WIDTH = 192
FIELD_ROWS = 640
NN = (((1,), (0,)), ((), ()))
NT = (((1,), (1,)), ((), ()))
TN = (((0,), (0,)), ((), ()))


def dot(a, b, dims=NN):
    return lax.dot_general(a, b, dims, preferred_element_type=f32)


def tables():
    t = np.arange(TOKENS)
    col, level, row = t // 12, t // 6 % 2, t % 6
    octant = (col // 6) * 4 + level * 2 + row // 3
    place = octant * 32 + (col % 6) * 3 + row % 3
    tok_to_oct = np.zeros((256, TOKENS))
    tok_to_oct[place, t] = 1
    natural = (level * 6 + row) * 16 + col
    nat_to_oct = np.zeros((256, 192))
    nat_to_oct[place, natural] = 1
    tok_to_nat = np.zeros((192, TOKENS))
    tok_to_nat[natural, t] = 1
    pick = np.zeros((4, TOKENS, 48))
    for c in range(4):
        pick[c, t, 4 * col + c] = 1
    key_row = np.full((2, 1, FIELD_ROWS), -1.0)
    fold_upper = np.zeros((4, 256, 160))
    fold_surface = np.zeros((4, 128, 64))
    for v in range(5):
        for a in range(2):
            for y in range(24):
                r = (v * 2 + a) * 24 + y
                key_row[1, 0, r] = y // 4
                key_row[:, 0, 256 + r] = 8 + y // 4
                for c in range(4):
                    fold_upper[c, r, v * 32 + a * 16 + (y % 4) * 4 + c] = 1
    for v in range(4):
        for y in range(24):
            r = v * 24 + y
            key_row[0, 0, 512 + r] = y // 4
            for c in range(4):
                fold_surface[c, r, v * 16 + (y % 4) * 4 + c] = 1
    key_tok = (level * 8 + row).reshape(TOKENS, 1)
    spread = np.zeros((2, 138, 276))
    for z in range(2):
        for a in range(6):
            for k in range(23):
                spread[z, a * 23 + k, (22 - k) * 12 + z * 6 + a] = 1
    heads = np.zeros((HEADS, 1, WIDTH))
    for h in range(HEADS):
        heads[h, 0, 32 * h : 32 * h + 32] = 1
    place_col = np.stack((level, row // 3)).reshape(2, TOKENS, 1)
    place_row = np.stack((level, row // 3)).reshape(2, 1, TOKENS)
    return {
        "tok_to_oct": tok_to_oct.astype(jnp.bfloat16),
        "oct_to_tok": tok_to_oct.T.astype(jnp.bfloat16),
        "nat_to_oct": nat_to_oct.astype(jnp.bfloat16),
        "tok_to_nat": tok_to_nat.astype(jnp.bfloat16),
        "pick": pick.astype(jnp.bfloat16),
        "key_row": key_row.astype(np.float32),
        "key_tok": key_tok.astype(np.float32),
        "fold_upper": fold_upper.astype(jnp.bfloat16),
        "fold_surface": fold_surface.astype(jnp.bfloat16),
        "spread": spread.astype(jnp.bfloat16),
        "heads": heads.astype(np.float32),
        "place_col": place_col.astype(np.float32),
        "place_row": place_row.astype(np.float32),
    }


def centre(values):
    average = jnp.mean(values, -1, keepdims=True)
    centred = values - average
    variance = jnp.mean(centred * centred, -1, keepdims=True)
    scale = lax.rsqrt(variance + norm_eps)
    return centred * scale, scale


def norm_backward(unit, scale, gain, cotangent):
    scaled = cotangent * gain
    first = jnp.mean(scaled, -1, keepdims=True)
    second = jnp.mean(scaled * unit, -1, keepdims=True)
    return scale * (scaled - first - unit * second)


def build_bias(table_ref, spread_ref, tab, strip, bias):
    for z in range(2):
        for zt in range(2):
            for a in range(6):
                start = ((zt * 2 + z) * 6 + a) * 138
                tab[z, (zt * 6 + a) * 8 : (zt * 6 + a) * 8 + 6, :] = table_ref[:, start : start + 138]
    total = None
    for z in range(2):
        rest = tab[z]
        for part in range(3):
            piece = rest.astype(bf16)
            rest = rest - piece.astype(f32)
            term = dot(piece, spread_ref[z])
            total = term if total is None else total + term
    strip[...] = total
    for h in range(HEADS):
        lines = jnp.concatenate([strip[8 * k + h : 8 * k + h + 1, :] for k in range(12)], 0)
        for o in range(12):
            bias[h, 12 * o : 12 * o + 12, :] = lines[:, 12 * (11 - o) : 12 * (11 - o) + TOKENS]


def block_forward(x, b, w, bias, saved, final):
    gains, qkv_w, proj_w, up_w, down_w, heads = w
    unit0, scale0 = centre(x)
    hidden = (unit0 * gains[b, 0:1, :]).astype(bf16)
    qkv = dot(hidden, qkv_w[b]).astype(bf16)
    saved["qkv"][b] = qkv
    query = qkv[:, :WIDTH]
    key = qkv[:, WIDTH : 2 * WIDTH]
    value = qkv[:, 2 * WIDTH :]
    mixed = None
    for h in range(HEADS):
        head = heads[h]
        score = dot(query * head.astype(bf16), key, NT) * 32 ** (-0.5) + bias[h]
        expo = jnp.exp(score - jnp.max(score, -1, keepdims=True))
        prob = expo / jnp.sum(expo, -1, keepdims=True)
        saved["prob"][b, h] = prob
        part = dot(prob.astype(bf16), value) * head
        mixed = part if mixed is None else mixed + part
    resid = x + dot(mixed.astype(bf16), proj_w[b])
    unit1, scale1 = centre(resid)
    normed = (unit1 * gains[b, 1:2, :]).astype(bf16)
    upward = dot(normed, up_w[b])
    saved["unit0"][b] = unit0
    saved["scale0"][b] = scale0
    saved["unit1"][b] = unit1
    saved["scale1"][b] = scale1
    saved["upward"][b] = upward
    if final:
        return None
    active = 0.5 * upward * (1.0 + lax.erf(upward * 2 ** (-0.5)))
    return resid + dot(active.astype(bf16), down_w[b])


def gelu_slope(b, saved):
    upward = saved["upward"][b]
    slope = 0.5 * (1.0 + lax.erf(upward * 2 ** (-0.5)))
    saved["slope"][...] = slope + upward * jnp.exp(-0.5 * upward * upward) * (2 * np.pi) ** (-0.5)


def block_backward(dout, b, w, saved):
    gains, qkv_w, proj_w, up_w, down_w, heads = w
    dactive = dot(dout.astype(bf16), down_w[b], NT).astype(bf16).astype(f32)
    dupward = dactive * saved["slope"][...]
    dnormed = dot(dupward.astype(bf16), up_w[b], NT).astype(bf16).astype(f32)
    dresid = dout + norm_backward(saved["unit1"][b], saved["scale1"][b], gains[b, 1:2, :], dnormed)
    dmixed = dot(dresid.astype(bf16), proj_w[b], NT).astype(bf16)
    qkv = saved["qkv"][b]
    query = qkv[:, :WIDTH]
    key = qkv[:, WIDTH : 2 * WIDTH]
    value = qkv[:, 2 * WIDTH :]
    dquery = dkey = dvalue = None
    for h in range(HEADS):
        head = heads[h]
        narrow = head.astype(bf16)
        prob = saved["prob"][b, h]
        dmixed_h = dmixed * narrow
        dweights = dot(dmixed_h, value, NT).astype(bf16).astype(f32)
        dv = dot(prob.astype(bf16), dmixed_h, TN)
        inner = jnp.sum(dweights * prob, -1, keepdims=True)
        dscore = (prob * (dweights - inner) * 32 ** (-0.5)).astype(bf16)
        dq = dot(dscore, key) * head
        dk = dot(dscore, query * narrow, TN)
        dquery = dq if dquery is None else dquery + dq
        dkey = dk if dkey is None else dkey + dk
        dvalue = dv if dvalue is None else dvalue + dv
    dqkv = jnp.concatenate((dquery, dkey, dvalue), 1).astype(bf16)
    dhidden = dot(dqkv, qkv_w[b], NT).astype(bf16).astype(f32)
    return dresid + norm_backward(saved["unit0"][b], saved["scale0"][b], gains[b, 0:1, :], dhidden)


def wait_bytes(buffer, start, count, sem):
    view = buffer.at[pl.ds(start, count)]
    pltpu.make_async_copy(view, view, sem).wait()


def send_octants(src, dst, send_sem, recv_sem, forward):
    lon_count, lat_count = lax.axis_size("lon"), lax.axis_size("lat")
    lon, lat, section = lax.axis_index("lon"), lax.axis_index("lat"), lax.axis_index("section")
    for k in range(8):
        step = tuple((1 - (k >> bit & 1)) if forward else (k >> bit & 1) for bit in (2, 1, 0))
        if step == (0, 0, 0):
            dst[7 - k] = src[k]
            continue
        sign = -1 if forward else 1
        target = {}
        if step[0]:
            target["lon"] = lax.rem(lon + sign + lon_count, lon_count)
        if step[1]:
            target["section"] = 1 - section
        if step[2]:
            target["lat"] = lax.rem(lat + sign + lat_count, lat_count)
        pltpu.make_async_remote_copy(
            src_ref=src.at[k],
            dst_ref=dst.at[7 - k],
            send_sem=send_sem,
            recv_sem=recv_sem,
            device_id=target,
            device_id_type=MESH,
        ).start()


def whole_kernel(names, owners, unit, *refs):
    consts = dict(zip(names, refs))
    (
        upper_ref,
        surface_ref,
        upper_embed,
        surface_embed,
        gains,
        qkv_w,
        proj_w,
        up_w,
        down_w,
        table_ref,
        grad_ref,
        latent_out,
        upper_out,
        surface_out,
        field,
        natural,
        tab,
        strip,
        bias0,
        bias1,
        qkv_s,
        prob_s,
        unit0_s,
        scale0_s,
        unit1_s,
        scale1_s,
        upward_s,
        slope_s,
        patch_upper,
        patch_surface,
        grad_send,
        grad_recv,
        x_send,
        x_recv,
        back_send,
        back_recv,
        terms,
        held,
        piece,
        across,
        last,
        result,
        sems,
    ) = refs[len(names) :]
    lon_count = lax.axis_size("lon")
    lat_count = lax.axis_size("lat")
    section_count = lax.axis_size("section")
    lon = lax.axis_index("lon")
    lat = lax.axis_index("lat")
    section = lax.axis_index("section")
    group = lat_count * section_count
    mine = section * lat_count + lat
    barrier = pltpu.get_barrier_semaphore()

    def peer_of(d):
        other = lax.rem(mine + d, group)
        return {"lat": lax.rem(other, lat_count), "section": other // lat_count}

    def greet_lon(d, carry):
        pl.semaphore_signal(
            barrier, inc=1, device_id={"lon": lax.rem(lon + d, lon_count)}, device_id_type=MESH
        )
        return carry

    def greet_group(d, carry):
        pl.semaphore_signal(barrier, inc=1, device_id=peer_of(d), device_id_type=MESH)
        return carry

    for sign in (-1, 1):
        lon_next = lax.rem(lon + sign + lon_count, lon_count)
        lat_next = lax.rem(lat + sign + lat_count, lat_count)
        for target in (
            {"lon": lon_next, "section": 1 - section},
            {"lon": lon_next, "lat": lat_next},
            {"lon": lon_next, "lat": lat_next, "section": 1 - section},
        ):
            pl.semaphore_signal(barrier, inc=1, device_id=target, device_id_type=MESH)
    lax.fori_loop(1, lon_count, greet_lon, 0)
    lax.fori_loop(1, group, greet_group, 0)

    natural[...] = jnp.zeros_like(natural)
    for z in range(2):
        for a in range(6):
            natural[z * 6 + a, 0:12, :] = grad_ref[z, a].astype(f32)
    octants = dot(consts["nat_to_oct"][...], natural[...].reshape(192, WIDTH).astype(bf16))
    grad_send[...] = octants.astype(bf16).reshape(8, 32, WIDTH)

    field[240:256, :] = jnp.zeros((16, 48), f32)
    field[496:512, :] = jnp.zeros((16, 48), f32)
    field[608:640, :] = jnp.zeros((32, 48), f32)
    for v in range(5):
        for a in range(2):
            row = (v * 2 + a) * 24
            field[row : row + 24, :] = upper_ref[v, 2 + a].astype(f32)
            field[256 + row : 256 + row + 24, :] = upper_ref[v, 4 * section + a].astype(f32)
    for v in range(4):
        field[512 + 24 * v : 512 + 24 * v + 24, :] = surface_ref[v].astype(f32)
    fields = field[...].astype(bf16)
    same = consts["key_tok"][...] == consts["key_row"][section]
    upper_total = surface_total = None
    for c in range(4):
        spreads = jnp.where(same, dot(consts["pick"][c], fields, NT), 0.0)
        upper_c = (spreads[:, :256] + spreads[:, 256:512]).astype(bf16)
        surface_c = spreads[:, 512:].astype(bf16)
        upper_c = dot(upper_c, consts["fold_upper"][c])
        surface_c = dot(surface_c, consts["fold_surface"][c])
        upper_total = upper_c if upper_total is None else upper_total + upper_c
        surface_total = surface_c if surface_total is None else surface_total + surface_c
    patch_upper[...] = upper_total.astype(bf16)
    patch_surface[...] = surface_total.astype(bf16)
    latent = dot(patch_upper[...], upper_embed[...]) + dot(patch_surface[...], surface_embed[...])
    latent = latent.astype(bf16).astype(f32)
    build_bias(table_ref.at[0], consts["spread"], tab, strip, bias0)

    pl.semaphore_wait(barrier, lon_count - 1 + group - 1 + 6)
    send_octants(grad_send, grad_recv, sems.at[0], sems.at[1], True)

    w = (gains, qkv_w, proj_w, up_w, down_w, consts["heads"])
    saved = {
        "qkv": qkv_s,
        "prob": prob_s,
        "unit0": unit0_s,
        "scale0": scale0_s,
        "unit1": unit1_s,
        "scale1": scale1_s,
        "upward": upward_s,
        "slope": slope_s,
    }
    first = block_forward(latent, 0, w, bias0, saved, False)
    octants = dot(consts["tok_to_oct"][...], first.astype(bf16))
    x_send[...] = octants.astype(bf16).reshape(8, 32, WIDTH)
    send_octants(x_send, x_recv, sems.at[2], sems.at[3], True)

    build_bias(table_ref.at[1], consts["spread"], tab, strip, bias1)
    last_section = (section == section_count - 1).astype(f32)
    last_band = (lat == lat_count - 1).astype(f32)
    apart = jnp.abs(consts["place_col"][0] - consts["place_row"][0]) * last_section
    apart = apart + jnp.abs(consts["place_col"][1] - consts["place_row"][1]) * last_band
    for h in range(HEADS):
        bias1[h] = jnp.where(apart > 0.5, -1e30, bias1[h])
    wait_bytes(grad_recv, 1, 7, sems.at[1])
    dshifted = dot(consts["oct_to_tok"][...], grad_recv[...].reshape(256, WIDTH))
    wait_bytes(x_recv, 1, 7, sems.at[3])
    shifted = dot(consts["oct_to_tok"][...], x_recv[...].reshape(256, WIDTH))

    block_forward(shifted, 1, w, bias1, saved, True)
    gelu_slope(1, saved)
    dmiddle = block_backward(dshifted, 1, w, saved)
    octants = dot(consts["tok_to_oct"][...], dmiddle.astype(bf16))
    back_send[...] = octants.astype(bf16).reshape(8, 32, WIDTH)
    send_octants(back_send, back_recv, sems.at[4], sems.at[5], False)
    gelu_slope(0, saved)
    wait_bytes(back_recv, 0, 7, sems.at[5])
    dfirst = dot(consts["oct_to_tok"][...], back_recv[...].reshape(256, WIDTH))
    dlatent = block_backward(dfirst, 0, w, saved).astype(bf16)

    upper_terms = dot(patch_upper[...], dlatent, TN)
    surface_terms = dot(patch_surface[...], dlatent, TN)
    both = jnp.concatenate((upper_terms, surface_terms), 0)
    terms[0:14, :, :] = both[:, :128].astype(bf16).reshape(14, 16, 128)
    low = both[:, 128:]
    low = jnp.concatenate((low[:112], low[112:]), 1)
    terms[14:21, :, :] = low.astype(bf16).reshape(7, 16, 128)

    def scatter(d, carry):
        peer = lax.rem(lon + d, lon_count)

        @pl.when(peer < owners)
        def _():
            pltpu.make_async_remote_copy(
                src_ref=terms.at[pl.ds(peer * unit, unit)],
                dst_ref=held.at[pl.ds((d - 1) * unit, unit)],
                send_sem=sems.at[6],
                recv_sem=sems.at[7],
                device_id={"lon": peer},
                device_id_type=MESH,
            ).start()

        return carry

    lax.fori_loop(1, lon_count, scatter, 0)

    grads = dot(consts["tok_to_nat"][...], dlatent).astype(bf16)
    for z in range(2):
        for a in range(6):
            k = (z * 6 + a) * 16
            latent_out[z, a] = grads[k : k + 16][:12]

    @pl.when(lon < owners)
    def _():
        wait_bytes(held, 0, (lon_count - 1) * unit, sems.at[7])
        total = terms[pl.ds(lon * unit, unit)].astype(f32)
        for d in range(lon_count - 1):
            total = total + held[d * unit : d * unit + unit].astype(f32)
        piece[...] = total.astype(bf16)
        across[pl.ds(mine * unit, unit)] = total.astype(bf16)

        def exchange(d, carry):
            pltpu.make_async_remote_copy(
                src_ref=piece,
                dst_ref=across.at[pl.ds(mine * unit, unit)],
                send_sem=sems.at[8],
                recv_sem=sems.at[9],
                device_id=peer_of(d),
                device_id_type=MESH,
            ).start()
            return carry

        lax.fori_loop(1, group, exchange, 0)
        wait_bytes(across, 0, (group - 1) * unit, sems.at[9])
        whole = across[0:unit].astype(f32)
        for d in range(1, group):
            whole = whole + across[d * unit : d * unit + unit].astype(f32)
        last[...] = whole.astype(bf16)
        result[pl.ds(lon * unit, unit)] = whole.astype(bf16)

        def gather(d, carry):
            pltpu.make_async_remote_copy(
                src_ref=last,
                dst_ref=result.at[pl.ds(lon * unit, unit)],
                send_sem=sems.at[10],
                recv_sem=sems.at[11],
                device_id={"lon": lax.rem(lon + d, lon_count)},
                device_id_type=MESH,
            ).start()
            return carry

        lax.fori_loop(1, lon_count, gather, 0)
        wait_bytes(terms, 0, (owners - 1) * unit, sems.at[6])
        wait_bytes(across, 0, (group - 1) * unit, sems.at[8])
        wait_bytes(result, 0, (owners - 1) * unit, sems.at[11])
        wait_bytes(held, 0, (lon_count - 1) * unit, sems.at[10])

    @pl.when(lon >= owners)
    def _():
        wait_bytes(terms, 0, owners * unit, sems.at[6])
        wait_bytes(result, 0, owners * unit, sems.at[11])

    scale = float(4 * 6 * lat_count * 12 * lon_count) ** (-0.5)
    high = result[0:14].astype(f32).reshape(224, 128) * scale
    low = result[14:21].astype(f32).reshape(112, 128) * scale
    upper_out[:, 0:128] = high[:160]
    surface_out[:, 0:128] = high[160:]
    upper_out[0:112, 128:192] = low[:, :64]
    upper_out[112:160, 128:192] = low[:48, 64:]
    surface_out[:, 128:192] = low[48:, 64:]
    wait_bytes(grad_send, 0, 7, sems.at[0])
    wait_bytes(x_send, 0, 7, sems.at[2])
    wait_bytes(back_send, 0, 7, sems.at[4])


def on_device(
    upper_fields,
    surface_fields,
    upper_embed,
    surface_embed,
    norm_gains,
    qkv_weight,
    proj_weight,
    up_weight,
    down_weight,
    earth_bias,
    out_grad,
):
    consts = tables()
    names = tuple(consts)
    lon_count = lax.axis_size("lon")
    group = lax.axis_size("lat") * lax.axis_size("section")
    unit = -(-21 // lon_count)
    owners = -(-21 // unit)
    vmem = pl.BlockSpec(memory_space=pltpu.VMEM)
    return pl.pallas_call(
        functools.partial(whole_kernel, names, owners, unit),
        out_shape=(
            jax.ShapeDtypeStruct(out_grad.shape, bf16),
            jax.ShapeDtypeStruct((160, WIDTH), f32),
            jax.ShapeDtypeStruct((64, WIDTH), f32),
        ),
        in_specs=[vmem] * (len(names) + 11),
        out_specs=(vmem,) * 3,
        scratch_shapes=[
            pltpu.VMEM((FIELD_ROWS, 48), f32),
            pltpu.VMEM((12, 16, WIDTH), f32),
            pltpu.VMEM((2, 96, 138), f32),
            pltpu.VMEM((96, 276), f32),
            pltpu.VMEM((HEADS, TOKENS, TOKENS), f32),
            pltpu.VMEM((HEADS, TOKENS, TOKENS), f32),
            pltpu.VMEM((2, TOKENS, 3 * WIDTH), bf16),
            pltpu.VMEM((2, HEADS, TOKENS, TOKENS), f32),
            pltpu.VMEM((2, TOKENS, WIDTH), f32),
            pltpu.VMEM((2, TOKENS, 1), f32),
            pltpu.VMEM((2, TOKENS, WIDTH), f32),
            pltpu.VMEM((2, TOKENS, 1), f32),
            pltpu.VMEM((2, TOKENS, 768), f32),
            pltpu.VMEM((TOKENS, 768), f32),
            pltpu.VMEM((TOKENS, 160), bf16),
            pltpu.VMEM((TOKENS, 64), bf16),
            pltpu.VMEM((8, 32, WIDTH), bf16),
            pltpu.VMEM((8, 32, WIDTH), bf16),
            pltpu.VMEM((8, 32, WIDTH), bf16),
            pltpu.VMEM((8, 32, WIDTH), bf16),
            pltpu.VMEM((8, 32, WIDTH), bf16),
            pltpu.VMEM((8, 32, WIDTH), bf16),
            pltpu.VMEM((owners * unit, 16, 128), bf16),
            pltpu.VMEM(((lon_count - 1) * unit, 16, 128), bf16),
            pltpu.VMEM((unit, 16, 128), bf16),
            pltpu.VMEM((group * unit, 16, 128), bf16),
            pltpu.VMEM((unit, 16, 128), bf16),
            pltpu.VMEM((owners * unit, 16, 128), bf16),
            pltpu.SemaphoreType.DMA((12,)),
        ],
        compiler_params=pltpu.CompilerParams(
            collective_id=0, has_side_effects=True, vmem_limit_bytes=48 * 2**20
        ),
    )(
        *consts.values(),
        upper_fields,
        surface_fields,
        upper_embed,
        surface_embed,
        norm_gains,
        qkv_weight,
        proj_weight,
        up_weight,
        down_weight,
        earth_bias.reshape(2, HEADS, -1),
        out_grad,
    )


def solution(mesh):
    placed = (
        P(None, None, "lat", "lon"),
        P(None, "lat", "lon"),
        P(),
        P(),
        P(),
        P(),
        P(),
        P(),
        P(),
        P(None, "lat", "section", None, None),
        P("section", "lat", "lon", None),
    )
    return jax.shard_map(
        on_device,
        mesh=mesh,
        in_specs=placed,
        out_specs=(P("section", "lat", "lon", None), P(), P()),
        check_vma=False,
    )
```

```python
import functools

import jax
import jax.numpy as jnp
import numpy as np
from jax import lax
from jax.experimental import pallas as pl
from jax.experimental.pallas import tpu as pltpu
from jax.sharding import PartitionSpec as P

MESH = pl.DeviceIdType.MESH
f32 = jnp.float32
bf16 = jnp.bfloat16
norm_eps = 1e-05
HEADS = 6
TOKENS = 144
WIDTH = 192
FIELD_ROWS = 640
NN = (((1,), (0,)), ((), ()))
NT = (((1,), (1,)), ((), ()))
TN = (((0,), (0,)), ((), ()))


def dot(a, b, dims=NN):
    return lax.dot_general(a, b, dims, preferred_element_type=f32)


def tables():
    t = np.arange(TOKENS)
    col, level, row = t // 12, t // 6 % 2, t % 6
    octant = (col // 6) * 4 + level * 2 + row // 3
    place = octant * 32 + (col % 6) * 3 + row % 3
    tok_to_oct = np.zeros((256, TOKENS))
    tok_to_oct[place, t] = 1
    natural = (level * 6 + row) * 16 + col
    nat_to_oct = np.zeros((256, 192))
    nat_to_oct[place, natural] = 1
    tok_to_nat = np.zeros((192, TOKENS))
    tok_to_nat[natural, t] = 1
    pick = np.zeros((4, TOKENS, 48))
    for c in range(4):
        pick[c, t, 4 * col + c] = 1
    key_row = np.full((2, 1, FIELD_ROWS), -1.0)
    fold_upper = np.zeros((4, 256, 160))
    fold_surface = np.zeros((4, 128, 64))
    for v in range(5):
        for a in range(2):
            for y in range(24):
                r = (v * 2 + a) * 24 + y
                key_row[1, 0, r] = y // 4
                key_row[:, 0, 256 + r] = 8 + y // 4
                for c in range(4):
                    fold_upper[c, r, v * 32 + a * 16 + (y % 4) * 4 + c] = 1
    for v in range(4):
        for y in range(24):
            r = v * 24 + y
            key_row[0, 0, 512 + r] = y // 4
            for c in range(4):
                fold_surface[c, r, v * 16 + (y % 4) * 4 + c] = 1
    key_tok = (level * 8 + row).reshape(TOKENS, 1)
    spread = np.zeros((2, 138, 276))
    for z in range(2):
        for a in range(6):
            for k in range(23):
                spread[z, a * 23 + k, (22 - k) * 12 + z * 6 + a] = 1
    heads = np.zeros((HEADS, 1, WIDTH))
    for h in range(HEADS):
        heads[h, 0, 32 * h : 32 * h + 32] = 1
    place_col = np.stack((level, row // 3)).reshape(2, TOKENS, 1)
    place_row = np.stack((level, row // 3)).reshape(2, 1, TOKENS)
    return {
        "tok_to_oct": tok_to_oct.astype(jnp.bfloat16),
        "oct_to_tok": tok_to_oct.T.astype(jnp.bfloat16),
        "nat_to_oct": nat_to_oct.astype(jnp.bfloat16),
        "tok_to_nat": tok_to_nat.astype(jnp.bfloat16),
        "pick": pick.astype(jnp.bfloat16),
        "key_row": key_row.astype(np.float32),
        "key_tok": key_tok.astype(np.float32),
        "fold_upper": fold_upper.astype(jnp.bfloat16),
        "fold_surface": fold_surface.astype(jnp.bfloat16),
        "spread": spread.astype(jnp.bfloat16),
        "heads": heads.astype(np.float32),
        "place_col": place_col.astype(np.float32),
        "place_row": place_row.astype(np.float32),
    }


def centre(values):
    average = jnp.mean(values, -1, keepdims=True)
    centred = values - average
    variance = jnp.mean(centred * centred, -1, keepdims=True)
    scale = lax.rsqrt(variance + norm_eps)
    return centred * scale, scale


def norm_backward(unit, scale, gain, cotangent):
    scaled = cotangent * gain
    first = jnp.mean(scaled, -1, keepdims=True)
    second = jnp.mean(scaled * unit, -1, keepdims=True)
    return scale * (scaled - first - unit * second)


def build_bias(table_ref, spread_ref, tab, strip, bias):
    for z in range(2):
        for zt in range(2):
            for a in range(6):
                start = ((zt * 2 + z) * 6 + a) * 138
                tab[z, (zt * 6 + a) * 8 : (zt * 6 + a) * 8 + 6, :] = table_ref[:, start : start + 138]
    total = None
    for z in range(2):
        rest = tab[z]
        for part in range(3):
            piece = rest.astype(bf16)
            rest = rest - piece.astype(f32)
            term = dot(piece, spread_ref[z])
            total = term if total is None else total + term
    strip[...] = total
    for h in range(HEADS):
        lines = jnp.concatenate([strip[8 * k + h : 8 * k + h + 1, :] for k in range(12)], 0)
        for o in range(12):
            bias[h, 12 * o : 12 * o + 12, :] = lines[:, 12 * (11 - o) : 12 * (11 - o) + TOKENS]


def block_forward(x, b, w, bias, saved, final):
    unit0, scale0 = centre(x)
    hidden = (unit0 * w["gains"][b, 0:1, :]).astype(bf16)
    qkv = dot(hidden, w["qkv"][b]).astype(bf16)
    saved["qkv"][b] = qkv
    query = qkv[:, :WIDTH]
    key = qkv[:, WIDTH : 2 * WIDTH]
    value = qkv[:, 2 * WIDTH :]
    mixed = None
    for h in range(HEADS):
        head = w["heads"][h]
        score = dot(query * head.astype(bf16), key, NT) * 32 ** (-0.5) + bias[h]
        expo = jnp.exp(score - jnp.max(score, -1, keepdims=True))
        prob = expo / jnp.sum(expo, -1, keepdims=True)
        saved["prob"][b, h] = prob
        part = dot(prob.astype(bf16), value) * head
        mixed = part if mixed is None else mixed + part
    resid = x + dot(mixed.astype(bf16), w["proj"][b])
    unit1, scale1 = centre(resid)
    normed = (unit1 * w["gains"][b, 1:2, :]).astype(bf16)
    upward = dot(normed, w["up"][b])
    saved["unit0"][b] = unit0
    saved["scale0"][b] = scale0
    saved["unit1"][b] = unit1
    saved["scale1"][b] = scale1
    saved["upward"][b] = upward
    if final:
        return None
    active = 0.5 * upward * (1.0 + lax.erf(upward * 2 ** (-0.5)))
    return resid + dot(active.astype(bf16), w["down"][b], NT)


def gelu_slope(b, saved):
    upward = saved["upward"][b]
    slope = 0.5 * (1.0 + lax.erf(upward * 2 ** (-0.5)))
    saved["slope"][...] = slope + upward * jnp.exp(-0.5 * upward * upward) * (2 * np.pi) ** (-0.5)


def block_backward(dout, b, w, saved):
    dactive = dot(dout.astype(bf16), w["down"][b]).astype(bf16).astype(f32)
    dupward = dactive * saved["slope"][...]
    dnormed = dot(dupward.astype(bf16), w["up"][b], NT).astype(bf16).astype(f32)
    dresid = dout + norm_backward(saved["unit1"][b], saved["scale1"][b], w["gains"][b, 1:2, :], dnormed)
    dmixed = dot(dresid.astype(bf16), w["proj"][b], NT).astype(bf16)
    qkv = saved["qkv"][b]
    query = qkv[:, :WIDTH]
    key = qkv[:, WIDTH : 2 * WIDTH]
    value = qkv[:, 2 * WIDTH :]
    dquery = dkey = dvalue = None
    for h in range(HEADS):
        head = w["heads"][h]
        narrow = head.astype(bf16)
        prob = saved["prob"][b, h]
        dmixed_h = dmixed * narrow
        dweights = dot(dmixed_h, value, NT).astype(bf16).astype(f32)
        dv = dot(prob.astype(bf16), dmixed_h, TN)
        inner = jnp.sum(dweights * prob, -1, keepdims=True)
        dscore = (prob * (dweights - inner) * 32 ** (-0.5)).astype(bf16)
        dq = dot(dscore, key) * head
        dk = dot(dscore, query * narrow, TN)
        dquery = dq if dquery is None else dquery + dq
        dkey = dk if dkey is None else dkey + dk
        dvalue = dv if dvalue is None else dvalue + dv
    dqkv = jnp.concatenate((dquery, dkey, dvalue), 1).astype(bf16)
    dhidden = dot(dqkv, w["qkv"][b], NT).astype(bf16).astype(f32)
    return dresid + norm_backward(saved["unit0"][b], saved["scale0"][b], w["gains"][b, 0:1, :], dhidden)


def wait_bytes(buffer, start, count, sem):
    view = buffer.at[pl.ds(start, count)]
    pltpu.make_async_copy(view, view, sem).wait()


def send_octants(src, dst, send_sem, recv_sem, forward):
    lon_count, lat_count = lax.axis_size("lon"), lax.axis_size("lat")
    lon, lat, section = lax.axis_index("lon"), lax.axis_index("lat"), lax.axis_index("section")
    for k in range(8):
        step = tuple((1 - (k >> bit & 1)) if forward else (k >> bit & 1) for bit in (2, 1, 0))
        if step == (0, 0, 0):
            dst[7 - k] = src[k]
            continue
        sign = -1 if forward else 1
        target = {}
        if step[0]:
            target["lon"] = lax.rem(lon + sign + lon_count, lon_count)
        if step[1]:
            target["section"] = 1 - section
        if step[2]:
            target["lat"] = lax.rem(lat + sign + lat_count, lat_count)
        pltpu.make_async_remote_copy(
            src_ref=src.at[k],
            dst_ref=dst.at[7 - k],
            send_sem=send_sem,
            recv_sem=recv_sem,
            device_id=target,
            device_id_type=MESH,
        ).start()


class Loads:
    def __init__(self, names, sources, targets, sems):
        self.targets = dict(zip(names, targets))
        self.copies = {}
        for i, name in enumerate(names):
            copy = pltpu.make_async_copy(sources[i], targets[i], sems.at[i])
            copy.start()
            self.copies[name] = copy

    def __getitem__(self, name):
        copy = self.copies.pop(name, None)
        if copy is not None:
            copy.wait()
        return self.targets[name]


def whole_kernel(names, owners, unit, *refs):
    count = len(names)
    consts = Loads(names, refs[:count], refs[-count - 1 : -1], refs[-1])
    (
        latent_out,
        upper_out,
        surface_out,
        field,
        natural,
        tab,
        strip,
        bias0,
        bias1,
        qkv_s,
        prob_s,
        unit0_s,
        scale0_s,
        unit1_s,
        scale1_s,
        upward_s,
        slope_s,
        patch_upper,
        patch_surface,
        grad_send,
        grad_recv,
        x_send,
        x_recv,
        back_send,
        back_recv,
        terms,
        held,
        piece,
        across,
        last,
        result,
        sems,
    ) = refs[count : -count - 1]
    lon_count = lax.axis_size("lon")
    lat_count = lax.axis_size("lat")
    section_count = lax.axis_size("section")
    lon = lax.axis_index("lon")
    lat = lax.axis_index("lat")
    section = lax.axis_index("section")
    group = lat_count * section_count
    mine = section * lat_count + lat
    barrier = pltpu.get_barrier_semaphore()

    def peer_of(d):
        other = lax.rem(mine + d, group)
        return {"lat": lax.rem(other, lat_count), "section": other // lat_count}

    def greet_lon(d, carry):
        pl.semaphore_signal(
            barrier, inc=1, device_id={"lon": lax.rem(lon + d, lon_count)}, device_id_type=MESH
        )
        return carry

    def greet_group(d, carry):
        pl.semaphore_signal(barrier, inc=1, device_id=peer_of(d), device_id_type=MESH)
        return carry

    for sign in (-1, 1):
        lon_next = lax.rem(lon + sign + lon_count, lon_count)
        lat_next = lax.rem(lat + sign + lat_count, lat_count)
        for target in (
            {"lon": lon_next, "section": 1 - section},
            {"lon": lon_next, "lat": lat_next},
            {"lon": lon_next, "lat": lat_next, "section": 1 - section},
        ):
            pl.semaphore_signal(barrier, inc=1, device_id=target, device_id_type=MESH)
    lax.fori_loop(1, lon_count, greet_lon, 0)
    lax.fori_loop(1, group, greet_group, 0)

    natural[...] = jnp.zeros_like(natural)
    for z in range(2):
        for a in range(6):
            natural[z * 6 + a, 0:12, :] = consts["grad"][z, a].astype(f32)
    octants = dot(consts["nat_to_oct"][...], natural[...].reshape(192, WIDTH).astype(bf16))
    grad_send[...] = octants.astype(bf16).reshape(8, 32, WIDTH)

    field[240:256, :] = jnp.zeros((16, 48), f32)
    field[496:512, :] = jnp.zeros((16, 48), f32)
    field[608:640, :] = jnp.zeros((32, 48), f32)
    for v in range(5):
        for a in range(2):
            row = (v * 2 + a) * 24
            field[row : row + 24, :] = consts["upper"][v, 2 + a].astype(f32)
            field[256 + row : 256 + row + 24, :] = consts["upper"][v, 4 * section + a].astype(f32)
    for v in range(4):
        field[512 + 24 * v : 512 + 24 * v + 24, :] = consts["surface"][v].astype(f32)
    fields = field[...].astype(bf16)
    same = consts["key_tok"][...] == consts["key_row"][section]
    upper_total = surface_total = None
    for c in range(4):
        spreads = jnp.where(same, dot(consts["pick"][c], fields, NT), 0.0)
        upper_c = (spreads[:, :256] + spreads[:, 256:512]).astype(bf16)
        surface_c = spreads[:, 512:].astype(bf16)
        upper_c = dot(upper_c, consts["fold_upper"][c])
        surface_c = dot(surface_c, consts["fold_surface"][c])
        upper_total = upper_c if upper_total is None else upper_total + upper_c
        surface_total = surface_c if surface_total is None else surface_total + surface_c
    patch_upper[...] = upper_total.astype(bf16)
    patch_surface[...] = surface_total.astype(bf16)
    latent = dot(patch_upper[...], consts["upper_embed"][...])
    latent = latent + dot(patch_surface[...], consts["surface_embed"][...])
    latent = latent.astype(bf16).astype(f32)
    build_bias(consts["table"].at[0], consts["spread"], tab, strip, bias0)

    pl.semaphore_wait(barrier, lon_count - 1 + group - 1 + 6)
    send_octants(grad_send, grad_recv, sems.at[0], sems.at[1], True)

    w = consts
    saved = {
        "qkv": qkv_s,
        "prob": prob_s,
        "unit0": unit0_s,
        "scale0": scale0_s,
        "unit1": unit1_s,
        "scale1": scale1_s,
        "upward": upward_s,
        "slope": slope_s,
    }
    first = block_forward(latent, 0, w, bias0, saved, False)
    octants = dot(consts["tok_to_oct"][...], first.astype(bf16))
    x_send[...] = octants.astype(bf16).reshape(8, 32, WIDTH)
    send_octants(x_send, x_recv, sems.at[2], sems.at[3], True)

    build_bias(consts["table"].at[1], consts["spread"], tab, strip, bias1)
    last_section = (section == section_count - 1).astype(f32)
    last_band = (lat == lat_count - 1).astype(f32)
    apart = jnp.abs(consts["place_col"][0] - consts["place_row"][0]) * last_section
    apart = apart + jnp.abs(consts["place_col"][1] - consts["place_row"][1]) * last_band
    for h in range(HEADS):
        bias1[h] = jnp.where(apart > 0.5, -1e30, bias1[h])
    wait_bytes(grad_recv, 1, 7, sems.at[1])
    dshifted = dot(consts["oct_to_tok"][...], grad_recv[...].reshape(256, WIDTH))
    wait_bytes(x_recv, 1, 7, sems.at[3])
    shifted = dot(consts["oct_to_tok"][...], x_recv[...].reshape(256, WIDTH))

    block_forward(shifted, 1, w, bias1, saved, True)
    gelu_slope(1, saved)
    dmiddle = block_backward(dshifted, 1, w, saved)
    octants = dot(consts["tok_to_oct"][...], dmiddle.astype(bf16))
    back_send[...] = octants.astype(bf16).reshape(8, 32, WIDTH)
    send_octants(back_send, back_recv, sems.at[4], sems.at[5], False)
    gelu_slope(0, saved)
    wait_bytes(back_recv, 0, 7, sems.at[5])
    dfirst = dot(consts["oct_to_tok"][...], back_recv[...].reshape(256, WIDTH))
    dlatent = block_backward(dfirst, 0, w, saved).astype(bf16)

    upper_terms = dot(patch_upper[...], dlatent, TN)
    surface_terms = dot(patch_surface[...], dlatent, TN)
    both = jnp.concatenate((upper_terms, surface_terms), 0)
    terms[0:14, :, :] = both[:, :128].astype(bf16).reshape(14, 16, 128)
    low = both[:, 128:]
    low = jnp.concatenate((low[:112], low[112:]), 1)
    terms[14:21, :, :] = low.astype(bf16).reshape(7, 16, 128)

    def scatter(d, carry):
        peer = lax.rem(lon + d, lon_count)

        @pl.when(peer < owners)
        def _():
            pltpu.make_async_remote_copy(
                src_ref=terms.at[pl.ds(peer * unit, unit)],
                dst_ref=held.at[pl.ds((d - 1) * unit, unit)],
                send_sem=sems.at[6],
                recv_sem=sems.at[7],
                device_id={"lon": peer},
                device_id_type=MESH,
            ).start()

        return carry

    lax.fori_loop(1, lon_count, scatter, 0)

    grads = dot(consts["tok_to_nat"][...], dlatent).astype(bf16)
    for z in range(2):
        for a in range(6):
            k = (z * 6 + a) * 16
            latent_out[z, a] = grads[k : k + 16][:12]

    @pl.when(lon < owners)
    def _():
        wait_bytes(held, 0, (lon_count - 1) * unit, sems.at[7])
        total = terms[pl.ds(lon * unit, unit)].astype(f32)
        for d in range(lon_count - 1):
            total = total + held[d * unit : d * unit + unit].astype(f32)
        piece[...] = total.astype(bf16)
        across[pl.ds(mine * unit, unit)] = total.astype(bf16)

        def exchange(d, carry):
            pltpu.make_async_remote_copy(
                src_ref=piece,
                dst_ref=across.at[pl.ds(mine * unit, unit)],
                send_sem=sems.at[8],
                recv_sem=sems.at[9],
                device_id=peer_of(d),
                device_id_type=MESH,
            ).start()
            return carry

        lax.fori_loop(1, group, exchange, 0)
        wait_bytes(across, 0, (group - 1) * unit, sems.at[9])
        whole = across[0:unit].astype(f32)
        for d in range(1, group):
            whole = whole + across[d * unit : d * unit + unit].astype(f32)
        last[...] = whole.astype(bf16)
        result[pl.ds(lon * unit, unit)] = whole.astype(bf16)

        def gather(d, carry):
            pltpu.make_async_remote_copy(
                src_ref=last,
                dst_ref=result.at[pl.ds(lon * unit, unit)],
                send_sem=sems.at[10],
                recv_sem=sems.at[11],
                device_id={"lon": lax.rem(lon + d, lon_count)},
                device_id_type=MESH,
            ).start()
            return carry

        lax.fori_loop(1, lon_count, gather, 0)
        wait_bytes(terms, 0, (owners - 1) * unit, sems.at[6])
        wait_bytes(across, 0, (group - 1) * unit, sems.at[8])
        wait_bytes(result, 0, (owners - 1) * unit, sems.at[11])
        wait_bytes(held, 0, (lon_count - 1) * unit, sems.at[10])

    @pl.when(lon >= owners)
    def _():
        wait_bytes(terms, 0, owners * unit, sems.at[6])
        wait_bytes(result, 0, owners * unit, sems.at[11])

    scale = float(4 * 6 * lat_count * 12 * lon_count) ** (-0.5)
    high = result[0:14].astype(f32).reshape(224, 128) * scale
    low = result[14:21].astype(f32).reshape(112, 128) * scale
    upper_out[:, 0:128] = high[:160]
    surface_out[:, 0:128] = high[160:]
    upper_out[0:112, 128:192] = low[:, :64]
    upper_out[112:160, 128:192] = low[:48, 64:]
    surface_out[:, 128:192] = low[48:, 64:]
    wait_bytes(grad_send, 0, 7, sems.at[0])
    wait_bytes(x_send, 0, 7, sems.at[2])
    wait_bytes(back_send, 0, 7, sems.at[4])


def on_device(
    upper_fields,
    surface_fields,
    upper_embed,
    surface_embed,
    norm_gains,
    qkv_weight,
    proj_weight,
    up_weight,
    down_weight,
    earth_bias,
    out_grad,
):
    consts = tables()
    operands = {
        "upper": upper_fields,
        "surface": surface_fields,
        "pick": consts["pick"],
        "key_tok": consts["key_tok"],
        "key_row": consts["key_row"],
        "fold_upper": consts["fold_upper"],
        "fold_surface": consts["fold_surface"],
        "upper_embed": upper_embed,
        "surface_embed": surface_embed,
        "table": earth_bias.reshape(2, HEADS, -1),
        "spread": consts["spread"],
        "grad": out_grad,
        "nat_to_oct": consts["nat_to_oct"],
        "gains": norm_gains,
        "qkv": qkv_weight,
        "heads": consts["heads"],
        "proj": proj_weight,
        "up": up_weight,
        "down": down_weight.swapaxes(1, 2),
        "tok_to_oct": consts["tok_to_oct"],
        "oct_to_tok": consts["oct_to_tok"],
        "tok_to_nat": consts["tok_to_nat"],
        "place_col": consts["place_col"],
        "place_row": consts["place_row"],
    }
    names = tuple(operands)
    lon_count = lax.axis_size("lon")
    group = lax.axis_size("lat") * lax.axis_size("section")
    unit = -(-21 // lon_count)
    owners = -(-21 // unit)
    vmem = pl.BlockSpec(memory_space=pltpu.VMEM)
    return pl.pallas_call(
        functools.partial(whole_kernel, names, owners, unit),
        out_shape=(
            jax.ShapeDtypeStruct(out_grad.shape, bf16),
            jax.ShapeDtypeStruct((160, WIDTH), f32),
            jax.ShapeDtypeStruct((64, WIDTH), f32),
        ),
        in_specs=[pl.BlockSpec(memory_space=pltpu.HBM)] * len(names),
        out_specs=(vmem,) * 3,
        scratch_shapes=[
            pltpu.VMEM((FIELD_ROWS, 48), f32),
            pltpu.VMEM((12, 16, WIDTH), f32),
            pltpu.VMEM((2, 96, 138), f32),
            pltpu.VMEM((96, 276), f32),
            pltpu.VMEM((HEADS, TOKENS, TOKENS), f32),
            pltpu.VMEM((HEADS, TOKENS, TOKENS), f32),
            pltpu.VMEM((2, TOKENS, 3 * WIDTH), bf16),
            pltpu.VMEM((2, HEADS, TOKENS, TOKENS), f32),
            pltpu.VMEM((2, TOKENS, WIDTH), f32),
            pltpu.VMEM((2, TOKENS, 1), f32),
            pltpu.VMEM((2, TOKENS, WIDTH), f32),
            pltpu.VMEM((2, TOKENS, 1), f32),
            pltpu.VMEM((2, TOKENS, 768), f32),
            pltpu.VMEM((TOKENS, 768), f32),
            pltpu.VMEM((TOKENS, 160), bf16),
            pltpu.VMEM((TOKENS, 64), bf16),
            pltpu.VMEM((8, 32, WIDTH), bf16),
            pltpu.VMEM((8, 32, WIDTH), bf16),
            pltpu.VMEM((8, 32, WIDTH), bf16),
            pltpu.VMEM((8, 32, WIDTH), bf16),
            pltpu.VMEM((8, 32, WIDTH), bf16),
            pltpu.VMEM((8, 32, WIDTH), bf16),
            pltpu.VMEM((owners * unit, 16, 128), bf16),
            pltpu.VMEM(((lon_count - 1) * unit, 16, 128), bf16),
            pltpu.VMEM((unit, 16, 128), bf16),
            pltpu.VMEM((group * unit, 16, 128), bf16),
            pltpu.VMEM((unit, 16, 128), bf16),
            pltpu.VMEM((owners * unit, 16, 128), bf16),
            pltpu.SemaphoreType.DMA((12,)),
            *(pltpu.VMEM(a.shape, a.dtype) for a in operands.values()),
            pltpu.SemaphoreType.DMA((len(names),)),
        ],
        compiler_params=pltpu.CompilerParams(
            collective_id=0, has_side_effects=True, vmem_limit_bytes=int(56 * 2**20)
        ),
    )(*operands.values())


def solution(mesh):
    placed = (
        P(None, None, "lat", "lon"),
        P(None, "lat", "lon"),
        P(),
        P(),
        P(),
        P(),
        P(),
        P(),
        P(),
        P(None, "lat", "section", None, None),
        P("section", "lat", "lon", None),
    )
    return jax.shard_map(
        on_device,
        mesh=mesh,
        in_specs=placed,
        out_specs=(P("section", "lat", "lon", None), P(), P()),
        check_vma=False,
    )
```

```python
import functools

import jax
import jax.numpy as jnp
import numpy as np
from jax import lax
from jax.experimental import pallas as pl
from jax.experimental.pallas import tpu as pltpu
from jax.sharding import PartitionSpec as P

MESH = pl.DeviceIdType.MESH
f32 = jnp.float32
bf16 = jnp.bfloat16
norm_eps = 1e-05
HEADS = 6
TOKENS = 144
WIDTH = 192
FIELD_ROWS = 640
NN = (((1,), (0,)), ((), ()))
NT = (((1,), (1,)), ((), ()))
TN = (((0,), (0,)), ((), ()))


def dot(a, b, dims=NN):
    return lax.dot_general(a, b, dims, preferred_element_type=f32)


def tables():
    t = np.arange(TOKENS)
    col, level, row = t // 12, t // 6 % 2, t % 6
    octant = (col // 6) * 4 + level * 2 + row // 3
    inner = (col % 6) * 3 + row % 3
    natural = (row * 12 + col) * 2 + level

    def packing(order):
        pack = np.zeros((256, 3, TOKENS))
        pack[octant * 32 + inner, 0, order] = 1
        first = inner < 9
        pack[(octant * 32 + 18 + inner)[first], 1, order[first]] = 1
        pack[(octant * 32 + 9 + inner)[~first], 2, order[~first]] = 1
        return pack.reshape(256, 3 * TOKENS)

    pack_tok = packing(t)
    tok_to_nat = np.zeros((TOKENS, TOKENS))
    tok_to_nat[natural, t] = 1
    pick = np.zeros((4, TOKENS, 48))
    for c in range(4):
        pick[c, t, 4 * col + c] = 1
    key_row = np.full((2, 1, FIELD_ROWS), -1.0)
    fold_upper = np.zeros((4, 256, 160))
    fold_surface = np.zeros((4, 128, 64))
    for v in range(5):
        for a in range(2):
            for y in range(24):
                r = (v * 2 + a) * 24 + y
                key_row[1, 0, r] = y // 4
                key_row[:, 0, 256 + r] = 8 + y // 4
                for c in range(4):
                    fold_upper[c, r, v * 32 + a * 16 + (y % 4) * 4 + c] = 1
    for v in range(4):
        for y in range(24):
            r = v * 24 + y
            key_row[0, 0, 512 + r] = y // 4
            for c in range(4):
                fold_surface[c, r, v * 16 + (y % 4) * 4 + c] = 1
    key_tok = (level * 8 + row).reshape(TOKENS, 1)
    spread = np.zeros((2, 138, 276))
    for z in range(2):
        for a in range(6):
            for k in range(23):
                spread[z, a * 23 + k, (22 - k) * 12 + z * 6 + a] = 1
    heads = np.zeros((HEADS, 1, WIDTH))
    for h in range(HEADS):
        heads[h, 0, 32 * h : 32 * h + 32] = 1
    place_col = np.stack((level, row // 3)).reshape(2, TOKENS, 1)
    place_row = np.stack((level, row // 3)).reshape(2, 1, TOKENS)
    return {
        "pack_tok": pack_tok.astype(jnp.bfloat16),
        "unpack_tok": pack_tok.T.astype(jnp.bfloat16),
        "pack_nat": packing(natural).astype(jnp.bfloat16),
        "tok_to_nat": tok_to_nat.astype(jnp.bfloat16),
        "pick": pick.astype(jnp.bfloat16),
        "key_row": key_row.astype(np.float32),
        "key_tok": key_tok.astype(np.float32),
        "fold_upper": fold_upper.astype(jnp.bfloat16),
        "fold_surface": fold_surface.astype(jnp.bfloat16),
        "spread": spread.astype(jnp.bfloat16),
        "heads": heads.astype(np.float32),
        "place_col": place_col.astype(np.float32),
        "place_row": place_row.astype(np.float32),
    }


def centre(values):
    average = jnp.mean(values, -1, keepdims=True)
    centred = values - average
    variance = jnp.mean(centred * centred, -1, keepdims=True)
    scale = lax.rsqrt(variance + norm_eps)
    return centred * scale, scale


def norm_backward(unit, scale, gain, cotangent):
    scaled = cotangent * gain
    first = jnp.mean(scaled, -1, keepdims=True)
    second = jnp.mean(scaled * unit, -1, keepdims=True)
    return scale * (scaled - first - unit * second)


def build_bias(table_ref, b, spread_ref, tab, strip, bias):
    for z in range(2):
        for zt in range(2):
            for a in range(6):
                start = ((zt * 2 + z) * 6 + a) * 138
                tab[z, (zt * 6 + a) * 8 : (zt * 6 + a) * 8 + 6, :] = table_ref[6 * b : 6 * b + 6, 0, start : start + 138]
    total = None
    for z in range(2):
        rest = tab[z]
        for part in range(3):
            piece = rest.astype(bf16)
            rest = rest - piece.astype(f32)
            term = dot(piece, spread_ref[z])
            total = term if total is None else total + term
    strip[...] = total
    for h in range(HEADS):
        lines = jnp.concatenate([strip[8 * k + h : 8 * k + h + 1, :] for k in range(12)], 0)
        for o in range(12):
            bias[h, 12 * o : 12 * o + 12, :] = lines[:, 12 * (11 - o) : 12 * (11 - o) + TOKENS]


def block_forward(x, b, w, bias, saved, final):
    unit0, scale0 = centre(x)
    hidden = (unit0 * w["gains"][b, 0:1, :]).astype(bf16)
    qkv = dot(hidden, w["qkv"][b]).astype(bf16)
    saved["qkv"][b] = qkv
    query = qkv[:, :WIDTH]
    key = qkv[:, WIDTH : 2 * WIDTH]
    value = qkv[:, 2 * WIDTH :]
    mixed = None
    for h in range(HEADS):
        head = w["heads"][h]
        score = dot(query * head.astype(bf16), key, NT) * 32 ** (-0.5) + bias[h]
        expo = jnp.exp(score - jnp.max(score, -1, keepdims=True))
        prob = expo / jnp.sum(expo, -1, keepdims=True)
        saved["prob"][b, h] = prob
        part = dot(prob.astype(bf16), value) * head
        mixed = part if mixed is None else mixed + part
    resid = x + dot(mixed.astype(bf16), w["proj"][b])
    unit1, scale1 = centre(resid)
    normed = (unit1 * w["gains"][b, 1:2, :]).astype(bf16)
    upward = dot(normed, w["up"][b])
    saved["unit0"][b] = unit0
    saved["scale0"][b] = scale0
    saved["unit1"][b] = unit1
    saved["scale1"][b] = scale1
    saved["upward"][b] = upward
    if final:
        return None
    active = 0.5 * upward * (1.0 + lax.erf(upward * 2 ** (-0.5)))
    return resid + dot(active.astype(bf16), w["down"][b], NT)


def gelu_slope(b, saved):
    upward = saved["upward"][b]
    slope = 0.5 * (1.0 + lax.erf(upward * 2 ** (-0.5)))
    saved["slope"][...] = slope + upward * jnp.exp(-0.5 * upward * upward) * (2 * np.pi) ** (-0.5)


def block_backward(dout, b, w, saved):
    dactive = dot(dout.astype(bf16), w["down"][b]).astype(bf16).astype(f32)
    dupward = dactive * saved["slope"][...]
    dnormed = dot(dupward.astype(bf16), w["up"][b], NT).astype(bf16).astype(f32)
    dresid = dout + norm_backward(saved["unit1"][b], saved["scale1"][b], w["gains"][b, 1:2, :], dnormed)
    dmixed = dot(dresid.astype(bf16), w["proj"][b], NT).astype(bf16)
    qkv = saved["qkv"][b]
    query = qkv[:, :WIDTH]
    key = qkv[:, WIDTH : 2 * WIDTH]
    value = qkv[:, 2 * WIDTH :]
    dquery = dkey = dvalue = None
    for h in range(HEADS):
        head = w["heads"][h]
        narrow = head.astype(bf16)
        prob = saved["prob"][b, h]
        dmixed_h = dmixed * narrow
        dweights = dot(dmixed_h, value, NT).astype(bf16).astype(f32)
        dv = dot(prob.astype(bf16), dmixed_h, TN)
        inner = jnp.sum(dweights * prob, -1, keepdims=True)
        dscore = (prob * (dweights - inner) * 32 ** (-0.5)).astype(bf16)
        dq = dot(dscore, key) * head
        dk = dot(dscore, query * narrow, TN)
        dquery = dq if dquery is None else dquery + dq
        dkey = dk if dkey is None else dkey + dk
        dvalue = dv if dvalue is None else dvalue + dv
    dqkv = jnp.concatenate((dquery, dkey, dvalue), 1).astype(bf16)
    dhidden = dot(dqkv, w["qkv"][b], NT).astype(bf16).astype(f32)
    return dresid + norm_backward(saved["unit0"][b], saved["scale0"][b], w["gains"][b, 0:1, :], dhidden)


def pack_octants(pack, tokens):
    low, high = tokens[:, :128], tokens[:, 128:]
    empty = jnp.zeros_like(high)
    parts = (low, jnp.concatenate((high, empty), 1), jnp.concatenate((empty, high), 1))
    rows = jnp.concatenate([part.astype(bf16) for part in parts], 0)
    return dot(pack, rows).astype(bf16).reshape(8, 32, 128)


def unpack_octants(unpack, octants):
    parts = dot(unpack, octants.reshape(256, 128))
    low = parts[:TOKENS]
    left = parts[TOKENS : 2 * TOKENS]
    right = parts[2 * TOKENS :]
    return jnp.concatenate((low, left[:, :64] + right[:, 64:]), 1)


def wait_bytes(buffer, start, count, sem):
    view = buffer.at[pl.ds(start, count)]
    pltpu.make_async_copy(view, view, sem).wait()


class Routes:
    def __init__(self):
        self.lon, self.lat, self.section = (lax.axis_index(n) for n in ("lon", "lat", "section"))
        self.lons, self.lats, self.sections = (lax.axis_size(n) for n in ("lon", "lat", "section"))
        self.inner = min(8, self.lons)
        self.outer = self.lons // self.inner
        hops = lambda d, n: min(d, n - d)
        self.lon_steps = sorted(
            ((a, b) for a in range(self.outer) for b in range(self.inner) if a or b),
            key=lambda d: -(2 * (d[0] > 0) + hops(d[1], self.inner)),
        )
        self.group_steps = sorted(
            ((a, b) for a in range(self.sections) for b in range(self.lats) if a or b),
            key=lambda d: -(4 * d[0] + hops(d[1], self.lats) / 2),
        )

    def lon_peer(self, step):
        outer = lax.rem(self.lon // self.inner + step[0], self.outer)
        return outer * self.inner + lax.rem(self.lon + step[1], self.inner)

    def group_peer(self, step):
        target = {}
        if step[0]:
            target["section"] = lax.rem(self.section + step[0], self.sections)
        if step[1]:
            target["lat"] = lax.rem(self.lat + step[1], self.lats)
        return target

    def corner(self, step, sign):
        target = {}
        if step[0]:
            target["lon"] = lax.rem(self.lon + sign + self.lons, self.lons)
        if step[1]:
            target["section"] = 1 - self.section
        if step[2]:
            target["lat"] = lax.rem(self.lat + sign + self.lats, self.lats)
        return target


def send_octants(routes, src, dst, send_sem, recv_sem, forward):
    for far in (7, 3, 6, 2, 5, 1, 4):
        step = (far >> 2, far >> 1 & 1, far & 1)
        k = 7 - far if forward else far
        pltpu.make_async_remote_copy(
            src_ref=src.at[k],
            dst_ref=dst.at[7 - k],
            send_sem=send_sem,
            recv_sem=recv_sem,
            device_id=routes.corner(step, -1 if forward else 1),
            device_id_type=MESH,
        ).start()
    stay = 7 if forward else 0
    dst[7 - stay] = src[stay]


class Loads:
    def __init__(self, names, sources, targets, sems):
        self.targets = dict(zip(names, targets))
        self.copies = {}
        for i, name in enumerate(names):
            copy = pltpu.make_async_copy(sources[i], targets[i], sems.at[i])
            copy.start()
            self.copies[name] = copy

    def __getitem__(self, name):
        copy = self.copies.pop(name, None)
        if copy is not None:
            copy.wait()
        return self.targets[name]


def whole_kernel(names, owners, unit, *refs):
    count = len(names)
    consts = Loads(names, refs[:count], refs[-count - 1 : -1], refs[-1])
    (
        latent_out,
        upper_out,
        surface_out,
        field,
        tab,
        strip,
        bias0,
        bias1,
        qkv_s,
        prob_s,
        unit0_s,
        scale0_s,
        unit1_s,
        scale1_s,
        upward_s,
        slope_s,
        patch_upper,
        patch_surface,
        grad_send,
        grad_recv,
        x_send,
        x_recv,
        back_send,
        back_recv,
        terms,
        held,
        piece,
        across,
        last,
        result,
        latent_s,
        upper_s,
        surface_s,
        sems,
    ) = refs[count : -count - 1]
    routes = Routes()
    lon, lat, section = routes.lon, routes.lat, routes.section
    lon_count, lat_count, section_count = routes.lons, routes.lats, routes.sections
    group = lat_count * section_count
    mine = section * lat_count + lat
    barrier = pltpu.get_barrier_semaphore()
    targets = [routes.corner(step, sign) for step in ((1, 1, 1), (1, 1, 0), (1, 0, 1)) for sign in (-1, 1)]
    targets += [{"lon": routes.lon_peer(step)} for step in routes.lon_steps]
    targets += [routes.group_peer(step) for step in routes.group_steps]
    for target in targets:
        pl.semaphore_signal(barrier, inc=1, device_id=target, device_id_type=MESH)

    field[240:256, :] = jnp.zeros((16, 48), f32)
    field[496:512, :] = jnp.zeros((16, 48), f32)
    field[608:640, :] = jnp.zeros((32, 48), f32)
    for v in range(5):
        for a in range(2):
            row = (v * 2 + a) * 24
            field[row : row + 24, :] = consts["upper"][v, 2 + a].astype(f32)
            field[256 + row : 256 + row + 24, :] = consts["upper"][v, 4 * section + a].astype(f32)
    for v in range(4):
        field[512 + 24 * v : 512 + 24 * v + 24, :] = consts["surface"][v].astype(f32)
    fields = field[...].astype(bf16)
    same = consts["key_tok"][...] == consts["key_row"][section]
    upper_total = surface_total = None
    for c in range(4):
        spreads = jnp.where(same, dot(consts["pick"][c], fields, NT), 0.0)
        upper_c = (spreads[:, :256] + spreads[:, 256:512]).astype(bf16)
        surface_c = spreads[:, 512:].astype(bf16)
        upper_c = dot(upper_c, consts["fold_upper"][c])
        surface_c = dot(surface_c, consts["fold_surface"][c])
        upper_total = upper_c if upper_total is None else upper_total + upper_c
        surface_total = surface_c if surface_total is None else surface_total + surface_c
    patch_upper[...] = upper_total.astype(bf16)
    patch_surface[...] = surface_total.astype(bf16)
    latent = dot(patch_upper[...], consts["upper_embed"][...])
    latent = latent + dot(patch_surface[...], consts["surface_embed"][...])
    latent = latent.astype(bf16).astype(f32)
    build_bias(consts["table"], 0, consts["spread"], tab, strip, bias0)

    w = consts
    saved = {
        "qkv": qkv_s,
        "prob": prob_s,
        "unit0": unit0_s,
        "scale0": scale0_s,
        "unit1": unit1_s,
        "scale1": scale1_s,
        "upward": upward_s,
        "slope": slope_s,
    }
    first = block_forward(latent, 0, w, bias0, saved, False)
    x_send[...] = pack_octants(consts["pack_tok"][...], first)
    pl.semaphore_wait(barrier, len(targets))
    send_octants(routes, x_send, x_recv, sems.at[2], sems.at[3], True)

    out_grad = consts["grad"][...].astype(f32).reshape(TOKENS, WIDTH)
    grad_send[...] = pack_octants(consts["pack_nat"][...], out_grad)
    send_octants(routes, grad_send, grad_recv, sems.at[0], sems.at[1], True)
    build_bias(consts["table"], 1, consts["spread"], tab, strip, bias1)
    last_section = (section == section_count - 1).astype(f32)
    last_band = (lat == lat_count - 1).astype(f32)
    apart = jnp.abs(consts["place_col"][0] - consts["place_row"][0]) * last_section
    apart = apart + jnp.abs(consts["place_col"][1] - consts["place_row"][1]) * last_band
    for h in range(HEADS):
        bias1[h] = jnp.where(apart > 0.5, -1e30, bias1[h])
    wait_bytes(x_recv, 1, 7, sems.at[3])
    shifted = unpack_octants(consts["unpack_tok"][...], x_recv[...])
    block_forward(shifted, 1, w, bias1, saved, True)
    gelu_slope(1, saved)
    wait_bytes(grad_recv, 1, 7, sems.at[1])
    dshifted = unpack_octants(consts["unpack_tok"][...], grad_recv[...])
    dmiddle = block_backward(dshifted, 1, w, saved)
    back_send[...] = pack_octants(consts["pack_tok"][...], dmiddle)
    send_octants(routes, back_send, back_recv, sems.at[4], sems.at[5], False)
    gelu_slope(0, saved)
    wait_bytes(back_recv, 0, 7, sems.at[5])
    dfirst = unpack_octants(consts["unpack_tok"][...], back_recv[...])
    dlatent = block_backward(dfirst, 0, w, saved).astype(bf16)

    upper_terms = dot(patch_upper[...], dlatent, TN)
    surface_terms = dot(patch_surface[...], dlatent, TN)
    both = jnp.concatenate((upper_terms, surface_terms), 0)
    terms[0:14, :, :] = both[:, :128].astype(bf16).reshape(14, 16, 128)
    low = both[:, 128:]
    low = jnp.concatenate((low[:112], low[112:]), 1)
    terms[14:21, :, :] = low.astype(bf16).reshape(7, 16, 128)

    for k, step in enumerate(routes.lon_steps):
        peer = routes.lon_peer(step)

        @pl.when(peer < owners)
        def _():
            pltpu.make_async_remote_copy(
                src_ref=terms.at[pl.ds(peer * unit, unit)],
                dst_ref=held.at[pl.ds(k * unit, unit)],
                send_sem=sems.at[6],
                recv_sem=sems.at[7],
                device_id={"lon": peer},
                device_id_type=MESH,
            ).start()

    latent_s[...] = dot(consts["tok_to_nat"][...], dlatent).reshape(6, 12, 2, WIDTH).astype(bf16)
    latent_copy = pltpu.make_async_copy(latent_s, latent_out, sems.at[12])
    latent_copy.start()

    @pl.when(lon < owners)
    def _():
        wait_bytes(held, 0, (lon_count - 1) * unit, sems.at[7])
        total = terms[pl.ds(lon * unit, unit)].astype(f32)
        for d in range(lon_count - 1):
            total = total + held[d * unit : d * unit + unit].astype(f32)
        piece[...] = total.astype(bf16)
        across[pl.ds(mine * unit, unit)] = total.astype(bf16)

        for step in routes.group_steps:
            pltpu.make_async_remote_copy(
                src_ref=piece,
                dst_ref=across.at[pl.ds(mine * unit, unit)],
                send_sem=sems.at[8],
                recv_sem=sems.at[9],
                device_id=routes.group_peer(step),
                device_id_type=MESH,
            ).start()

        wait_bytes(across, 0, (group - 1) * unit, sems.at[9])
        whole = across[0:unit].astype(f32)
        for d in range(1, group):
            whole = whole + across[d * unit : d * unit + unit].astype(f32)
        last[...] = whole.astype(bf16)
        result[pl.ds(lon * unit, unit)] = whole.astype(bf16)

        for step in routes.lon_steps:
            pltpu.make_async_remote_copy(
                src_ref=last,
                dst_ref=result.at[pl.ds(lon * unit, unit)],
                send_sem=sems.at[10],
                recv_sem=sems.at[11],
                device_id={"lon": routes.lon_peer(step)},
                device_id_type=MESH,
            ).start()

        wait_bytes(terms, 0, (owners - 1) * unit, sems.at[6])
        wait_bytes(across, 0, (group - 1) * unit, sems.at[8])
        wait_bytes(result, 0, (owners - 1) * unit, sems.at[11])
        wait_bytes(held, 0, (lon_count - 1) * unit, sems.at[10])

    @pl.when(lon >= owners)
    def _():
        wait_bytes(terms, 0, owners * unit, sems.at[6])
        wait_bytes(result, 0, owners * unit, sems.at[11])

    scale = float(4 * 6 * lat_count * 12 * lon_count) ** (-0.5)
    high = result[0:14].astype(f32).reshape(224, 128) * scale
    low = result[14:21].astype(f32).reshape(112, 128) * scale
    upper_s[:, 0:128] = high[:160]
    surface_s[:, 0:128] = high[160:]
    upper_s[0:112, 128:192] = low[:, :64]
    upper_s[112:160, 128:192] = low[:48, 64:]
    surface_s[:, 128:192] = low[48:, 64:]
    upper_copy = pltpu.make_async_copy(upper_s, upper_out, sems.at[13])
    surface_copy = pltpu.make_async_copy(surface_s, surface_out, sems.at[14])
    upper_copy.start()
    surface_copy.start()
    upper_copy.wait()
    surface_copy.wait()
    latent_copy.wait()
    wait_bytes(grad_send, 0, 7, sems.at[0])
    wait_bytes(x_send, 0, 7, sems.at[2])
    wait_bytes(back_send, 0, 7, sems.at[4])


def on_device(
    upper_fields,
    surface_fields,
    upper_embed,
    surface_embed,
    norm_gains,
    qkv_weight,
    proj_weight,
    up_weight,
    down_weight,
    earth_bias,
    out_grad,
):
    consts = tables()
    operands = {
        "upper": upper_fields,
        "surface": surface_fields,
        "pick": consts["pick"],
        "key_tok": consts["key_tok"],
        "key_row": consts["key_row"],
        "fold_upper": consts["fold_upper"],
        "fold_surface": consts["fold_surface"],
        "upper_embed": upper_embed,
        "surface_embed": surface_embed,
        "table": earth_bias.reshape(2 * HEADS, 1, -1),
        "spread": consts["spread"],
        "grad": out_grad.transpose(1, 2, 0, 3),
        "gains": norm_gains,
        "qkv": qkv_weight,
        "heads": consts["heads"],
        "proj": proj_weight,
        "up": up_weight,
        "down": down_weight.swapaxes(1, 2),
        "pack_tok": consts["pack_tok"],
        "pack_nat": consts["pack_nat"],
        "unpack_tok": consts["unpack_tok"],
        "tok_to_nat": consts["tok_to_nat"],
        "place_col": consts["place_col"],
        "place_row": consts["place_row"],
    }
    names = tuple(operands)
    lon_count = lax.axis_size("lon")
    group = lax.axis_size("lat") * lax.axis_size("section")
    unit = -(-21 // lon_count)
    owners = -(-21 // unit)
    hbm = pl.BlockSpec(memory_space=pltpu.HBM)
    latent_grad, upper_grad, surface_grad = pl.pallas_call(
        functools.partial(whole_kernel, names, owners, unit),
        out_shape=(
            jax.ShapeDtypeStruct((6, 12, 2, WIDTH), bf16),
            jax.ShapeDtypeStruct((160, WIDTH), f32),
            jax.ShapeDtypeStruct((64, WIDTH), f32),
        ),
        in_specs=[hbm] * len(names),
        out_specs=(hbm,) * 3,
        scratch_shapes=[
            pltpu.VMEM((FIELD_ROWS, 48), f32),
            pltpu.VMEM((2, 96, 138), f32),
            pltpu.VMEM((96, 276), f32),
            pltpu.VMEM((HEADS, TOKENS, TOKENS), f32),
            pltpu.VMEM((HEADS, TOKENS, TOKENS), f32),
            pltpu.VMEM((2, TOKENS, 3 * WIDTH), bf16),
            pltpu.VMEM((2, HEADS, TOKENS, TOKENS), f32),
            pltpu.VMEM((2, TOKENS, WIDTH), f32),
            pltpu.VMEM((2, TOKENS, 1), f32),
            pltpu.VMEM((2, TOKENS, WIDTH), f32),
            pltpu.VMEM((2, TOKENS, 1), f32),
            pltpu.VMEM((2, TOKENS, 768), f32),
            pltpu.VMEM((TOKENS, 768), f32),
            pltpu.VMEM((TOKENS, 160), bf16),
            pltpu.VMEM((TOKENS, 64), bf16),
            pltpu.VMEM((8, 32, 128), bf16),
            pltpu.VMEM((8, 32, 128), bf16),
            pltpu.VMEM((8, 32, 128), bf16),
            pltpu.VMEM((8, 32, 128), bf16),
            pltpu.VMEM((8, 32, 128), bf16),
            pltpu.VMEM((8, 32, 128), bf16),
            pltpu.VMEM((owners * unit, 16, 128), bf16),
            pltpu.VMEM(((lon_count - 1) * unit, 16, 128), bf16),
            pltpu.VMEM((unit, 16, 128), bf16),
            pltpu.VMEM((group * unit, 16, 128), bf16),
            pltpu.VMEM((unit, 16, 128), bf16),
            pltpu.VMEM((owners * unit, 16, 128), bf16),
            pltpu.VMEM((6, 12, 2, WIDTH), bf16),
            pltpu.VMEM((160, WIDTH), f32),
            pltpu.VMEM((64, WIDTH), f32),
            pltpu.SemaphoreType.DMA((15,)),
            *(pltpu.VMEM(a.shape, a.dtype) for a in operands.values()),
            pltpu.SemaphoreType.DMA((len(names),)),
        ],
        compiler_params=pltpu.CompilerParams(
            collective_id=0, has_side_effects=True, vmem_limit_bytes=int(56 * 2**20)
        ),
    )(*operands.values())
    return latent_grad.transpose(2, 0, 1, 3), upper_grad, surface_grad


def solution(mesh):
    placed = (
        P(None, None, "lat", "lon"),
        P(None, "lat", "lon"),
        P(),
        P(),
        P(),
        P(),
        P(),
        P(),
        P(),
        P(None, "lat", "section", None, None),
        P("section", "lat", "lon", None),
    )
    return jax.shard_map(
        on_device,
        mesh=mesh,
        in_specs=placed,
        out_specs=(P("section", "lat", "lon", None), P(), P()),
        check_vma=False,
    )
```

```python
import functools
import itertools

import jax
import jax.numpy as jnp
import numpy as np
from jax import lax
from jax.experimental import pallas as pl
from jax.experimental.pallas import tpu as pltpu
from jax.sharding import PartitionSpec as P

MESH = pl.DeviceIdType.MESH
f32 = jnp.float32
bf16 = jnp.bfloat16
norm_eps = 1e-05
HEADS = 6
TOKENS = 144
WIDTH = 192
FIELD_ROWS = 640
NN = (((1,), (0,)), ((), ()))
NT = (((1,), (1,)), ((), ()))
TN = (((0,), (0,)), ((), ()))


def dot(a, b, dims=NN):
    return lax.dot_general(a, b, dims, preferred_element_type=f32)


def tables():
    t = np.arange(TOKENS)
    col, level, row = t // 12, t // 6 % 2, t % 6
    octant = (col // 6) * 4 + level * 2 + row // 3
    inner = (col % 6) * 3 + row % 3
    natural = (row * 12 + col) * 2 + level

    def packing(order):
        pack = np.zeros((256, 3, TOKENS))
        pack[octant * 32 + inner, 0, order] = 1
        first = inner < 9
        pack[(octant * 32 + 18 + inner)[first], 1, order[first]] = 1
        pack[(octant * 32 + 9 + inner)[~first], 2, order[~first]] = 1
        return pack.reshape(256, 3 * TOKENS)

    pack_tok = packing(t)
    tok_to_nat = np.zeros((TOKENS, TOKENS))
    tok_to_nat[natural, t] = 1
    pick = np.zeros((4, TOKENS, 48))
    for c in range(4):
        pick[c, t, 4 * col + c] = 1
    key_row = np.full((2, 1, FIELD_ROWS), -1.0)
    fold_upper = np.zeros((4, 256, 160))
    fold_surface = np.zeros((4, 128, 64))
    for v in range(5):
        for a in range(2):
            for y in range(24):
                r = (v * 2 + a) * 24 + y
                key_row[1, 0, r] = y // 4
                key_row[:, 0, 256 + r] = 8 + y // 4
                for c in range(4):
                    fold_upper[c, r, v * 32 + a * 16 + (y % 4) * 4 + c] = 1
    for v in range(4):
        for y in range(24):
            r = v * 24 + y
            key_row[0, 0, 512 + r] = y // 4
            for c in range(4):
                fold_surface[c, r, v * 16 + (y % 4) * 4 + c] = 1
    key_tok = (level * 8 + row).reshape(TOKENS, 1)
    spread = np.zeros((2, 138, 276))
    for z in range(2):
        for a in range(6):
            for k in range(23):
                spread[z, a * 23 + k, (22 - k) * 12 + z * 6 + a] = 1
    heads = np.zeros((HEADS, 1, WIDTH))
    for h in range(HEADS):
        heads[h, 0, 32 * h : 32 * h + 32] = 1
    place_col = np.stack((level, row // 3)).reshape(2, TOKENS, 1)
    place_row = np.stack((level, row // 3)).reshape(2, 1, TOKENS)
    return {
        "pack_tok": pack_tok.astype(jnp.bfloat16),
        "unpack_tok": pack_tok.T.astype(jnp.bfloat16),
        "pack_nat": packing(natural).astype(jnp.bfloat16),
        "tok_to_nat": tok_to_nat.astype(jnp.bfloat16),
        "pick": pick.astype(jnp.bfloat16),
        "key_row": key_row.astype(np.float32),
        "key_tok": key_tok.astype(np.float32),
        "fold_upper": fold_upper.astype(jnp.bfloat16),
        "fold_surface": fold_surface.astype(jnp.bfloat16),
        "spread": spread.astype(jnp.bfloat16),
        "heads": heads.astype(np.float32),
        "place_col": place_col.astype(np.float32),
        "place_row": place_row.astype(np.float32),
    }


def centre(values):
    average = jnp.mean(values, -1, keepdims=True)
    centred = values - average
    variance = jnp.mean(centred * centred, -1, keepdims=True)
    scale = lax.rsqrt(variance + norm_eps)
    return centred * scale, scale


def norm_backward(unit, scale, gain, cotangent):
    scaled = cotangent * gain
    first = jnp.mean(scaled, -1, keepdims=True)
    second = jnp.mean(scaled * unit, -1, keepdims=True)
    return scale * (scaled - first - unit * second)


def build_bias(table_ref, b, spread_ref, tab, strip, bias):
    for z in range(2):
        for zt in range(2):
            for a in range(6):
                start = ((zt * 2 + z) * 6 + a) * 138
                tab[z, (zt * 6 + a) * 8 : (zt * 6 + a) * 8 + 6, :] = table_ref[6 * b : 6 * b + 6, 0, start : start + 138]
    total = None
    for z in range(2):
        rest = tab[z]
        for part in range(3):
            piece = rest.astype(bf16)
            rest = rest - piece.astype(f32)
            term = dot(piece, spread_ref[z])
            total = term if total is None else total + term
    strip[...] = total
    for h in range(HEADS):
        lines = jnp.concatenate([strip[8 * k + h : 8 * k + h + 1, :] for k in range(12)], 0)
        for o in range(12):
            bias[h, 12 * o : 12 * o + 12, :] = lines[:, 12 * (11 - o) : 12 * (11 - o) + TOKENS]


def block_forward(x, b, w, bias, saved, final):
    unit0, scale0 = centre(x)
    hidden = (unit0 * w["gains"][b, 0:1, :]).astype(bf16)
    qkv = dot(hidden, w["qkv"][b]).astype(bf16)
    saved["qkv"][b] = qkv
    query = qkv[:, :WIDTH]
    key = qkv[:, WIDTH : 2 * WIDTH]
    value = qkv[:, 2 * WIDTH :]
    mixed = None
    for h in range(HEADS):
        head = w["heads"][h]
        score = dot(query * head.astype(bf16), key, NT) * 32 ** (-0.5) + bias[h]
        expo = jnp.exp(score - jnp.max(score, -1, keepdims=True))
        prob = expo / jnp.sum(expo, -1, keepdims=True)
        saved["prob"][b, h] = prob
        part = dot(prob.astype(bf16), value) * head
        mixed = part if mixed is None else mixed + part
    resid = x + dot(mixed.astype(bf16), w["proj"][b])
    unit1, scale1 = centre(resid)
    normed = (unit1 * w["gains"][b, 1:2, :]).astype(bf16)
    upward = dot(normed, w["up"][b])
    saved["unit0"][b] = unit0
    saved["scale0"][b] = scale0
    saved["unit1"][b] = unit1
    saved["scale1"][b] = scale1
    saved["upward"][b] = upward
    if final:
        return None
    active = 0.5 * upward * (1.0 + lax.erf(upward * 2 ** (-0.5)))
    return resid + dot(active.astype(bf16), w["down"][b], NT)


def gelu_slope(b, saved):
    upward = saved["upward"][b]
    slope = 0.5 * (1.0 + lax.erf(upward * 2 ** (-0.5)))
    saved["slope"][...] = slope + upward * jnp.exp(-0.5 * upward * upward) * (2 * np.pi) ** (-0.5)


def block_backward(dout, b, w, saved):
    dactive = dot(dout.astype(bf16), w["down"][b]).astype(bf16).astype(f32)
    dupward = dactive * saved["slope"][...]
    dnormed = dot(dupward.astype(bf16), w["up"][b], NT).astype(bf16).astype(f32)
    dresid = dout + norm_backward(saved["unit1"][b], saved["scale1"][b], w["gains"][b, 1:2, :], dnormed)
    dmixed = dot(dresid.astype(bf16), w["proj"][b], NT).astype(bf16)
    qkv = saved["qkv"][b]
    query = qkv[:, :WIDTH]
    key = qkv[:, WIDTH : 2 * WIDTH]
    value = qkv[:, 2 * WIDTH :]
    dquery = dkey = dvalue = None
    for h in range(HEADS):
        head = w["heads"][h]
        narrow = head.astype(bf16)
        prob = saved["prob"][b, h]
        dmixed_h = dmixed * narrow
        dweights = dot(dmixed_h, value, NT).astype(bf16).astype(f32)
        dv = dot(prob.astype(bf16), dmixed_h, TN)
        inner = jnp.sum(dweights * prob, -1, keepdims=True)
        dscore = (prob * (dweights - inner) * 32 ** (-0.5)).astype(bf16)
        dq = dot(dscore, key) * head
        dk = dot(dscore, query * narrow, TN)
        dquery = dq if dquery is None else dquery + dq
        dkey = dk if dkey is None else dkey + dk
        dvalue = dv if dvalue is None else dvalue + dv
    dqkv = jnp.concatenate((dquery, dkey, dvalue), 1).astype(bf16)
    dhidden = dot(dqkv, w["qkv"][b], NT).astype(bf16).astype(f32)
    return dresid + norm_backward(saved["unit0"][b], saved["scale0"][b], w["gains"][b, 0:1, :], dhidden)


def pack_octants(pack, tokens):
    low, high = tokens[:, :128], tokens[:, 128:]
    empty = jnp.zeros_like(high)
    parts = (low, jnp.concatenate((high, empty), 1), jnp.concatenate((empty, high), 1))
    rows = jnp.concatenate([part.astype(bf16) for part in parts], 0)
    return dot(pack, rows).astype(bf16).reshape(8, 32, 128)


def unpack_octants(unpack, octants):
    parts = dot(unpack, octants.reshape(256, 128))
    low = parts[:TOKENS]
    left = parts[TOKENS : 2 * TOKENS]
    right = parts[2 * TOKENS :]
    return jnp.concatenate((low, left[:, :64] + right[:, 64:]), 1)


def wait_bytes(buffer, start, count, sem):
    view = buffer.at[pl.ds(start, count)]
    pltpu.make_async_copy(view, view, sem).wait()


class Routes:
    def __init__(self):
        self.lon, self.lat, self.section = (lax.axis_index(n) for n in ("lon", "lat", "section"))
        self.lons, self.lats, self.sections = (lax.axis_size(n) for n in ("lon", "lat", "section"))
        self.inner = min(8, self.lons)
        self.outer = self.lons // self.inner
        self.pair_in, self.pair_out = min(2, self.inner), min(2, self.outer)
        self.high = self.lon // self.inner
        self.low = lax.rem(self.lon, self.inner)
        hops = lambda d, n: min(d, n - d)
        near = itertools.product(range(self.pair_out), range(self.pair_in), range(self.lats))
        self.near_steps = sorted(
            (d for d in near if any(d)), key=lambda d: -(d[0] + d[1] + hops(d[2], self.lats) / 2)
        )
        far = itertools.product(
            range(self.sections), range(self.outer // self.pair_out), range(self.inner // self.pair_in)
        )
        self.far_steps = sorted(
            (d for d in far if any(d)),
            key=lambda d: -((4 - 2 * d[1] if d[0] else 2 * d[1]) + 2 * hops(d[2], self.inner // self.pair_in)),
        )

    def near_index(self, step=(0, 0, 0)):
        out = lax.rem(self.high + step[0], self.pair_out)
        into = lax.rem(self.low + step[1], self.pair_in)
        return (out * self.pair_in + into) * self.lats + lax.rem(self.lat + step[2], self.lats)

    def near_peer(self, step):
        target = {}
        if step[0] or step[1]:
            out = self.high // self.pair_out * self.pair_out + lax.rem(self.high + step[0], self.pair_out)
            into = self.low // self.pair_in * self.pair_in + lax.rem(self.low + step[1], self.pair_in)
            target["lon"] = out * self.inner + into
        if step[2]:
            target["lat"] = lax.rem(self.lat + step[2], self.lats)
        return target

    def far_index(self):
        index = self.section * (self.outer // self.pair_out) + self.high // self.pair_out
        return index * (self.inner // self.pair_in) + self.low // self.pair_in

    def far_peer(self, step):
        target = {}
        if step[0]:
            target["section"] = lax.rem(self.section + step[0], self.sections)
        if step[1] or step[2]:
            out = lax.rem(self.high + step[1] * self.pair_out, self.outer)
            target["lon"] = out * self.inner + lax.rem(self.low + step[2] * self.pair_in, self.inner)
        return target

    def corner(self, step, sign):
        target = {}
        if step[0]:
            target["lon"] = lax.rem(self.lon + sign + self.lons, self.lons)
        if step[1]:
            target["section"] = 1 - self.section
        if step[2]:
            target["lat"] = lax.rem(self.lat + sign + self.lats, self.lats)
        return target


def send_octants(routes, src, dst, send_sem, recv_sem, forward):
    for far in (7, 3, 6, 2, 5, 1, 4):
        step = (far >> 2, far >> 1 & 1, far & 1)
        k = 7 - far if forward else far
        pltpu.make_async_remote_copy(
            src_ref=src.at[k],
            dst_ref=dst.at[7 - k],
            send_sem=send_sem,
            recv_sem=recv_sem,
            device_id=routes.corner(step, -1 if forward else 1),
            device_id_type=MESH,
        ).start()
    stay = 7 if forward else 0
    dst[7 - stay] = src[stay]


class Loads:
    def __init__(self, names, sources, targets, sems):
        self.targets = dict(zip(names, targets))
        self.copies = {}
        for i, name in enumerate(names):
            copy = pltpu.make_async_copy(sources[i], targets[i], sems.at[i])
            copy.start()
            self.copies[name] = copy

    def __getitem__(self, name):
        copy = self.copies.pop(name, None)
        if copy is not None:
            copy.wait()
        return self.targets[name]


def whole_kernel(names, owners, unit, *refs):
    count = len(names)
    consts = Loads(names, refs[:count], refs[-count - 1 : -1], refs[-1])
    (
        latent_out,
        upper_out,
        surface_out,
        field,
        tab,
        strip,
        bias0,
        bias1,
        qkv_s,
        prob_s,
        unit0_s,
        scale0_s,
        unit1_s,
        scale1_s,
        upward_s,
        slope_s,
        patch_upper,
        patch_surface,
        grad_send,
        grad_recv,
        x_send,
        x_recv,
        back_send,
        back_recv,
        terms,
        held,
        piece,
        across,
        last,
        result,
        latent_s,
        upper_s,
        surface_s,
        sems,
    ) = refs[count : -count - 1]
    routes = Routes()
    lon, lat, section = routes.lon, routes.lat, routes.section
    lon_count, lat_count, section_count = routes.lons, routes.lats, routes.sections
    count_near, count_far = len(routes.near_steps), len(routes.far_steps)
    owner, mine = routes.near_index(), routes.far_index()
    barrier = pltpu.get_barrier_semaphore()
    corners = sorted(itertools.product(range(2), repeat=3), reverse=True)
    targets = [routes.corner(d, sign) for d in corners[:-1] for sign in (-1, 1) if d != (0, 1, 0) or sign > 0]
    targets += [routes.far_peer(step) for step in routes.far_steps]
    targets += [routes.near_peer(step) for step in routes.near_steps]
    for target in targets:
        pl.semaphore_signal(barrier, inc=1, device_id=target, device_id_type=MESH)

    field[240:256, :] = jnp.zeros((16, 48), f32)
    field[496:512, :] = jnp.zeros((16, 48), f32)
    field[608:640, :] = jnp.zeros((32, 48), f32)
    for v in range(5):
        for a in range(2):
            row = (v * 2 + a) * 24
            field[row : row + 24, :] = consts["upper"][v, 2 + a].astype(f32)
            field[256 + row : 256 + row + 24, :] = consts["upper"][v, 4 * section + a].astype(f32)
    for v in range(4):
        field[512 + 24 * v : 512 + 24 * v + 24, :] = consts["surface"][v].astype(f32)
    fields = field[...].astype(bf16)
    same = consts["key_tok"][...] == consts["key_row"][section]
    upper_total = surface_total = None
    for c in range(4):
        spreads = jnp.where(same, dot(consts["pick"][c], fields, NT), 0.0)
        upper_c = (spreads[:, :256] + spreads[:, 256:512]).astype(bf16)
        surface_c = spreads[:, 512:].astype(bf16)
        upper_c = dot(upper_c, consts["fold_upper"][c])
        surface_c = dot(surface_c, consts["fold_surface"][c])
        upper_total = upper_c if upper_total is None else upper_total + upper_c
        surface_total = surface_c if surface_total is None else surface_total + surface_c
    patch_upper[...] = upper_total.astype(bf16)
    patch_surface[...] = surface_total.astype(bf16)
    latent = dot(patch_upper[...], consts["upper_embed"][...])
    latent = latent + dot(patch_surface[...], consts["surface_embed"][...])
    latent = latent.astype(bf16).astype(f32)
    build_bias(consts["table"], 0, consts["spread"], tab, strip, bias0)

    w = consts
    saved = {
        "qkv": qkv_s,
        "prob": prob_s,
        "unit0": unit0_s,
        "scale0": scale0_s,
        "unit1": unit1_s,
        "scale1": scale1_s,
        "upward": upward_s,
        "slope": slope_s,
    }
    first = block_forward(latent, 0, w, bias0, saved, False)
    x_send[...] = pack_octants(consts["pack_tok"][...], first)
    pl.semaphore_wait(barrier, len(targets))
    send_octants(routes, x_send, x_recv, sems.at[2], sems.at[3], True)

    out_grad = consts["grad"][...].astype(f32).reshape(TOKENS, WIDTH)
    grad_send[...] = pack_octants(consts["pack_nat"][...], out_grad)
    send_octants(routes, grad_send, grad_recv, sems.at[0], sems.at[1], True)
    build_bias(consts["table"], 1, consts["spread"], tab, strip, bias1)
    last_section = (section == section_count - 1).astype(f32)
    last_band = (lat == lat_count - 1).astype(f32)
    apart = jnp.abs(consts["place_col"][0] - consts["place_row"][0]) * last_section
    apart = apart + jnp.abs(consts["place_col"][1] - consts["place_row"][1]) * last_band
    for h in range(HEADS):
        bias1[h] = jnp.where(apart > 0.5, -1e30, bias1[h])
    wait_bytes(x_recv, 1, 7, sems.at[3])
    shifted = unpack_octants(consts["unpack_tok"][...], x_recv[...])
    block_forward(shifted, 1, w, bias1, saved, True)
    gelu_slope(1, saved)
    wait_bytes(grad_recv, 1, 7, sems.at[1])
    dshifted = unpack_octants(consts["unpack_tok"][...], grad_recv[...])
    dmiddle = block_backward(dshifted, 1, w, saved)
    back_send[...] = pack_octants(consts["pack_tok"][...], dmiddle)
    send_octants(routes, back_send, back_recv, sems.at[4], sems.at[5], False)
    gelu_slope(0, saved)
    wait_bytes(back_recv, 0, 7, sems.at[5])
    dfirst = unpack_octants(consts["unpack_tok"][...], back_recv[...])
    dlatent = block_backward(dfirst, 0, w, saved).astype(bf16)

    upper_terms = dot(patch_upper[...], dlatent, TN)
    surface_terms = dot(patch_surface[...], dlatent, TN)
    both = jnp.concatenate((upper_terms, surface_terms), 0)
    terms[0:14, :, :] = both[:, :128].astype(bf16).reshape(14, 16, 128)
    low = both[:, 128:]
    low = jnp.concatenate((low[:112], low[112:]), 1)
    terms[14:21, :, :] = low.astype(bf16).reshape(7, 16, 128)

    for k, step in enumerate(routes.near_steps):
        peer = routes.near_index(step)

        @pl.when(peer < owners)
        def _():
            pltpu.make_async_remote_copy(
                src_ref=terms.at[pl.ds(peer * unit, unit)],
                dst_ref=held.at[pl.ds(k * unit, unit)],
                send_sem=sems.at[6],
                recv_sem=sems.at[7],
                device_id=routes.near_peer(step),
                device_id_type=MESH,
            ).start()

    latent_s[...] = dot(consts["tok_to_nat"][...], dlatent).reshape(6, 12, 2, WIDTH).astype(bf16)
    latent_copy = pltpu.make_async_copy(latent_s, latent_out, sems.at[12])
    latent_copy.start()

    @pl.when(owner < owners)
    def _():
        wait_bytes(held, 0, count_near * unit, sems.at[7])
        total = terms[pl.ds(owner * unit, unit)].astype(f32)
        for d in range(count_near):
            total = total + held[d * unit : d * unit + unit].astype(f32)
        piece[...] = total.astype(bf16)
        across[pl.ds(mine * unit, unit)] = total.astype(bf16)
        for step in routes.far_steps:
            pltpu.make_async_remote_copy(
                src_ref=piece,
                dst_ref=across.at[pl.ds(mine * unit, unit)],
                send_sem=sems.at[8],
                recv_sem=sems.at[9],
                device_id=routes.far_peer(step),
                device_id_type=MESH,
            ).start()

        wait_bytes(across, 0, count_far * unit, sems.at[9])
        whole = across[0:unit].astype(f32)
        for d in range(1, count_far + 1):
            whole = whole + across[d * unit : d * unit + unit].astype(f32)
        last[...] = whole.astype(bf16)
        result[pl.ds(owner * unit, unit)] = whole.astype(bf16)
        for step in routes.near_steps:
            pltpu.make_async_remote_copy(
                src_ref=last,
                dst_ref=result.at[pl.ds(owner * unit, unit)],
                send_sem=sems.at[10],
                recv_sem=sems.at[11],
                device_id=routes.near_peer(step),
                device_id_type=MESH,
            ).start()

        wait_bytes(terms, 0, (owners - 1) * unit, sems.at[6])
        wait_bytes(across, 0, count_far * unit, sems.at[8])
        wait_bytes(result, 0, (owners - 1) * unit, sems.at[11])
        wait_bytes(held, 0, count_near * unit, sems.at[10])

    @pl.when(owner >= owners)
    def _():
        wait_bytes(terms, 0, owners * unit, sems.at[6])
        wait_bytes(result, 0, owners * unit, sems.at[11])

    scale = float(4 * 6 * lat_count * 12 * lon_count) ** (-0.5)
    high = result[0:14].astype(f32).reshape(224, 128) * scale
    low = result[14:21].astype(f32).reshape(112, 128) * scale
    upper_s[:, 0:128] = high[:160]
    surface_s[:, 0:128] = high[160:]
    upper_s[0:112, 128:192] = low[:, :64]
    upper_s[112:160, 128:192] = low[:48, 64:]
    surface_s[:, 128:192] = low[48:, 64:]
    upper_copy = pltpu.make_async_copy(upper_s, upper_out, sems.at[13])
    surface_copy = pltpu.make_async_copy(surface_s, surface_out, sems.at[14])
    upper_copy.start()
    surface_copy.start()
    upper_copy.wait()
    surface_copy.wait()
    latent_copy.wait()
    wait_bytes(grad_send, 0, 7, sems.at[0])
    wait_bytes(x_send, 0, 7, sems.at[2])
    wait_bytes(back_send, 0, 7, sems.at[4])


def hand_over(*refs):
    copies = [pltpu.make_async_copy(refs[k], refs[3 + k], refs[6].at[k]) for k in range(3)]
    for copy in copies:
        copy.start()
    for copy in copies:
        copy.wait()


def on_device(
    upper_fields,
    surface_fields,
    upper_embed,
    surface_embed,
    norm_gains,
    qkv_weight,
    proj_weight,
    up_weight,
    down_weight,
    earth_bias,
    out_grad,
):
    consts = tables()
    operands = {
        "upper": upper_fields,
        "surface": surface_fields,
        "pick": consts["pick"],
        "key_tok": consts["key_tok"],
        "key_row": consts["key_row"],
        "fold_upper": consts["fold_upper"],
        "fold_surface": consts["fold_surface"],
        "upper_embed": upper_embed,
        "surface_embed": surface_embed,
        "table": earth_bias.reshape(2 * HEADS, 1, -1),
        "spread": consts["spread"],
        "grad": out_grad.transpose(1, 2, 0, 3),
        "gains": norm_gains,
        "qkv": qkv_weight,
        "heads": consts["heads"],
        "proj": proj_weight,
        "up": up_weight,
        "down": down_weight.swapaxes(1, 2),
        "pack_tok": consts["pack_tok"],
        "pack_nat": consts["pack_nat"],
        "unpack_tok": consts["unpack_tok"],
        "tok_to_nat": consts["tok_to_nat"],
        "place_col": consts["place_col"],
        "place_row": consts["place_row"],
    }
    names = tuple(operands)
    lon_count = lax.axis_size("lon")
    near = min(4, lon_count) * lax.axis_size("lat")
    if lon_count < 16:
        near = min(2, lon_count) * lax.axis_size("lat")
    group = lon_count * lax.axis_size("lat") * lax.axis_size("section") // near
    unit = -(-21 // near)
    owners = -(-21 // unit)
    hbm = pl.BlockSpec(memory_space=pltpu.HBM)
    latent_grad, upper_grad, surface_grad = pl.pallas_call(
        functools.partial(whole_kernel, names, owners, unit),
        out_shape=(
            jax.ShapeDtypeStruct((6, 12, 2, WIDTH), bf16),
            jax.ShapeDtypeStruct((160, WIDTH), f32),
            jax.ShapeDtypeStruct((64, WIDTH), f32),
        ),
        in_specs=[hbm] * len(names),
        out_specs=(hbm,) * 3,
        scratch_shapes=[
            pltpu.VMEM((FIELD_ROWS, 48), f32),
            pltpu.VMEM((2, 96, 138), f32),
            pltpu.VMEM((96, 276), f32),
            pltpu.VMEM((HEADS, TOKENS, TOKENS), f32),
            pltpu.VMEM((HEADS, TOKENS, TOKENS), f32),
            pltpu.VMEM((2, TOKENS, 3 * WIDTH), bf16),
            pltpu.VMEM((2, HEADS, TOKENS, TOKENS), f32),
            pltpu.VMEM((2, TOKENS, WIDTH), f32),
            pltpu.VMEM((2, TOKENS, 1), f32),
            pltpu.VMEM((2, TOKENS, WIDTH), f32),
            pltpu.VMEM((2, TOKENS, 1), f32),
            pltpu.VMEM((2, TOKENS, 768), f32),
            pltpu.VMEM((TOKENS, 768), f32),
            pltpu.VMEM((TOKENS, 160), bf16),
            pltpu.VMEM((TOKENS, 64), bf16),
            pltpu.VMEM((8, 32, 128), bf16),
            pltpu.VMEM((8, 32, 128), bf16),
            pltpu.VMEM((8, 32, 128), bf16),
            pltpu.VMEM((8, 32, 128), bf16),
            pltpu.VMEM((8, 32, 128), bf16),
            pltpu.VMEM((8, 32, 128), bf16),
            pltpu.VMEM((owners * unit, 16, 128), bf16),
            pltpu.VMEM(((near - 1) * unit, 16, 128), bf16),
            pltpu.VMEM((unit, 16, 128), bf16),
            pltpu.VMEM((group * unit, 16, 128), bf16),
            pltpu.VMEM((unit, 16, 128), bf16),
            pltpu.VMEM((owners * unit, 16, 128), bf16),
            pltpu.VMEM((6, 12, 2, WIDTH), bf16),
            pltpu.VMEM((160, WIDTH), f32),
            pltpu.VMEM((64, WIDTH), f32),
            pltpu.SemaphoreType.DMA((15,)),
            *(pltpu.VMEM(a.shape, a.dtype) for a in operands.values()),
            pltpu.SemaphoreType.DMA((len(names),)),
        ],
        compiler_params=pltpu.CompilerParams(
            collective_id=0, has_side_effects=True, vmem_limit_bytes=int(56 * 2**20)
        ),
    )(*operands.values())
    latent_grad, upper_grad, surface_grad = pl.pallas_call(
        hand_over,
        out_shape=tuple(
            jax.ShapeDtypeStruct(a.shape, a.dtype) for a in (latent_grad, upper_grad, surface_grad)
        ),
        in_specs=[hbm] * 3,
        out_specs=(hbm,) * 3,
        scratch_shapes=[pltpu.SemaphoreType.DMA((3,))],
    )(latent_grad, upper_grad, surface_grad)
    return latent_grad.transpose(2, 0, 1, 3), upper_grad, surface_grad


def solution(mesh):
    placed = (
        P(None, None, "lat", "lon"),
        P(None, "lat", "lon"),
        P(),
        P(),
        P(),
        P(),
        P(),
        P(),
        P(),
        P(None, "lat", "section", None, None),
        P("section", "lat", "lon", None),
    )
    return jax.shard_map(
        on_device,
        mesh=mesh,
        in_specs=placed,
        out_specs=(P("section", "lat", "lon", None), P(), P()),
        check_vma=False,
    )
```

```python
import functools
import itertools

import jax
import jax.numpy as jnp
import numpy as np
from jax import lax
from jax.experimental import pallas as pl
from jax.experimental.pallas import tpu as pltpu
from jax.sharding import PartitionSpec as P

MESH = pl.DeviceIdType.MESH
f32 = jnp.float32
bf16 = jnp.bfloat16
norm_eps = 1e-05
HEADS = 6
BATCH = 3
TOKENS = 144
WIDTH = 192
FIELD_ROWS = 640
NN = (((1,), (0,)), ((), ()))
NT = (((1,), (1,)), ((), ()))
TN = (((0,), (0,)), ((), ()))


def dot(a, b, dims=NN):
    return lax.dot_general(a, b, dims, preferred_element_type=f32)


def tables():
    t = np.arange(TOKENS)
    col, level, row = t // 12, t // 6 % 2, t % 6
    octant = (col // 6) * 4 + level * 2 + row // 3
    inner = (col % 6) * 3 + row % 3
    natural = (row * 12 + col) * 2 + level

    def packing(order):
        pack = np.zeros((256, 3, TOKENS))
        pack[octant * 32 + inner, 0, order] = 1
        first = inner < 9
        pack[(octant * 32 + 18 + inner)[first], 1, order[first]] = 1
        pack[(octant * 32 + 9 + inner)[~first], 2, order[~first]] = 1
        return pack.reshape(256, 3 * TOKENS)

    pack_tok = packing(t)
    tok_to_nat = np.zeros((TOKENS, TOKENS))
    tok_to_nat[natural, t] = 1
    pick = np.zeros((4, TOKENS, 48))
    for c in range(4):
        pick[c, t, 4 * col + c] = 1
    key_row = np.full((2, 1, FIELD_ROWS), -1.0)
    fold_upper = np.zeros((4, 256, 160))
    fold_surface = np.zeros((4, 128, 64))
    for v in range(5):
        for a in range(2):
            for y in range(24):
                r = (v * 2 + a) * 24 + y
                key_row[1, 0, r] = y // 4
                key_row[:, 0, 256 + r] = 8 + y // 4
                for c in range(4):
                    fold_upper[c, r, v * 32 + a * 16 + (y % 4) * 4 + c] = 1
    for v in range(4):
        for y in range(24):
            r = v * 24 + y
            key_row[0, 0, 512 + r] = y // 4
            for c in range(4):
                fold_surface[c, r, v * 16 + (y % 4) * 4 + c] = 1
    key_tok = (level * 8 + row).reshape(TOKENS, 1)
    spread = np.zeros((2, 138, 276))
    for z in range(2):
        for a in range(6):
            for k in range(23):
                spread[z, a * 23 + k, (22 - k) * 12 + z * 6 + a] = 1
    heads = np.zeros((HEADS, 1, WIDTH))
    for h in range(HEADS):
        heads[h, 0, 32 * h : 32 * h + 32] = 1
    place_col = np.stack((level, row // 3)).reshape(2, TOKENS, 1)
    place_row = np.stack((level, row // 3)).reshape(2, 1, TOKENS)
    return {
        "pack_tok": pack_tok.astype(jnp.bfloat16),
        "unpack_tok": pack_tok.T.astype(jnp.bfloat16),
        "pack_nat": packing(natural).astype(jnp.bfloat16),
        "tok_to_nat": tok_to_nat.astype(jnp.bfloat16),
        "pick": pick.astype(jnp.bfloat16),
        "key_row": key_row.astype(np.float32),
        "key_tok": key_tok.astype(np.float32),
        "fold_upper": fold_upper.astype(jnp.bfloat16),
        "fold_surface": fold_surface.astype(jnp.bfloat16),
        "spread": spread.astype(jnp.bfloat16),
        "heads": heads.astype(np.float32),
        "place_col": place_col.astype(np.float32),
        "place_row": place_row.astype(np.float32),
    }


def centre(values):
    average = jnp.mean(values, -1, keepdims=True)
    centred = values - average
    variance = jnp.mean(centred * centred, -1, keepdims=True)
    scale = lax.rsqrt(variance + norm_eps)
    return centred * scale, scale


def norm_backward(unit, scale, gain, cotangent):
    scaled = cotangent * gain
    first = jnp.mean(scaled, -1, keepdims=True)
    second = jnp.mean(scaled * unit, -1, keepdims=True)
    return scale * (scaled - first - unit * second)


def build_bias(table_ref, b, spread_ref, tab, strip, bias):
    for z in range(2):
        for zt in range(2):
            for a in range(6):
                start = ((zt * 2 + z) * 6 + a) * 138
                tab[z, (zt * 6 + a) * 8 : (zt * 6 + a) * 8 + 6, :] = table_ref[6 * b : 6 * b + 6, 0, start : start + 138]
    total = None
    for z in range(2):
        rest = tab[z]
        for part in range(3):
            piece = rest.astype(bf16)
            rest = rest - piece.astype(f32)
            term = dot(piece, spread_ref[z])
            total = term if total is None else total + term
    strip[...] = total
    for h in range(HEADS):
        lines = jnp.concatenate([strip[8 * k + h : 8 * k + h + 1, :] for k in range(12)], 0)
        for o in range(12):
            bias[h * TOKENS + 12 * o : h * TOKENS + 12 * o + 12, :] = lines[:, 12 * (11 - o) : 12 * (11 - o) + TOKENS]


def by_head(values, w, first):
    return jnp.concatenate([values * w["heads"][h].astype(bf16) for h in range(first, first + BATCH)], 0)


def own_heads(stacked, w, first, total):
    for k in range(BATCH):
        part = stacked[k * TOKENS : (k + 1) * TOKENS] * w["heads"][first + k]
        total = part if total is None else total + part
    return total


def block_forward(x, b, w, bias, saved, final):
    unit0, scale0 = centre(x)
    hidden = (unit0 * w["gains"][b, 0:1, :]).astype(bf16)
    qkv = dot(hidden, w["qkv"][b]).astype(bf16)
    saved["qkv"][b] = qkv
    query = qkv[:, :WIDTH]
    key = qkv[:, WIDTH : 2 * WIDTH]
    value = qkv[:, 2 * WIDTH :]
    mixed = None
    for g in range(0, HEADS, BATCH):
        rows = slice(g * TOKENS, (g + BATCH) * TOKENS)
        score = dot(by_head(query, w, g), key, NT) * 32 ** (-0.5) + bias[rows]
        expo = jnp.exp(score - jnp.max(score, -1, keepdims=True))
        prob = expo * (1.0 / jnp.sum(expo, -1, keepdims=True))
        saved["prob"][b, rows] = prob
        mixed = own_heads(dot(prob.astype(bf16), value), w, g, mixed)
    resid = x + dot(mixed.astype(bf16), w["proj"][b])
    unit1, scale1 = centre(resid)
    normed = (unit1 * w["gains"][b, 1:2, :]).astype(bf16)
    upward = dot(normed, w["up"][b])
    saved["unit0"][b] = unit0
    saved["scale0"][b] = scale0
    saved["unit1"][b] = unit1
    saved["scale1"][b] = scale1
    saved["upward"][b] = upward
    if final:
        return None
    active = 0.5 * upward * (1.0 + lax.erf(upward * 2 ** (-0.5)))
    return resid + dot(active.astype(bf16), w["down"][b], NT)


def gelu_slope(b, saved):
    upward = saved["upward"][b]
    slope = 0.5 * (1.0 + lax.erf(upward * 2 ** (-0.5)))
    saved["slope"][...] = slope + upward * jnp.exp(-0.5 * upward * upward) * (2 * np.pi) ** (-0.5)


def block_backward(dout, b, w, saved):
    dactive = dot(dout.astype(bf16), w["down"][b]).astype(bf16).astype(f32)
    dupward = dactive * saved["slope"][...]
    dnormed = dot(dupward.astype(bf16), w["up"][b], NT).astype(bf16).astype(f32)
    dresid = dout + norm_backward(saved["unit1"][b], saved["scale1"][b], w["gains"][b, 1:2, :], dnormed)
    dmixed = dot(dresid.astype(bf16), w["proj"][b], NT).astype(bf16)
    qkv = saved["qkv"][b]
    query = qkv[:, :WIDTH]
    key = qkv[:, WIDTH : 2 * WIDTH]
    value = qkv[:, 2 * WIDTH :]
    dquery = dkey = dvalue = None
    for g in range(0, HEADS, BATCH):
        rows = slice(g * TOKENS, (g + BATCH) * TOKENS)
        prob = saved["prob"][b, rows]
        dmixed_g = by_head(dmixed, w, g)
        dweights = dot(dmixed_g, value, NT).astype(bf16).astype(f32)
        dv = dot(prob.astype(bf16), dmixed_g, TN)
        inner = jnp.sum(dweights * prob, -1, keepdims=True)
        dscore = (prob * (dweights - inner)).astype(bf16)
        dquery = own_heads(dot(dscore, key), w, g, dquery)
        dk = dot(dscore, by_head(query, w, g), TN)
        dkey = dk if dkey is None else dkey + dk
        dvalue = dv if dvalue is None else dvalue + dv
    dquery = dquery * 32 ** (-0.5)
    dkey = dkey * 32 ** (-0.5)
    dqkv = jnp.concatenate((dquery, dkey, dvalue), 1).astype(bf16)
    dhidden = dot(dqkv, w["qkv"][b], NT).astype(bf16).astype(f32)
    return dresid + norm_backward(saved["unit0"][b], saved["scale0"][b], w["gains"][b, 0:1, :], dhidden)


def pack_octants(pack, tokens):
    low, high = tokens[:, :128], tokens[:, 128:]
    empty = jnp.zeros_like(high)
    parts = (low, jnp.concatenate((high, empty), 1), jnp.concatenate((empty, high), 1))
    rows = jnp.concatenate([part.astype(bf16) for part in parts], 0)
    return dot(pack, rows).astype(bf16).reshape(8, 32, 128)


def unpack_octants(unpack, octants):
    parts = dot(unpack, octants.reshape(256, 128))
    low = parts[:TOKENS]
    left = parts[TOKENS : 2 * TOKENS]
    right = parts[2 * TOKENS :]
    return jnp.concatenate((low, left[:, :64] + right[:, 64:]), 1)


def wait_bytes(buffer, start, count, sem):
    view = buffer.at[pl.ds(start, count)]
    pltpu.make_async_copy(view, view, sem).wait()


class Routes:
    def __init__(self):
        self.lon, self.lat, self.section = (lax.axis_index(n) for n in ("lon", "lat", "section"))
        self.lons, self.lats, self.sections = (lax.axis_size(n) for n in ("lon", "lat", "section"))
        self.inner = min(8, self.lons)
        self.outer = self.lons // self.inner
        self.pair_in, self.pair_out = min(2, self.inner), min(2, self.outer)
        self.high = self.lon // self.inner
        self.low = lax.rem(self.lon, self.inner)
        hops = lambda d, n: min(d, n - d)
        near = itertools.product(range(self.pair_out), range(self.pair_in), range(self.lats))
        self.near_steps = sorted(
            (d for d in near if any(d)), key=lambda d: -(d[0] + d[1] + hops(d[2], self.lats) / 2)
        )
        far = itertools.product(
            range(self.sections), range(self.outer // self.pair_out), range(self.inner // self.pair_in)
        )
        self.far_steps = sorted(
            (d for d in far if any(d)),
            key=lambda d: -((4 - 2 * d[1] if d[0] else 2 * d[1]) + 2 * hops(d[2], self.inner // self.pair_in)),
        )

    def near_index(self, step=(0, 0, 0)):
        out = lax.rem(self.high + step[0], self.pair_out)
        into = lax.rem(self.low + step[1], self.pair_in)
        return (out * self.pair_in + into) * self.lats + lax.rem(self.lat + step[2], self.lats)

    def near_peer(self, step):
        target = {}
        if step[0] or step[1]:
            out = self.high // self.pair_out * self.pair_out + lax.rem(self.high + step[0], self.pair_out)
            into = self.low // self.pair_in * self.pair_in + lax.rem(self.low + step[1], self.pair_in)
            target["lon"] = out * self.inner + into
        if step[2]:
            target["lat"] = lax.rem(self.lat + step[2], self.lats)
        return target

    def far_index(self):
        index = self.section * (self.outer // self.pair_out) + self.high // self.pair_out
        return index * (self.inner // self.pair_in) + self.low // self.pair_in

    def far_peer(self, step):
        target = {}
        if step[0]:
            target["section"] = lax.rem(self.section + step[0], self.sections)
        if step[1] or step[2]:
            out = lax.rem(self.high + step[1] * self.pair_out, self.outer)
            target["lon"] = out * self.inner + lax.rem(self.low + step[2] * self.pair_in, self.inner)
        return target

    def corner(self, step, sign):
        target = {}
        if step[0]:
            target["lon"] = lax.rem(self.lon + sign + self.lons, self.lons)
        if step[1]:
            target["section"] = 1 - self.section
        if step[2]:
            target["lat"] = lax.rem(self.lat + sign + self.lats, self.lats)
        return target


def send_octants(routes, src, dst, send_sem, recv_sem, forward):
    for far in (7, 3, 6, 2, 5, 1, 4):
        step = (far >> 2, far >> 1 & 1, far & 1)
        k = 7 - far if forward else far
        pltpu.make_async_remote_copy(
            src_ref=src.at[k],
            dst_ref=dst.at[7 - k],
            send_sem=send_sem,
            recv_sem=recv_sem,
            device_id=routes.corner(step, -1 if forward else 1),
            device_id_type=MESH,
        ).start()
    stay = 7 if forward else 0
    dst[7 - stay] = src[stay]


class Loads:
    def __init__(self, names, sources, targets, sems):
        self.targets = dict(zip(names, targets))
        self.copies = {}
        for i, name in enumerate(names):
            copy = pltpu.make_async_copy(sources[i], targets[i], sems.at[i])
            copy.start()
            self.copies[name] = copy

    def __getitem__(self, name):
        copy = self.copies.pop(name, None)
        if copy is not None:
            copy.wait()
        return self.targets[name]


def whole_kernel(names, owners, unit, *refs):
    count = len(names)
    consts = Loads(names, refs[:count], refs[-count - 1 : -1], refs[-1])
    (
        latent_out,
        upper_out,
        surface_out,
        field,
        tab,
        strip,
        bias0,
        bias1,
        qkv_s,
        prob_s,
        unit0_s,
        scale0_s,
        unit1_s,
        scale1_s,
        upward_s,
        slope_s,
        patch_upper,
        patch_surface,
        grad_send,
        grad_recv,
        x_send,
        x_recv,
        back_send,
        back_recv,
        terms,
        held,
        piece,
        across,
        last,
        result,
        sems,
    ) = refs[count : -count - 1]
    routes = Routes()
    lon, lat, section = routes.lon, routes.lat, routes.section
    lon_count, lat_count, section_count = routes.lons, routes.lats, routes.sections
    count_near, count_far = len(routes.near_steps), len(routes.far_steps)
    owner, mine = routes.near_index(), routes.far_index()
    barrier = pltpu.get_barrier_semaphore()
    corners = sorted(itertools.product(range(2), repeat=3), reverse=True)
    targets = [routes.corner(d, sign) for d in corners[:-1] for sign in (-1, 1) if d != (0, 1, 0) or sign > 0]
    targets += [routes.far_peer(step) for step in routes.far_steps]
    targets += [routes.near_peer(step) for step in routes.near_steps]
    for target in targets:
        pl.semaphore_signal(barrier, inc=1, device_id=target, device_id_type=MESH)

    field[240:256, :] = jnp.zeros((16, 48), f32)
    field[496:512, :] = jnp.zeros((16, 48), f32)
    field[608:640, :] = jnp.zeros((32, 48), f32)
    for v in range(5):
        for a in range(2):
            row = (v * 2 + a) * 24
            field[row : row + 24, :] = consts["upper"][v, 2 + a].astype(f32)
            field[256 + row : 256 + row + 24, :] = consts["upper"][v, 4 * section + a].astype(f32)
    for v in range(4):
        field[512 + 24 * v : 512 + 24 * v + 24, :] = consts["surface"][v].astype(f32)
    fields = field[...].astype(bf16)
    same = consts["key_tok"][...] == consts["key_row"][section]
    upper_total = surface_total = None
    for c in range(4):
        spreads = jnp.where(same, dot(consts["pick"][c], fields, NT), 0.0)
        upper_c = (spreads[:, :256] + spreads[:, 256:512]).astype(bf16)
        surface_c = spreads[:, 512:].astype(bf16)
        upper_c = dot(upper_c, consts["fold_upper"][c])
        surface_c = dot(surface_c, consts["fold_surface"][c])
        upper_total = upper_c if upper_total is None else upper_total + upper_c
        surface_total = surface_c if surface_total is None else surface_total + surface_c
    patch_upper[...] = upper_total.astype(bf16)
    patch_surface[...] = surface_total.astype(bf16)
    latent = dot(patch_upper[...], consts["upper_embed"][...])
    latent = latent + dot(patch_surface[...], consts["surface_embed"][...])
    latent = latent.astype(bf16).astype(f32)
    build_bias(consts["table"], 0, consts["spread"], tab, strip, bias0)

    w = consts
    saved = {
        "qkv": qkv_s,
        "prob": prob_s,
        "unit0": unit0_s,
        "scale0": scale0_s,
        "unit1": unit1_s,
        "scale1": scale1_s,
        "upward": upward_s,
        "slope": slope_s,
    }
    first = block_forward(latent, 0, w, bias0, saved, False)
    x_send[...] = pack_octants(consts["pack_tok"][...], first)
    pl.semaphore_wait(barrier, len(targets))
    send_octants(routes, x_send, x_recv, sems.at[2], sems.at[3], True)

    out_grad = consts["grad"][...].astype(f32).reshape(TOKENS, WIDTH)
    grad_send[...] = pack_octants(consts["pack_nat"][...], out_grad)
    send_octants(routes, grad_send, grad_recv, sems.at[0], sems.at[1], True)
    build_bias(consts["table"], 1, consts["spread"], tab, strip, bias1)
    last_section = (section == section_count - 1).astype(f32)
    last_band = (lat == lat_count - 1).astype(f32)
    apart = jnp.abs(consts["place_col"][0] - consts["place_row"][0]) * last_section
    apart = apart + jnp.abs(consts["place_col"][1] - consts["place_row"][1]) * last_band
    for h in range(HEADS):
        rows = slice(h * TOKENS, (h + 1) * TOKENS)
        bias1[rows] = jnp.where(apart > 0.5, -1e30, bias1[rows])
    wait_bytes(x_recv, 1, 7, sems.at[3])
    shifted = unpack_octants(consts["unpack_tok"][...], x_recv[...])
    block_forward(shifted, 1, w, bias1, saved, True)
    gelu_slope(1, saved)
    wait_bytes(grad_recv, 1, 7, sems.at[1])
    dshifted = unpack_octants(consts["unpack_tok"][...], grad_recv[...])
    dmiddle = block_backward(dshifted, 1, w, saved)
    back_send[...] = pack_octants(consts["pack_tok"][...], dmiddle)
    send_octants(routes, back_send, back_recv, sems.at[4], sems.at[5], False)
    gelu_slope(0, saved)
    wait_bytes(back_recv, 0, 7, sems.at[5])
    dfirst = unpack_octants(consts["unpack_tok"][...], back_recv[...])
    dlatent = block_backward(dfirst, 0, w, saved).astype(bf16)

    upper_terms = dot(patch_upper[...], dlatent, TN)
    surface_terms = dot(patch_surface[...], dlatent, TN)
    both = jnp.concatenate((upper_terms, surface_terms), 0)
    terms[0:14, :, :] = both[:, :128].astype(bf16).reshape(14, 16, 128)
    low = both[:, 128:]
    low = jnp.concatenate((low[:112], low[112:]), 1)
    terms[14:21, :, :] = low.astype(bf16).reshape(7, 16, 128)

    for k, step in enumerate(routes.near_steps):
        peer = routes.near_index(step)

        @pl.when(peer < owners)
        def _():
            pltpu.make_async_remote_copy(
                src_ref=terms.at[pl.ds(peer * unit, unit)],
                dst_ref=held.at[pl.ds(k * unit, unit)],
                send_sem=sems.at[6],
                recv_sem=sems.at[7],
                device_id=routes.near_peer(step),
                device_id_type=MESH,
            ).start()

    latent_out[...] = dot(consts["tok_to_nat"][...], dlatent).reshape(6, 12, 2, WIDTH).astype(bf16)

    @pl.when(owner < owners)
    def _():
        wait_bytes(held, 0, count_near * unit, sems.at[7])
        total = terms[pl.ds(owner * unit, unit)].astype(f32)
        for d in range(count_near):
            total = total + held[d * unit : d * unit + unit].astype(f32)
        piece[...] = total.astype(bf16)
        across[pl.ds(mine * unit, unit)] = total.astype(bf16)
        for step in routes.far_steps:
            pltpu.make_async_remote_copy(
                src_ref=piece,
                dst_ref=across.at[pl.ds(mine * unit, unit)],
                send_sem=sems.at[8],
                recv_sem=sems.at[9],
                device_id=routes.far_peer(step),
                device_id_type=MESH,
            ).start()

        wait_bytes(across, 0, count_far * unit, sems.at[9])
        whole = across[0:unit].astype(f32)
        for d in range(1, count_far + 1):
            whole = whole + across[d * unit : d * unit + unit].astype(f32)
        last[...] = whole.astype(bf16)
        result[pl.ds(owner * unit, unit)] = whole.astype(bf16)
        for step in routes.near_steps:
            pltpu.make_async_remote_copy(
                src_ref=last,
                dst_ref=result.at[pl.ds(owner * unit, unit)],
                send_sem=sems.at[10],
                recv_sem=sems.at[11],
                device_id=routes.near_peer(step),
                device_id_type=MESH,
            ).start()

        wait_bytes(terms, 0, (owners - 1) * unit, sems.at[6])
        wait_bytes(across, 0, count_far * unit, sems.at[8])
        wait_bytes(result, 0, (owners - 1) * unit, sems.at[11])
        wait_bytes(held, 0, count_near * unit, sems.at[10])

    @pl.when(owner >= owners)
    def _():
        wait_bytes(terms, 0, owners * unit, sems.at[6])
        wait_bytes(result, 0, owners * unit, sems.at[11])

    scale = float(4 * 6 * lat_count * 12 * lon_count) ** (-0.5)
    high = result[0:14].astype(f32).reshape(224, 128) * scale
    low = result[14:21].astype(f32).reshape(112, 128) * scale
    upper_out[:, 0:128] = high[:160]
    surface_out[:, 0:128] = high[160:]
    upper_out[0:112, 128:192] = low[:, :64]
    upper_out[112:160, 128:192] = low[:48, 64:]
    surface_out[:, 128:192] = low[48:, 64:]
    wait_bytes(grad_send, 0, 7, sems.at[0])
    wait_bytes(x_send, 0, 7, sems.at[2])
    wait_bytes(back_send, 0, 7, sems.at[4])


def on_device(
    upper_fields,
    surface_fields,
    upper_embed,
    surface_embed,
    norm_gains,
    qkv_weight,
    proj_weight,
    up_weight,
    down_weight,
    earth_bias,
    out_grad,
):
    consts = tables()
    operands = {
        "upper": upper_fields,
        "surface": surface_fields,
        "pick": consts["pick"],
        "key_tok": consts["key_tok"],
        "key_row": consts["key_row"],
        "fold_upper": consts["fold_upper"],
        "fold_surface": consts["fold_surface"],
        "upper_embed": upper_embed,
        "surface_embed": surface_embed,
        "table": earth_bias.reshape(2 * HEADS, 1, -1),
        "spread": consts["spread"],
        "grad": out_grad.transpose(1, 2, 0, 3),
        "gains": norm_gains,
        "qkv": qkv_weight,
        "heads": consts["heads"],
        "proj": proj_weight,
        "up": up_weight,
        "down": down_weight.swapaxes(1, 2),
        "pack_tok": consts["pack_tok"],
        "pack_nat": consts["pack_nat"],
        "unpack_tok": consts["unpack_tok"],
        "tok_to_nat": consts["tok_to_nat"],
        "place_col": consts["place_col"],
        "place_row": consts["place_row"],
    }
    names = tuple(operands)
    lon_count = lax.axis_size("lon")
    near = min(4, lon_count) * lax.axis_size("lat")
    if lon_count < 16:
        near = min(2, lon_count) * lax.axis_size("lat")
    group = lon_count * lax.axis_size("lat") * lax.axis_size("section") // near
    unit = -(-21 // near)
    owners = -(-21 // unit)
    hbm = pl.BlockSpec(memory_space=pltpu.HBM)
    latent_grad, upper_grad, surface_grad = pl.pallas_call(
        functools.partial(whole_kernel, names, owners, unit),
        out_shape=(
            jax.ShapeDtypeStruct((6, 12, 2, WIDTH), bf16),
            jax.ShapeDtypeStruct((160, WIDTH), f32),
            jax.ShapeDtypeStruct((64, WIDTH), f32),
        ),
        in_specs=[hbm] * len(names),
        out_specs=(pl.BlockSpec(memory_space=pltpu.VMEM),) * 3,
        scratch_shapes=[
            pltpu.VMEM((FIELD_ROWS, 48), f32),
            pltpu.VMEM((2, 96, 138), f32),
            pltpu.VMEM((96, 276), f32),
            pltpu.VMEM((HEADS * TOKENS, TOKENS), f32),
            pltpu.VMEM((HEADS * TOKENS, TOKENS), f32),
            pltpu.VMEM((2, TOKENS, 3 * WIDTH), bf16),
            pltpu.VMEM((2, HEADS * TOKENS, TOKENS), f32),
            pltpu.VMEM((2, TOKENS, WIDTH), f32),
            pltpu.VMEM((2, TOKENS, 1), f32),
            pltpu.VMEM((2, TOKENS, WIDTH), f32),
            pltpu.VMEM((2, TOKENS, 1), f32),
            pltpu.VMEM((2, TOKENS, 768), f32),
            pltpu.VMEM((TOKENS, 768), f32),
            pltpu.VMEM((TOKENS, 160), bf16),
            pltpu.VMEM((TOKENS, 64), bf16),
            pltpu.VMEM((8, 32, 128), bf16),
            pltpu.VMEM((8, 32, 128), bf16),
            pltpu.VMEM((8, 32, 128), bf16),
            pltpu.VMEM((8, 32, 128), bf16),
            pltpu.VMEM((8, 32, 128), bf16),
            pltpu.VMEM((8, 32, 128), bf16),
            pltpu.VMEM((owners * unit, 16, 128), bf16),
            pltpu.VMEM(((near - 1) * unit, 16, 128), bf16),
            pltpu.VMEM((unit, 16, 128), bf16),
            pltpu.VMEM((group * unit, 16, 128), bf16),
            pltpu.VMEM((unit, 16, 128), bf16),
            pltpu.VMEM((owners * unit, 16, 128), bf16),
            pltpu.SemaphoreType.DMA((12,)),
            *(pltpu.VMEM(a.shape, a.dtype) for a in operands.values()),
            pltpu.SemaphoreType.DMA((len(names),)),
        ],
        compiler_params=pltpu.CompilerParams(
            collective_id=0, has_side_effects=True, vmem_limit_bytes=40 * 2**20
        ),
    )(*(pltpu.with_memory_space_constraint(a, pltpu.HBM) for a in operands.values()))
    return latent_grad.transpose(2, 0, 1, 3), upper_grad, surface_grad


def solution(mesh):
    placed = (
        P(None, None, "lat", "lon"),
        P(None, "lat", "lon"),
        P(),
        P(),
        P(),
        P(),
        P(),
        P(),
        P(),
        P(None, "lat", "section", None, None),
        P("section", "lat", "lon", None),
    )
    return jax.shard_map(
        on_device,
        mesh=mesh,
        in_specs=placed,
        out_specs=(P("section", "lat", "lon", None), P(), P()),
        check_vma=False,
    )
```

```python
import functools
import itertools

import jax
import jax.numpy as jnp
import numpy as np
from jax import lax
from jax.experimental import pallas as pl
from jax.experimental.pallas import tpu as pltpu
from jax.sharding import PartitionSpec as P

MESH = pl.DeviceIdType.MESH
f32 = jnp.float32
bf16 = jnp.bfloat16
norm_eps = 1e-05
HEADS = 6
BATCH = 3
TOKENS = 144
WIDTH = 192
FIELD_ROWS = 640
NN = (((1,), (0,)), ((), ()))
NT = (((1,), (1,)), ((), ()))
TN = (((0,), (0,)), ((), ()))


def dot(a, b, dims=NN):
    return lax.dot_general(a, b, dims, preferred_element_type=f32)


def tables():
    t = np.arange(TOKENS)
    col, level, row = t // 12, t // 6 % 2, t % 6
    octant = (col // 6) * 4 + level * 2 + row // 3
    inner = (col % 6) * 3 + row % 3
    natural = (row * 12 + col) * 2 + level

    def packing(order):
        pack = np.zeros((256, 3, TOKENS))
        pack[octant * 32 + inner, 0, order] = 1
        first = inner < 9
        pack[(octant * 32 + 18 + inner)[first], 1, order[first]] = 1
        pack[(octant * 32 + 9 + inner)[~first], 2, order[~first]] = 1
        return pack.reshape(256, 3 * TOKENS)

    pack_tok = packing(t)
    tok_to_nat = np.zeros((TOKENS, TOKENS))
    tok_to_nat[natural, t] = 1
    pick = np.zeros((4, TOKENS, 48))
    for c in range(4):
        pick[c, t, 4 * col + c] = 1
    key_row = np.full((2, 1, FIELD_ROWS), -1.0)
    fold_upper = np.zeros((4, 256, 160))
    fold_surface = np.zeros((4, 128, 64))
    for v in range(5):
        for a in range(2):
            for y in range(24):
                r = (v * 2 + a) * 24 + y
                key_row[1, 0, r] = y // 4
                key_row[:, 0, 256 + r] = 8 + y // 4
                for c in range(4):
                    fold_upper[c, r, v * 32 + a * 16 + (y % 4) * 4 + c] = 1
    for v in range(4):
        for y in range(24):
            r = v * 24 + y
            key_row[0, 0, 512 + r] = y // 4
            for c in range(4):
                fold_surface[c, r, v * 16 + (y % 4) * 4 + c] = 1
    key_tok = (level * 8 + row).reshape(TOKENS, 1)
    spread = np.zeros((2, 138, 276))
    for z in range(2):
        for a in range(6):
            for k in range(23):
                spread[z, a * 23 + k, (22 - k) * 12 + z * 6 + a] = 1
    heads = np.zeros((HEADS, 1, WIDTH))
    for h in range(HEADS):
        heads[h, 0, 32 * h : 32 * h + 32] = 1
    place_col = np.stack((level, row // 3)).reshape(2, TOKENS, 1)
    place_row = np.stack((level, row // 3)).reshape(2, 1, TOKENS)
    return {
        "pack_tok": pack_tok.astype(jnp.bfloat16),
        "unpack_tok": pack_tok.T.astype(jnp.bfloat16),
        "pack_nat": packing(natural).astype(jnp.bfloat16),
        "tok_to_nat": tok_to_nat.astype(jnp.bfloat16),
        "pick": pick.astype(jnp.bfloat16),
        "key_row": key_row.astype(np.float32),
        "key_tok": key_tok.astype(np.float32),
        "fold_upper": fold_upper.astype(jnp.bfloat16),
        "fold_surface": fold_surface.astype(jnp.bfloat16),
        "spread": spread.astype(jnp.bfloat16),
        "heads": heads.astype(np.float32),
        "place_col": place_col.astype(np.float32),
        "place_row": place_row.astype(np.float32),
    }


def centre(values):
    average = jnp.mean(values, -1, keepdims=True)
    centred = values - average
    variance = jnp.mean(centred * centred, -1, keepdims=True)
    scale = lax.rsqrt(variance + norm_eps)
    return centred * scale, scale


def norm_backward(unit, scale, gain, cotangent):
    scaled = cotangent * gain
    first = jnp.mean(scaled, -1, keepdims=True)
    second = jnp.mean(scaled * unit, -1, keepdims=True)
    return scale * (scaled - first - unit * second)


def build_bias(table_ref, b, spread_ref, tab, strip, bias):
    for z in range(2):
        for zt in range(2):
            for a in range(6):
                start = ((zt * 2 + z) * 6 + a) * 138
                tab[z, (zt * 6 + a) * 8 : (zt * 6 + a) * 8 + 6, :] = table_ref[6 * b : 6 * b + 6, 0, start : start + 138]
    total = None
    for z in range(2):
        rest = tab[z]
        for part in range(3):
            piece = rest.astype(bf16)
            rest = rest - piece.astype(f32)
            term = dot(piece, spread_ref[z])
            total = term if total is None else total + term
    strip[...] = total
    for h in range(HEADS):
        lines = jnp.concatenate([strip[8 * k + h : 8 * k + h + 1, :] for k in range(12)], 0)
        for o in range(12):
            bias[h * TOKENS + 12 * o : h * TOKENS + 12 * o + 12, :] = lines[:, 12 * (11 - o) : 12 * (11 - o) + TOKENS]


def by_head(values, w, first):
    return jnp.concatenate([values * w["heads"][h].astype(bf16) for h in range(first, first + BATCH)], 0)


def own_heads(stacked, w, first, total):
    for k in range(BATCH):
        part = stacked[k * TOKENS : (k + 1) * TOKENS] * w["heads"][first + k]
        total = part if total is None else total + part
    return total


def block_forward(x, b, w, bias, saved, final):
    unit0, scale0 = centre(x)
    hidden = (unit0 * w["gains"][b, 0:1, :]).astype(bf16)
    qkv = dot(hidden, w["qkv"][b]).astype(bf16)
    saved["qkv"][b] = qkv
    query = qkv[:, :WIDTH]
    key = qkv[:, WIDTH : 2 * WIDTH]
    value = qkv[:, 2 * WIDTH :]
    mixed = None
    for g in range(0, HEADS, BATCH):
        rows = slice(g * TOKENS, (g + BATCH) * TOKENS)
        score = dot(by_head(query, w, g), key, NT) * 32 ** (-0.5) + bias[rows]
        expo = jnp.exp(score - jnp.max(score, -1, keepdims=True))
        prob = expo * (1.0 / jnp.sum(expo, -1, keepdims=True))
        saved["prob"][b, rows] = prob
        mixed = own_heads(dot(prob.astype(bf16), value), w, g, mixed)
    resid = x + dot(mixed.astype(bf16), w["proj"][b])
    unit1, scale1 = centre(resid)
    normed = (unit1 * w["gains"][b, 1:2, :]).astype(bf16)
    upward = dot(normed, w["up"][b])
    saved["unit0"][b] = unit0
    saved["scale0"][b] = scale0
    saved["unit1"][b] = unit1
    saved["scale1"][b] = scale1
    saved["upward"][b] = upward
    if final:
        return None
    active = 0.5 * upward * (1.0 + lax.erf(upward * 2 ** (-0.5)))
    return resid + dot(active.astype(bf16), w["down"][b], NT)


def gelu_slope(b, saved):
    upward = saved["upward"][b]
    slope = 0.5 * (1.0 + lax.erf(upward * 2 ** (-0.5)))
    saved["slope"][...] = slope + upward * jnp.exp(-0.5 * upward * upward) * (2 * np.pi) ** (-0.5)


def block_backward(dout, b, w, saved):
    dactive = dot(dout.astype(bf16), w["down"][b]).astype(bf16).astype(f32)
    dupward = dactive * saved["slope"][...]
    dnormed = dot(dupward.astype(bf16), w["up"][b], NT).astype(bf16).astype(f32)
    dresid = dout + norm_backward(saved["unit1"][b], saved["scale1"][b], w["gains"][b, 1:2, :], dnormed)
    dmixed = dot(dresid.astype(bf16), w["proj"][b], NT).astype(bf16)
    qkv = saved["qkv"][b]
    query = qkv[:, :WIDTH]
    key = qkv[:, WIDTH : 2 * WIDTH]
    value = qkv[:, 2 * WIDTH :]
    dquery = dkey = dvalue = None
    for g in range(0, HEADS, BATCH):
        rows = slice(g * TOKENS, (g + BATCH) * TOKENS)
        prob = saved["prob"][b, rows]
        dmixed_g = by_head(dmixed, w, g)
        dweights = dot(dmixed_g, value, NT).astype(bf16).astype(f32)
        dv = dot(prob.astype(bf16), dmixed_g, TN)
        inner = jnp.sum(dweights * prob, -1, keepdims=True)
        dscore = (prob * (dweights - inner)).astype(bf16)
        dquery = own_heads(dot(dscore, key), w, g, dquery)
        dk = dot(dscore, by_head(query, w, g), TN)
        dkey = dk if dkey is None else dkey + dk
        dvalue = dv if dvalue is None else dvalue + dv
    dquery = dquery * 32 ** (-0.5)
    dkey = dkey * 32 ** (-0.5)
    dqkv = jnp.concatenate((dquery, dkey, dvalue), 1).astype(bf16)
    dhidden = dot(dqkv, w["qkv"][b], NT).astype(bf16).astype(f32)
    return dresid + norm_backward(saved["unit0"][b], saved["scale0"][b], w["gains"][b, 0:1, :], dhidden)


def pack_octants(pack, tokens):
    low, high = tokens[:, :128], tokens[:, 128:]
    empty = jnp.zeros_like(high)
    parts = (low, jnp.concatenate((high, empty), 1), jnp.concatenate((empty, high), 1))
    rows = jnp.concatenate([part.astype(bf16) for part in parts], 0)
    return dot(pack, rows).astype(bf16).reshape(8, 32, 128)


def unpack_octants(unpack, octants):
    parts = dot(unpack, octants.reshape(256, 128))
    low = parts[:TOKENS]
    left = parts[TOKENS : 2 * TOKENS]
    right = parts[2 * TOKENS :]
    return jnp.concatenate((low, left[:, :64] + right[:, 64:]), 1)


def wait_bytes(buffer, start, count, sem):
    view = buffer.at[pl.ds(start, count)]
    pltpu.make_async_copy(view, view, sem).wait()


class Routes:
    def __init__(self):
        self.lon, self.lat, self.section = (lax.axis_index(n) for n in ("lon", "lat", "section"))
        self.lons, self.lats, self.sections = (lax.axis_size(n) for n in ("lon", "lat", "section"))
        self.inner = min(8, self.lons)
        self.outer = self.lons // self.inner
        self.pair_in, self.pair_out = min(2, self.inner), min(2, self.outer)
        self.high = self.lon // self.inner
        self.low = lax.rem(self.lon, self.inner)
        hops = lambda d, n: min(d, n - d)
        near = itertools.product(range(self.pair_out), range(self.pair_in), range(self.lats))
        self.near_steps = sorted(
            (d for d in near if any(d)), key=lambda d: -(d[0] + d[1] + hops(d[2], self.lats) / 2)
        )
        far = itertools.product(
            range(self.sections), range(self.outer // self.pair_out), range(self.inner // self.pair_in)
        )
        self.far_steps = sorted(
            (d for d in far if any(d)),
            key=lambda d: -((4 - 2 * d[1] if d[0] else 2 * d[1]) + 2 * hops(d[2], self.inner // self.pair_in)),
        )

    def near_index(self, step=(0, 0, 0)):
        out = lax.rem(self.high + step[0], self.pair_out)
        into = lax.rem(self.low + step[1], self.pair_in)
        return (out * self.pair_in + into) * self.lats + lax.rem(self.lat + step[2], self.lats)

    def near_peer(self, step):
        target = {}
        if step[0] or step[1]:
            out = self.high // self.pair_out * self.pair_out + lax.rem(self.high + step[0], self.pair_out)
            into = self.low // self.pair_in * self.pair_in + lax.rem(self.low + step[1], self.pair_in)
            target["lon"] = out * self.inner + into
        if step[2]:
            target["lat"] = lax.rem(self.lat + step[2], self.lats)
        return target

    def far_index(self):
        index = self.section * (self.outer // self.pair_out) + self.high // self.pair_out
        return index * (self.inner // self.pair_in) + self.low // self.pair_in

    def far_peer(self, step):
        target = {}
        if step[0]:
            target["section"] = lax.rem(self.section + step[0], self.sections)
        if step[1] or step[2]:
            out = lax.rem(self.high + step[1] * self.pair_out, self.outer)
            target["lon"] = out * self.inner + lax.rem(self.low + step[2] * self.pair_in, self.inner)
        return target

    def corner(self, step, sign):
        target = {}
        if step[0]:
            target["lon"] = lax.rem(self.lon + sign + self.lons, self.lons)
        if step[1]:
            target["section"] = 1 - self.section
        if step[2]:
            target["lat"] = lax.rem(self.lat + sign + self.lats, self.lats)
        return target


def send_octants(routes, src, dst, send_sem, recv_sem, forward):
    for far in (7, 3, 6, 2, 5, 1, 4):
        step = (far >> 2, far >> 1 & 1, far & 1)
        k = 7 - far if forward else far
        pltpu.make_async_remote_copy(
            src_ref=src.at[k],
            dst_ref=dst.at[7 - k],
            send_sem=send_sem,
            recv_sem=recv_sem,
            device_id=routes.corner(step, -1 if forward else 1),
            device_id_type=MESH,
        ).start()
    stay = 7 if forward else 0
    dst[7 - stay] = src[stay]


class Loads:
    def __init__(self, names, sources, targets, sems):
        self.targets = dict(zip(names, targets))
        self.copies = {}
        for i, name in enumerate(names):
            copy = pltpu.make_async_copy(sources[i], targets[i], sems.at[i])
            copy.start()
            self.copies[name] = copy

    def __getitem__(self, name):
        copy = self.copies.pop(name, None)
        if copy is not None:
            copy.wait()
        return self.targets[name]


def whole_kernel(names, owners, unit, *refs):
    count = len(names)
    consts = Loads(names, refs[:count], refs[-count - 1 : -1], refs[-1])
    (
        latent_out,
        upper_out,
        surface_out,
        field,
        tab,
        strip,
        bias0,
        bias1,
        qkv_s,
        prob_s,
        unit0_s,
        scale0_s,
        unit1_s,
        scale1_s,
        upward_s,
        slope_s,
        patch_upper,
        patch_surface,
        grad_send,
        grad_recv,
        x_send,
        x_recv,
        back_send,
        back_recv,
        terms,
        held,
        piece,
        across,
        last,
        result,
        sems,
    ) = refs[count : -count - 1]
    routes = Routes()
    lon, lat, section = routes.lon, routes.lat, routes.section
    lon_count, lat_count, section_count = routes.lons, routes.lats, routes.sections
    count_near, count_far = len(routes.near_steps), len(routes.far_steps)
    owner, mine = routes.near_index(), routes.far_index()
    barrier = pltpu.get_barrier_semaphore()
    corners = sorted(itertools.product(range(2), repeat=3), reverse=True)
    targets = [routes.corner(d, sign) for d in corners[:-1] for sign in (-1, 1) if d != (0, 1, 0) or sign > 0]
    targets += [routes.far_peer(step) for step in routes.far_steps]
    targets += [routes.near_peer(step) for step in routes.near_steps]
    for target in targets:
        pl.semaphore_signal(barrier, inc=1, device_id=target, device_id_type=MESH)

    field[240:256, :] = jnp.zeros((16, 48), f32)
    field[496:512, :] = jnp.zeros((16, 48), f32)
    field[608:640, :] = jnp.zeros((32, 48), f32)
    for v in range(5):
        for a in range(2):
            row = (v * 2 + a) * 24
            field[row : row + 24, :] = consts["upper"][v, 2 + a].astype(f32)
            field[256 + row : 256 + row + 24, :] = consts["upper"][v, 4 * section + a].astype(f32)
    for v in range(4):
        field[512 + 24 * v : 512 + 24 * v + 24, :] = consts["surface"][v].astype(f32)
    fields = field[...].astype(bf16)
    same = consts["key_tok"][...] == consts["key_row"][section]
    upper_total = surface_total = None
    for c in range(4):
        spreads = jnp.where(same, dot(consts["pick"][c], fields, NT), 0.0)
        upper_c = (spreads[:, :256] + spreads[:, 256:512]).astype(bf16)
        surface_c = spreads[:, 512:].astype(bf16)
        upper_c = dot(upper_c, consts["fold_upper"][c])
        surface_c = dot(surface_c, consts["fold_surface"][c])
        upper_total = upper_c if upper_total is None else upper_total + upper_c
        surface_total = surface_c if surface_total is None else surface_total + surface_c
    patch_upper[...] = upper_total.astype(bf16)
    patch_surface[...] = surface_total.astype(bf16)
    latent = dot(patch_upper[...], consts["upper_embed"][...])
    latent = latent + dot(patch_surface[...], consts["surface_embed"][...])
    latent = latent.astype(bf16).astype(f32)
    build_bias(consts["table"], 0, consts["spread"], tab, strip, bias0)

    w = consts
    saved = {
        "qkv": qkv_s,
        "prob": prob_s,
        "unit0": unit0_s,
        "scale0": scale0_s,
        "unit1": unit1_s,
        "scale1": scale1_s,
        "upward": upward_s,
        "slope": slope_s,
    }
    first = block_forward(latent, 0, w, bias0, saved, False)
    x_send[...] = pack_octants(consts["pack_tok"][...], first)
    pl.semaphore_wait(barrier, len(targets))
    send_octants(routes, x_send, x_recv, sems.at[2], sems.at[3], True)

    out_grad = consts["grad"][...].astype(f32).reshape(TOKENS, WIDTH)
    grad_send[...] = pack_octants(consts["pack_nat"][...], out_grad)
    send_octants(routes, grad_send, grad_recv, sems.at[0], sems.at[1], True)
    build_bias(consts["table"], 1, consts["spread"], tab, strip, bias1)
    last_section = (section == section_count - 1).astype(f32)
    last_band = (lat == lat_count - 1).astype(f32)
    apart = jnp.abs(consts["place_col"][0] - consts["place_row"][0]) * last_section
    apart = apart + jnp.abs(consts["place_col"][1] - consts["place_row"][1]) * last_band
    for h in range(HEADS):
        rows = slice(h * TOKENS, (h + 1) * TOKENS)
        bias1[rows] = jnp.where(apart > 0.5, -1e30, bias1[rows])
    wait_bytes(x_recv, 1, 7, sems.at[3])
    shifted = unpack_octants(consts["unpack_tok"][...], x_recv[...])
    block_forward(shifted, 1, w, bias1, saved, True)
    gelu_slope(1, saved)
    wait_bytes(grad_recv, 1, 7, sems.at[1])
    dshifted = unpack_octants(consts["unpack_tok"][...], grad_recv[...])
    dmiddle = block_backward(dshifted, 1, w, saved)
    back_send[...] = pack_octants(consts["pack_tok"][...], dmiddle)
    send_octants(routes, back_send, back_recv, sems.at[4], sems.at[5], False)
    gelu_slope(0, saved)
    wait_bytes(back_recv, 0, 7, sems.at[5])
    dfirst = unpack_octants(consts["unpack_tok"][...], back_recv[...])
    dlatent = block_backward(dfirst, 0, w, saved).astype(bf16)

    upper_terms = dot(patch_upper[...], dlatent, TN)
    surface_terms = dot(patch_surface[...], dlatent, TN)
    both = jnp.concatenate((upper_terms, surface_terms), 0)
    terms[0:14, :, :] = both[:, :128].astype(bf16).reshape(14, 16, 128)
    low = both[:, 128:]
    low = jnp.concatenate((low[:112], low[112:]), 1)
    terms[14:21, :, :] = low.astype(bf16).reshape(7, 16, 128)

    for k, step in enumerate(routes.near_steps):
        peer = routes.near_index(step)

        @pl.when(peer < owners)
        def _():
            pltpu.make_async_remote_copy(
                src_ref=terms.at[pl.ds(peer * unit, unit)],
                dst_ref=held.at[pl.ds(k * unit, unit)],
                send_sem=sems.at[6],
                recv_sem=sems.at[7],
                device_id=routes.near_peer(step),
                device_id_type=MESH,
            ).start()

    latent_out[...] = dot(consts["tok_to_nat"][...], dlatent).reshape(6, 12, 2, WIDTH).astype(bf16)

    @pl.when(owner < owners)
    def _():
        wait_bytes(held, 0, count_near * unit, sems.at[7])
        total = terms[pl.ds(owner * unit, unit)].astype(f32)
        for d in range(count_near):
            total = total + held[d * unit : d * unit + unit].astype(f32)
        piece[...] = total.astype(bf16)
        across[pl.ds(mine * unit, unit)] = total.astype(bf16)
        for step in routes.far_steps:
            pltpu.make_async_remote_copy(
                src_ref=piece,
                dst_ref=across.at[pl.ds(mine * unit, unit)],
                send_sem=sems.at[8],
                recv_sem=sems.at[9],
                device_id=routes.far_peer(step),
                device_id_type=MESH,
            ).start()

        wait_bytes(across, 0, count_far * unit, sems.at[9])
        whole = across[0:unit].astype(f32)
        for d in range(1, count_far + 1):
            whole = whole + across[d * unit : d * unit + unit].astype(f32)
        last[...] = whole.astype(bf16)
        result[pl.ds(owner * unit, unit)] = whole.astype(bf16)
        for step in routes.near_steps:
            pltpu.make_async_remote_copy(
                src_ref=last,
                dst_ref=result.at[pl.ds(owner * unit, unit)],
                send_sem=sems.at[10],
                recv_sem=sems.at[11],
                device_id=routes.near_peer(step),
                device_id_type=MESH,
            ).start()

        wait_bytes(terms, 0, (owners - 1) * unit, sems.at[6])
        wait_bytes(across, 0, count_far * unit, sems.at[8])
        wait_bytes(result, 0, (owners - 1) * unit, sems.at[11])
        wait_bytes(held, 0, count_near * unit, sems.at[10])

    @pl.when(owner >= owners)
    def _():
        wait_bytes(terms, 0, owners * unit, sems.at[6])
        wait_bytes(result, 0, owners * unit, sems.at[11])

    scale = float(4 * 6 * lat_count * 12 * lon_count) ** (-0.5)
    high = result[0:14].astype(f32).reshape(224, 128) * scale
    low = result[14:21].astype(f32).reshape(112, 128) * scale
    upper_out[:, 0:128] = high[:160]
    surface_out[:, 0:128] = high[160:]
    upper_out[0:112, 128:192] = low[:, :64]
    upper_out[112:160, 128:192] = low[:48, 64:]
    surface_out[:, 128:192] = low[48:, 64:]
    wait_bytes(grad_send, 0, 7, sems.at[0])
    wait_bytes(x_send, 0, 7, sems.at[2])
    wait_bytes(back_send, 0, 7, sems.at[4])


def hand_over(*refs):
    copies = [pltpu.make_async_copy(refs[k], refs[3 + k], refs[6].at[k]) for k in range(3)]
    for copy in copies:
        copy.start()
    for copy in copies:
        copy.wait()


def on_device(
    upper_fields,
    surface_fields,
    upper_embed,
    surface_embed,
    norm_gains,
    qkv_weight,
    proj_weight,
    up_weight,
    down_weight,
    earth_bias,
    out_grad,
):
    consts = tables()
    operands = {
        "upper": upper_fields,
        "surface": surface_fields,
        "pick": consts["pick"],
        "key_tok": consts["key_tok"],
        "key_row": consts["key_row"],
        "fold_upper": consts["fold_upper"],
        "fold_surface": consts["fold_surface"],
        "upper_embed": upper_embed,
        "surface_embed": surface_embed,
        "table": earth_bias.reshape(2 * HEADS, 1, -1),
        "spread": consts["spread"],
        "grad": out_grad.transpose(1, 2, 0, 3),
        "gains": norm_gains,
        "qkv": qkv_weight,
        "heads": consts["heads"],
        "proj": proj_weight,
        "up": up_weight,
        "down": down_weight.swapaxes(1, 2),
        "pack_tok": consts["pack_tok"],
        "pack_nat": consts["pack_nat"],
        "unpack_tok": consts["unpack_tok"],
        "tok_to_nat": consts["tok_to_nat"],
        "place_col": consts["place_col"],
        "place_row": consts["place_row"],
    }
    names = tuple(operands)
    lon_count = lax.axis_size("lon")
    near = min(4, lon_count) * lax.axis_size("lat")
    if lon_count < 16:
        near = min(2, lon_count) * lax.axis_size("lat")
    group = lon_count * lax.axis_size("lat") * lax.axis_size("section") // near
    unit = -(-21 // near)
    owners = -(-21 // unit)
    hbm = pl.BlockSpec(memory_space=pltpu.HBM)
    latent_grad, upper_grad, surface_grad = pl.pallas_call(
        functools.partial(whole_kernel, names, owners, unit),
        out_shape=(
            jax.ShapeDtypeStruct((6, 12, 2, WIDTH), bf16),
            jax.ShapeDtypeStruct((160, WIDTH), f32),
            jax.ShapeDtypeStruct((64, WIDTH), f32),
        ),
        in_specs=[hbm] * len(names),
        out_specs=(pl.BlockSpec(memory_space=pltpu.VMEM),) * 3,
        scratch_shapes=[
            pltpu.VMEM((FIELD_ROWS, 48), f32),
            pltpu.VMEM((2, 96, 138), f32),
            pltpu.VMEM((96, 276), f32),
            pltpu.VMEM((HEADS * TOKENS, TOKENS), f32),
            pltpu.VMEM((HEADS * TOKENS, TOKENS), f32),
            pltpu.VMEM((2, TOKENS, 3 * WIDTH), bf16),
            pltpu.VMEM((2, HEADS * TOKENS, TOKENS), f32),
            pltpu.VMEM((2, TOKENS, WIDTH), f32),
            pltpu.VMEM((2, TOKENS, 1), f32),
            pltpu.VMEM((2, TOKENS, WIDTH), f32),
            pltpu.VMEM((2, TOKENS, 1), f32),
            pltpu.VMEM((2, TOKENS, 768), f32),
            pltpu.VMEM((TOKENS, 768), f32),
            pltpu.VMEM((TOKENS, 160), bf16),
            pltpu.VMEM((TOKENS, 64), bf16),
            pltpu.VMEM((8, 32, 128), bf16),
            pltpu.VMEM((8, 32, 128), bf16),
            pltpu.VMEM((8, 32, 128), bf16),
            pltpu.VMEM((8, 32, 128), bf16),
            pltpu.VMEM((8, 32, 128), bf16),
            pltpu.VMEM((8, 32, 128), bf16),
            pltpu.VMEM((owners * unit, 16, 128), bf16),
            pltpu.VMEM(((near - 1) * unit, 16, 128), bf16),
            pltpu.VMEM((unit, 16, 128), bf16),
            pltpu.VMEM((group * unit, 16, 128), bf16),
            pltpu.VMEM((unit, 16, 128), bf16),
            pltpu.VMEM((owners * unit, 16, 128), bf16),
            pltpu.SemaphoreType.DMA((12,)),
            *(pltpu.VMEM(a.shape, a.dtype) for a in operands.values()),
            pltpu.SemaphoreType.DMA((len(names),)),
        ],
        compiler_params=pltpu.CompilerParams(
            collective_id=0, has_side_effects=True, vmem_limit_bytes=40 * 2**20
        ),
    )(*(pltpu.with_memory_space_constraint(a, pltpu.HBM) for a in operands.values()))
    latent_grad, upper_grad, surface_grad = pl.pallas_call(
        hand_over,
        out_shape=tuple(
            jax.ShapeDtypeStruct(a.shape, a.dtype) for a in (latent_grad, upper_grad, surface_grad)
        ),
        in_specs=[pl.BlockSpec(memory_space=pltpu.VMEM)] * 3,
        out_specs=(hbm,) * 3,
        scratch_shapes=[pltpu.SemaphoreType.DMA((3,))],
        compiler_params=pltpu.CompilerParams(vmem_limit_bytes=2**20),
    )(latent_grad, upper_grad, surface_grad)
    return latent_grad.transpose(2, 0, 1, 3), upper_grad, surface_grad


def solution(mesh):
    placed = (
        P(None, None, "lat", "lon"),
        P(None, "lat", "lon"),
        P(),
        P(),
        P(),
        P(),
        P(),
        P(),
        P(),
        P(None, "lat", "section", None, None),
        P("section", "lat", "lon", None),
    )
    return jax.shard_map(
        on_device,
        mesh=mesh,
        in_specs=placed,
        out_specs=(P("section", "lat", "lon", None), P(), P()),
        check_vma=False,
    )
```

```python
import functools
import itertools

import jax
import jax.numpy as jnp
import numpy as np
from jax import lax
from jax.experimental import pallas as pl
from jax.experimental.pallas import tpu as pltpu
from jax.sharding import PartitionSpec as P

MESH = pl.DeviceIdType.MESH
f32 = jnp.float32
bf16 = jnp.bfloat16
norm_eps = 1e-05
HEADS = 6
BATCH = 3
TOKENS = 144
WIDTH = 192
FIELD_ROWS = 640
NN = (((1,), (0,)), ((), ()))
NT = (((1,), (1,)), ((), ()))
TN = (((0,), (0,)), ((), ()))


def dot(a, b, dims=NN):
    return lax.dot_general(a, b, dims, preferred_element_type=f32)


def tables():
    t = np.arange(TOKENS)
    col, level, row = t // 12, t // 6 % 2, t % 6
    octant = (col // 6) * 4 + level * 2 + row // 3
    inner = (col % 6) * 3 + row % 3
    natural = (row * 12 + col) * 2 + level

    def packing(order):
        pack = np.zeros((256, 3, TOKENS))
        pack[octant * 32 + inner, 0, order] = 1
        first = inner < 9
        pack[(octant * 32 + 18 + inner)[first], 1, order[first]] = 1
        pack[(octant * 32 + 9 + inner)[~first], 2, order[~first]] = 1
        return pack.reshape(256, 3 * TOKENS)

    pack_tok = packing(t)
    tok_to_nat = np.zeros((TOKENS, TOKENS))
    tok_to_nat[natural, t] = 1
    pick = np.zeros((4, TOKENS, 48))
    for c in range(4):
        pick[c, t, 4 * col + c] = 1
    key_row = np.full((2, 1, FIELD_ROWS), -1.0)
    fold_upper = np.zeros((4, 256, 160))
    fold_surface = np.zeros((4, 128, 64))
    for v in range(5):
        for a in range(2):
            for y in range(24):
                r = (v * 2 + a) * 24 + y
                key_row[1, 0, r] = y // 4
                key_row[:, 0, 256 + r] = 8 + y // 4
                for c in range(4):
                    fold_upper[c, r, v * 32 + a * 16 + (y % 4) * 4 + c] = 1
    for v in range(4):
        for y in range(24):
            r = v * 24 + y
            key_row[0, 0, 512 + r] = y // 4
            for c in range(4):
                fold_surface[c, r, v * 16 + (y % 4) * 4 + c] = 1
    key_tok = (level * 8 + row).reshape(TOKENS, 1)
    spread = np.zeros((2, 138, 276))
    for z in range(2):
        for a in range(6):
            for k in range(23):
                spread[z, a * 23 + k, (22 - k) * 12 + z * 6 + a] = 1
    heads = np.zeros((HEADS, 1, WIDTH))
    for h in range(HEADS):
        heads[h, 0, 32 * h : 32 * h + 32] = 1
    place_col = np.stack((level, row // 3)).reshape(2, TOKENS, 1)
    place_row = np.stack((level, row // 3)).reshape(2, 1, TOKENS)
    return {
        "pack_tok": pack_tok.astype(jnp.bfloat16),
        "unpack_tok": pack_tok.T.astype(jnp.bfloat16),
        "pack_nat": packing(natural).astype(jnp.bfloat16),
        "tok_to_nat": tok_to_nat.astype(jnp.bfloat16),
        "pick": pick.astype(jnp.bfloat16),
        "key_row": key_row.astype(np.float32),
        "key_tok": key_tok.astype(np.float32),
        "fold_upper": fold_upper.astype(jnp.bfloat16),
        "fold_surface": fold_surface.astype(jnp.bfloat16),
        "spread": spread.astype(jnp.bfloat16),
        "heads": heads.astype(np.float32),
        "place_col": place_col.astype(np.float32),
        "place_row": place_row.astype(np.float32),
    }


def centre(values):
    average = jnp.mean(values, -1, keepdims=True)
    centred = values - average
    variance = jnp.mean(centred * centred, -1, keepdims=True)
    scale = lax.rsqrt(variance + norm_eps)
    return centred * scale, scale


def norm_backward(unit, scale, gain, cotangent):
    scaled = cotangent * gain
    first = jnp.mean(scaled, -1, keepdims=True)
    second = jnp.mean(scaled * unit, -1, keepdims=True)
    return scale * (scaled - first - unit * second)


def build_bias(table_ref, b, spread_ref, tab, strip, bias):
    for z in range(2):
        for zt in range(2):
            for a in range(6):
                start = ((zt * 2 + z) * 6 + a) * 138
                tab[z, (zt * 6 + a) * 8 : (zt * 6 + a) * 8 + 6, :] = table_ref[6 * b : 6 * b + 6, 0, start : start + 138]
    total = None
    for z in range(2):
        rest = tab[z]
        for part in range(3):
            piece = rest.astype(bf16)
            rest = rest - piece.astype(f32)
            term = dot(piece, spread_ref[z])
            total = term if total is None else total + term
    strip[...] = total
    for h in range(HEADS):
        lines = jnp.concatenate([strip[8 * k + h : 8 * k + h + 1, :] for k in range(12)], 0)
        for o in range(12):
            bias[h * TOKENS + 12 * o : h * TOKENS + 12 * o + 12, :] = lines[:, 12 * (11 - o) : 12 * (11 - o) + TOKENS]


def by_head(values, w, first):
    return jnp.concatenate([values * w["heads"][h].astype(bf16) for h in range(first, first + BATCH)], 0)


def own_heads(stacked, w, first, total):
    for k in range(BATCH):
        part = stacked[k * TOKENS : (k + 1) * TOKENS] * w["heads"][first + k]
        total = part if total is None else total + part
    return total


def block_forward(x, b, w, bias, saved, final):
    unit0, scale0 = centre(x)
    hidden = (unit0 * w["gains"][b, 0:1, :]).astype(bf16)
    qkv = dot(hidden, w["qkv"][b]).astype(bf16)
    saved["qkv"][b] = qkv
    query = qkv[:, :WIDTH]
    key = qkv[:, WIDTH : 2 * WIDTH]
    value = qkv[:, 2 * WIDTH :]
    mixed = None
    for g in range(0, HEADS, BATCH):
        rows = slice(g * TOKENS, (g + BATCH) * TOKENS)
        score = dot(by_head(query, w, g), key, NT) * 32 ** (-0.5) + bias[rows]
        expo = jnp.exp(score - jnp.max(score, -1, keepdims=True))
        prob = expo * (1.0 / jnp.sum(expo, -1, keepdims=True))
        saved["prob"][b, rows] = prob
        mixed = own_heads(dot(prob.astype(bf16), value), w, g, mixed)
    resid = x + dot(mixed.astype(bf16), w["proj"][b])
    unit1, scale1 = centre(resid)
    normed = (unit1 * w["gains"][b, 1:2, :]).astype(bf16)
    upward = dot(normed, w["up"][b])
    saved["unit0"][b] = unit0
    saved["scale0"][b] = scale0
    saved["unit1"][b] = unit1
    saved["scale1"][b] = scale1
    saved["upward"][b] = upward
    if final:
        return None
    active = 0.5 * upward * (1.0 + lax.erf(upward * 2 ** (-0.5)))
    return resid + dot(active.astype(bf16), w["down"][b], NT)


def gelu_slope(b, saved):
    upward = saved["upward"][b]
    slope = 0.5 * (1.0 + lax.erf(upward * 2 ** (-0.5)))
    saved["slope"][...] = slope + upward * jnp.exp(-0.5 * upward * upward) * (2 * np.pi) ** (-0.5)


def block_backward(dout, b, w, saved):
    dactive = dot(dout.astype(bf16), w["down"][b]).astype(bf16).astype(f32)
    dupward = dactive * saved["slope"][...]
    dnormed = dot(dupward.astype(bf16), w["up"][b], NT).astype(bf16).astype(f32)
    dresid = dout + norm_backward(saved["unit1"][b], saved["scale1"][b], w["gains"][b, 1:2, :], dnormed)
    dmixed = dot(dresid.astype(bf16), w["proj"][b], NT).astype(bf16)
    qkv = saved["qkv"][b]
    query = qkv[:, :WIDTH]
    key = qkv[:, WIDTH : 2 * WIDTH]
    value = qkv[:, 2 * WIDTH :]
    dquery = dkey = dvalue = None
    for g in range(0, HEADS, BATCH):
        rows = slice(g * TOKENS, (g + BATCH) * TOKENS)
        prob = saved["prob"][b, rows]
        dmixed_g = by_head(dmixed, w, g)
        dweights = dot(dmixed_g, value, NT).astype(bf16).astype(f32)
        dv = dot(prob.astype(bf16), dmixed_g, TN)
        inner = jnp.sum(dweights * prob, -1, keepdims=True)
        dscore = (prob * (dweights - inner)).astype(bf16)
        dquery = own_heads(dot(dscore, key), w, g, dquery)
        dk = dot(dscore, by_head(query, w, g), TN)
        dkey = dk if dkey is None else dkey + dk
        dvalue = dv if dvalue is None else dvalue + dv
    dquery = dquery * 32 ** (-0.5)
    dkey = dkey * 32 ** (-0.5)
    dqkv = jnp.concatenate((dquery, dkey, dvalue), 1).astype(bf16)
    dhidden = dot(dqkv, w["qkv"][b], NT).astype(bf16).astype(f32)
    return dresid + norm_backward(saved["unit0"][b], saved["scale0"][b], w["gains"][b, 0:1, :], dhidden)


def pack_octants(pack, tokens):
    low, high = tokens[:, :128], tokens[:, 128:]
    empty = jnp.zeros_like(high)
    parts = (low, jnp.concatenate((high, empty), 1), jnp.concatenate((empty, high), 1))
    rows = jnp.concatenate([part.astype(bf16) for part in parts], 0)
    return dot(pack, rows).astype(bf16).reshape(8, 32, 128)


def unpack_octants(unpack, octants):
    parts = dot(unpack, octants.reshape(256, 128))
    low = parts[:TOKENS]
    left = parts[TOKENS : 2 * TOKENS]
    right = parts[2 * TOKENS :]
    return jnp.concatenate((low, left[:, :64] + right[:, 64:]), 1)


def wait_bytes(buffer, start, count, sem):
    view = buffer.at[pl.ds(start, count)]
    pltpu.make_async_copy(view, view, sem).wait()


class Routes:
    def __init__(self):
        self.lon, self.lat, self.section = (lax.axis_index(n) for n in ("lon", "lat", "section"))
        self.lons, self.lats, self.sections = (lax.axis_size(n) for n in ("lon", "lat", "section"))
        self.inner = min(8, self.lons)
        self.outer = self.lons // self.inner
        self.pair_in, self.pair_out = min(2, self.inner), min(2, self.outer)
        self.high = self.lon // self.inner
        self.low = lax.rem(self.lon, self.inner)
        hops = lambda d, n: min(d, n - d)
        near = itertools.product(range(self.pair_out), range(self.pair_in), range(self.lats))
        self.near_steps = sorted(
            (d for d in near if any(d)), key=lambda d: -(d[0] + d[1] + hops(d[2], self.lats) / 2)
        )
        far = itertools.product(
            range(self.sections), range(self.outer // self.pair_out), range(self.inner // self.pair_in)
        )
        self.far_steps = sorted(
            (d for d in far if any(d)),
            key=lambda d: -((4 - 2 * d[1] if d[0] else 2 * d[1]) + 2 * hops(d[2], self.inner // self.pair_in)),
        )

    def near_index(self, step=(0, 0, 0)):
        out = lax.rem(self.high + step[0], self.pair_out)
        into = lax.rem(self.low + step[1], self.pair_in)
        return (out * self.pair_in + into) * self.lats + lax.rem(self.lat + step[2], self.lats)

    def near_peer(self, step):
        target = {}
        if step[0] or step[1]:
            out = self.high // self.pair_out * self.pair_out + lax.rem(self.high + step[0], self.pair_out)
            into = self.low // self.pair_in * self.pair_in + lax.rem(self.low + step[1], self.pair_in)
            target["lon"] = out * self.inner + into
        if step[2]:
            target["lat"] = lax.rem(self.lat + step[2], self.lats)
        return target

    def far_index(self):
        index = self.section * (self.outer // self.pair_out) + self.high // self.pair_out
        return index * (self.inner // self.pair_in) + self.low // self.pair_in

    def far_peer(self, step):
        target = {}
        if step[0]:
            target["section"] = lax.rem(self.section + step[0], self.sections)
        if step[1] or step[2]:
            out = lax.rem(self.high + step[1] * self.pair_out, self.outer)
            target["lon"] = out * self.inner + lax.rem(self.low + step[2] * self.pair_in, self.inner)
        return target

    def corner(self, step, sign):
        target = {}
        if step[0]:
            target["lon"] = lax.rem(self.lon + sign + self.lons, self.lons)
        if step[1]:
            target["section"] = 1 - self.section
        if step[2]:
            target["lat"] = lax.rem(self.lat + sign + self.lats, self.lats)
        return target


def send_octants(routes, src, dst, send_sem, recv_sem, forward):
    for far in (7, 3, 6, 2, 5, 1, 4):
        step = (far >> 2, far >> 1 & 1, far & 1)
        k = 7 - far if forward else far
        pltpu.make_async_remote_copy(
            src_ref=src.at[k],
            dst_ref=dst.at[7 - k],
            send_sem=send_sem,
            recv_sem=recv_sem,
            device_id=routes.corner(step, -1 if forward else 1),
            device_id_type=MESH,
        ).start()
    stay = 7 if forward else 0
    dst[7 - stay] = src[stay]


class Loads:
    def __init__(self, names, sources, targets, sems):
        self.targets = dict(zip(names, targets))
        self.copies = {n: pltpu.make_async_copy(*refs) for n, refs in zip(names, self.pairs(sources, targets, sems))}
        self.pending = list(names)

    @staticmethod
    def pairs(sources, targets, sems):
        return [(source, targets[i], sems.at[i]) for i, source in enumerate(sources)]

    def start(self, count):
        for name in self.pending[:count]:
            self.copies[name].start()
        self.pending = self.pending[count:]

    def __getitem__(self, name):
        copy = self.copies.pop(name, None)
        if copy is not None:
            copy.wait()
        return self.targets[name]


def whole_kernel(names, owners, unit, *refs):
    count = len(names)
    consts = Loads(names, refs[:count], refs[-count - 1 : -1], refs[-1])
    (
        latent_out,
        upper_out,
        surface_out,
        field,
        tab,
        strip,
        bias0,
        bias1,
        qkv_s,
        prob_s,
        unit0_s,
        scale0_s,
        unit1_s,
        scale1_s,
        upward_s,
        slope_s,
        patch_upper,
        patch_surface,
        grad_send,
        grad_recv,
        x_send,
        x_recv,
        back_send,
        back_recv,
        terms,
        held,
        piece,
        across,
        last,
        result,
        sems,
    ) = refs[count : -count - 1]
    consts.start(11)
    routes = Routes()
    lon, lat, section = routes.lon, routes.lat, routes.section
    lon_count, lat_count, section_count = routes.lons, routes.lats, routes.sections
    count_near, count_far = len(routes.near_steps), len(routes.far_steps)
    owner, mine = routes.near_index(), routes.far_index()
    barrier = pltpu.get_barrier_semaphore()
    corners = sorted(itertools.product(range(2), repeat=3), reverse=True)
    targets = [routes.corner(d, sign) for d in corners if d[0] or sum(d) > 1 for sign in (-1, 1)]
    targets += [routes.far_peer(step) for step in routes.far_steps]
    targets += [routes.near_peer(step) for step in routes.near_steps]
    for target in targets:
        pl.semaphore_signal(barrier, inc=1, device_id=target, device_id_type=MESH)
    consts.start(count)
    for name in names[:11]:
        consts[name]

    field[240:256, :] = jnp.zeros((16, 48), f32)
    field[496:512, :] = jnp.zeros((16, 48), f32)
    field[608:640, :] = jnp.zeros((32, 48), f32)
    for v in range(5):
        for a in range(2):
            row = (v * 2 + a) * 24
            field[row : row + 24, :] = consts["upper"][v, 2 + a].astype(f32)
            field[256 + row : 256 + row + 24, :] = consts["upper"][v, 4 * section + a].astype(f32)
    for v in range(4):
        field[512 + 24 * v : 512 + 24 * v + 24, :] = consts["surface"][v].astype(f32)
    fields = field[...].astype(bf16)
    same = consts["key_tok"][...] == consts["key_row"][section]
    upper_total = surface_total = None
    for c in range(4):
        spreads = jnp.where(same, dot(consts["pick"][c], fields, NT), 0.0)
        upper_c = (spreads[:, :256] + spreads[:, 256:512]).astype(bf16)
        surface_c = spreads[:, 512:].astype(bf16)
        upper_c = dot(upper_c, consts["fold_upper"][c])
        surface_c = dot(surface_c, consts["fold_surface"][c])
        upper_total = upper_c if upper_total is None else upper_total + upper_c
        surface_total = surface_c if surface_total is None else surface_total + surface_c
    patch_upper[...] = upper_total.astype(bf16)
    patch_surface[...] = surface_total.astype(bf16)
    latent = dot(patch_upper[...], consts["upper_embed"][...])
    latent = latent + dot(patch_surface[...], consts["surface_embed"][...])
    latent = latent.astype(bf16).astype(f32)
    build_bias(consts["table"], 0, consts["spread"], tab, strip, bias0)

    w = consts
    saved = {
        "qkv": qkv_s,
        "prob": prob_s,
        "unit0": unit0_s,
        "scale0": scale0_s,
        "unit1": unit1_s,
        "scale1": scale1_s,
        "upward": upward_s,
        "slope": slope_s,
    }
    first = block_forward(latent, 0, w, bias0, saved, False)
    x_send[...] = pack_octants(consts["pack_tok"][...], first)
    pl.semaphore_wait(barrier, len(targets))
    send_octants(routes, x_send, x_recv, sems.at[2], sems.at[3], True)

    out_grad = consts["grad"][...].astype(f32).reshape(TOKENS, WIDTH)
    grad_send[...] = pack_octants(consts["pack_nat"][...], out_grad)
    send_octants(routes, grad_send, grad_recv, sems.at[0], sems.at[1], True)
    build_bias(consts["table"], 1, consts["spread"], tab, strip, bias1)
    last_section = (section == section_count - 1).astype(f32)
    last_band = (lat == lat_count - 1).astype(f32)
    apart = jnp.abs(consts["place_col"][0] - consts["place_row"][0]) * last_section
    apart = apart + jnp.abs(consts["place_col"][1] - consts["place_row"][1]) * last_band
    for h in range(HEADS):
        rows = slice(h * TOKENS, (h + 1) * TOKENS)
        bias1[rows] = jnp.where(apart > 0.5, -1e30, bias1[rows])
    wait_bytes(x_recv, 1, 7, sems.at[3])
    shifted = unpack_octants(consts["unpack_tok"][...], x_recv[...])
    block_forward(shifted, 1, w, bias1, saved, True)
    gelu_slope(1, saved)
    wait_bytes(grad_recv, 1, 7, sems.at[1])
    dshifted = unpack_octants(consts["unpack_tok"][...], grad_recv[...])
    dmiddle = block_backward(dshifted, 1, w, saved)
    back_send[...] = pack_octants(consts["pack_tok"][...], dmiddle)
    send_octants(routes, back_send, back_recv, sems.at[4], sems.at[5], False)
    gelu_slope(0, saved)
    wait_bytes(back_recv, 0, 7, sems.at[5])
    dfirst = unpack_octants(consts["unpack_tok"][...], back_recv[...])
    dlatent = block_backward(dfirst, 0, w, saved).astype(bf16)

    upper_terms = dot(patch_upper[...], dlatent, TN)
    surface_terms = dot(patch_surface[...], dlatent, TN)
    both = jnp.concatenate((upper_terms, surface_terms), 0)
    terms[0:14, :, :] = both[:, :128].astype(bf16).reshape(14, 16, 128)
    low = both[:, 128:]
    low = jnp.concatenate((low[:112], low[112:]), 1)
    terms[14:21, :, :] = low.astype(bf16).reshape(7, 16, 128)

    for k, step in enumerate(routes.near_steps):
        peer = routes.near_index(step)

        @pl.when(peer < owners)
        def _():
            pltpu.make_async_remote_copy(
                src_ref=terms.at[pl.ds(peer * unit, unit)],
                dst_ref=held.at[pl.ds(k * unit, unit)],
                send_sem=sems.at[6],
                recv_sem=sems.at[7],
                device_id=routes.near_peer(step),
                device_id_type=MESH,
            ).start()

    latent_out[...] = dot(consts["tok_to_nat"][...], dlatent).reshape(6, 12, 2, WIDTH).astype(bf16)

    @pl.when(owner < owners)
    def _():
        wait_bytes(held, 0, count_near * unit, sems.at[7])
        total = terms[pl.ds(owner * unit, unit)].astype(f32)
        for d in range(count_near):
            total = total + held[d * unit : d * unit + unit].astype(f32)
        piece[...] = total.astype(bf16)
        across[pl.ds(mine * unit, unit)] = total.astype(bf16)
        for step in routes.far_steps:
            pltpu.make_async_remote_copy(
                src_ref=piece,
                dst_ref=across.at[pl.ds(mine * unit, unit)],
                send_sem=sems.at[8],
                recv_sem=sems.at[9],
                device_id=routes.far_peer(step),
                device_id_type=MESH,
            ).start()

        wait_bytes(across, 0, count_far * unit, sems.at[9])
        whole = across[0:unit].astype(f32)
        for d in range(1, count_far + 1):
            whole = whole + across[d * unit : d * unit + unit].astype(f32)
        last[...] = whole.astype(bf16)
        result[pl.ds(owner * unit, unit)] = whole.astype(bf16)
        for step in routes.near_steps:
            pltpu.make_async_remote_copy(
                src_ref=last,
                dst_ref=result.at[pl.ds(owner * unit, unit)],
                send_sem=sems.at[10],
                recv_sem=sems.at[11],
                device_id=routes.near_peer(step),
                device_id_type=MESH,
            ).start()

        wait_bytes(terms, 0, (owners - 1) * unit, sems.at[6])
        wait_bytes(across, 0, count_far * unit, sems.at[8])
        wait_bytes(result, 0, (owners - 1) * unit, sems.at[11])
        wait_bytes(held, 0, count_near * unit, sems.at[10])

    @pl.when(owner >= owners)
    def _():
        wait_bytes(terms, 0, owners * unit, sems.at[6])
        wait_bytes(result, 0, owners * unit, sems.at[11])

    scale = float(4 * 6 * lat_count * 12 * lon_count) ** (-0.5)
    high = result[0:14].astype(f32).reshape(224, 128) * scale
    low = result[14:21].astype(f32).reshape(112, 128) * scale
    upper_out[:, 0:128] = high[:160]
    surface_out[:, 0:128] = high[160:]
    upper_out[0:112, 128:192] = low[:, :64]
    upper_out[112:160, 128:192] = low[:48, 64:]
    surface_out[:, 128:192] = low[48:, 64:]
    wait_bytes(grad_send, 0, 7, sems.at[0])
    wait_bytes(x_send, 0, 7, sems.at[2])
    wait_bytes(back_send, 0, 7, sems.at[4])


def hand_over(*refs):
    copies = [pltpu.make_async_copy(refs[k], refs[3 + k], refs[6].at[k]) for k in range(3)]
    for copy in copies:
        copy.start()
    for copy in copies:
        copy.wait()


def on_device(
    upper_fields,
    surface_fields,
    upper_embed,
    surface_embed,
    norm_gains,
    qkv_weight,
    proj_weight,
    up_weight,
    down_weight,
    earth_bias,
    out_grad,
):
    consts = tables()
    operands = {
        "upper": upper_fields,
        "surface": surface_fields,
        "pick": consts["pick"],
        "key_tok": consts["key_tok"],
        "key_row": consts["key_row"],
        "fold_upper": consts["fold_upper"],
        "fold_surface": consts["fold_surface"],
        "upper_embed": upper_embed,
        "surface_embed": surface_embed,
        "table": earth_bias.reshape(2 * HEADS, 1, -1),
        "spread": consts["spread"],
        "grad": out_grad.transpose(1, 2, 0, 3),
        "gains": norm_gains,
        "qkv": qkv_weight,
        "heads": consts["heads"],
        "proj": proj_weight,
        "up": up_weight,
        "down": down_weight.swapaxes(1, 2),
        "pack_tok": consts["pack_tok"],
        "pack_nat": consts["pack_nat"],
        "unpack_tok": consts["unpack_tok"],
        "tok_to_nat": consts["tok_to_nat"],
        "place_col": consts["place_col"],
        "place_row": consts["place_row"],
    }
    names = tuple(operands)
    lon_count = lax.axis_size("lon")
    near = min(4, lon_count) * lax.axis_size("lat")
    if lon_count < 16:
        near = min(2, lon_count) * lax.axis_size("lat")
    group = lon_count * lax.axis_size("lat") * lax.axis_size("section") // near
    unit = -(-21 // near)
    owners = -(-21 // unit)
    hbm = pl.BlockSpec(memory_space=pltpu.HBM)
    latent_grad, upper_grad, surface_grad = pl.pallas_call(
        functools.partial(whole_kernel, names, owners, unit),
        out_shape=(
            jax.ShapeDtypeStruct((6, 12, 2, WIDTH), bf16),
            jax.ShapeDtypeStruct((160, WIDTH), f32),
            jax.ShapeDtypeStruct((64, WIDTH), f32),
        ),
        in_specs=[hbm] * len(names),
        out_specs=(pl.BlockSpec(memory_space=pltpu.VMEM),) * 3,
        scratch_shapes=[
            pltpu.VMEM((FIELD_ROWS, 48), f32),
            pltpu.VMEM((2, 96, 138), f32),
            pltpu.VMEM((96, 276), f32),
            pltpu.VMEM((HEADS * TOKENS, TOKENS), f32),
            pltpu.VMEM((HEADS * TOKENS, TOKENS), f32),
            pltpu.VMEM((2, TOKENS, 3 * WIDTH), bf16),
            pltpu.VMEM((2, HEADS * TOKENS, TOKENS), f32),
            pltpu.VMEM((2, TOKENS, WIDTH), f32),
            pltpu.VMEM((2, TOKENS, 1), f32),
            pltpu.VMEM((2, TOKENS, WIDTH), f32),
            pltpu.VMEM((2, TOKENS, 1), f32),
            pltpu.VMEM((2, TOKENS, 768), f32),
            pltpu.VMEM((TOKENS, 768), f32),
            pltpu.VMEM((TOKENS, 160), bf16),
            pltpu.VMEM((TOKENS, 64), bf16),
            pltpu.VMEM((8, 32, 128), bf16),
            pltpu.VMEM((8, 32, 128), bf16),
            pltpu.VMEM((8, 32, 128), bf16),
            pltpu.VMEM((8, 32, 128), bf16),
            pltpu.VMEM((8, 32, 128), bf16),
            pltpu.VMEM((8, 32, 128), bf16),
            pltpu.VMEM((owners * unit, 16, 128), bf16),
            pltpu.VMEM(((near - 1) * unit, 16, 128), bf16),
            pltpu.VMEM((unit, 16, 128), bf16),
            pltpu.VMEM((group * unit, 16, 128), bf16),
            pltpu.VMEM((unit, 16, 128), bf16),
            pltpu.VMEM((owners * unit, 16, 128), bf16),
            pltpu.SemaphoreType.DMA((12,)),
            *(pltpu.VMEM(a.shape, a.dtype) for a in operands.values()),
            pltpu.SemaphoreType.DMA((len(names),)),
        ],
        compiler_params=pltpu.CompilerParams(
            collective_id=0, has_side_effects=True, vmem_limit_bytes=40 * 2**20
        ),
    )(*(pltpu.with_memory_space_constraint(a, pltpu.HBM) for a in operands.values()))
    latent_grad, upper_grad, surface_grad = pl.pallas_call(
        hand_over,
        out_shape=tuple(
            jax.ShapeDtypeStruct(a.shape, a.dtype) for a in (latent_grad, upper_grad, surface_grad)
        ),
        in_specs=[pl.BlockSpec(memory_space=pltpu.VMEM)] * 3,
        out_specs=(hbm,) * 3,
        scratch_shapes=[pltpu.SemaphoreType.DMA((3,))],
        compiler_params=pltpu.CompilerParams(vmem_limit_bytes=2**20),
    )(latent_grad, upper_grad, surface_grad)
    return latent_grad.transpose(2, 0, 1, 3), upper_grad, surface_grad


def solution(mesh):
    placed = (
        P(None, None, "lat", "lon"),
        P(None, "lat", "lon"),
        P(),
        P(),
        P(),
        P(),
        P(),
        P(),
        P(),
        P(None, "lat", "section", None, None),
        P("section", "lat", "lon", None),
    )
    return jax.shard_map(
        on_device,
        mesh=mesh,
        in_specs=placed,
        out_specs=(P("section", "lat", "lon", None), P(), P()),
        check_vma=False,
    )
```
